512 devices in a mesh: row: 32 (over z, x), col: 16 (over y, core).
Axes of the slice: x: 4, y: 8, z: 8, core: 2. Of those that a mesh axis runs over, the one named last changes fastest.
Arguments:
- tiles: bfloat16 [32, 16, 32, 128, 128], P('row', 'col'), may hold values from -0.375 to 0.375
- coords: int32 [32, 16, 32, 2], P('row', 'col'), may hold values from 0 to 2047, as said below
- counts: int32 [32, 16], P('row', 'col'), may hold values from 16 to 32, as said below
- rhs: float32 [2, 4194304], P(None, ('row', 'col')), may hold values from -50 to 50
Outputs:
- solution: float32 [2, 4194304], P(None, ('col', 'row'))
- phi_bar: float32 [2], replicated
The draws below stay inside these ranges and needn't reach their ends.
Inputs may be any that keep to these rules, and one draw needn't show every extreme that they name: coords[p, q, k, 0] is a local block row below 1024 and coords[p, q, k, 1] a local block column below 2048; within one tile no two slots share a block row and no two share a block column; counting all 32 slots of a tile, exactly 2 of its block rows fall in each of the 16 ranges of 64 consecutive block rows, and exactly 1 of its block columns in each of the 32 ranges of 64 consecutive block columns. The first counts[p, q] slots of tile (p, q) are used; some tile uses all 32.
All inputs are finite; a program needn't handle non-finite values.
Results may differ from the reference program's by a relative error of at most 0.015.
Values may be sent and summed in bfloat16 or wider, within the bound.
No kernel may reach another device: no remote copies, remote signals or barrier semaphores. Data moves between devices by JAX's collectives and lax.ppermute only.
A program may use at most 192 MiB of HBM per device.

```python
import math
import jax
import jax.numpy as jnp
from jax import lax

ORDER = 4194304
BLOCK = 128
SLOTS = 32
RHS = 2
ITERS = 2
TILE_ROWS = 1024
TILE_COLS = 2048
N_ROW = 32
N_COL = 16


def tile_numbers():
    return jnp.arange(N_ROW, dtype=jnp.int32)[:, None] * N_COL + jnp.arange(N_COL, dtype=jnp.int32)[None, :]


def pool_draw(key, first, second, range_len):
    inner = jnp.broadcast_to(jnp.arange(range_len - 2, dtype=jnp.int32) + 1, (first, second, range_len - 2))
    mixed = jax.random.permutation(key, inner, axis=2, independent=True).astype(jnp.int32)
    top_value = jnp.full((first, second, 1), range_len - 1, jnp.int32)
    low_value = jnp.zeros((first, second, 1), jnp.int32)
    return jnp.concatenate([top_value, low_value, mixed], axis=2).astype(jnp.int32)


def draw_coords(key, part):
    key_rows, key_cols, key_rpool, key_cpool = jax.random.split(jax.random.fold_in(key, 11), 4)
    range_len = TILE_ROWS // N_COL
    row_cap = SLOTS // N_COL
    col_cap = SLOTS // N_ROW
    slot_base = jnp.broadcast_to(jnp.arange(SLOTS, dtype=jnp.int32), (N_ROW, N_COL, SLOTS))
    row_perm = jax.random.permutation(key_rows, slot_base, axis=2, independent=True).astype(jnp.int32)
    col_perm = jax.random.permutation(key_cols, slot_base, axis=2, independent=True).astype(jnp.int32)
    row_pool = pool_draw(key_rpool, N_ROW, N_COL, range_len)
    col_pool = pool_draw(key_cpool, N_COL, N_ROW, range_len)
    p_index = jnp.arange(N_ROW, dtype=jnp.int32)[:, None, None]
    q_index = jnp.arange(N_COL, dtype=jnp.int32)[None, :, None]
    row_owner = row_perm % N_COL
    row_rank = row_perm // N_COL
    row_pos = (q_index * row_cap + row_rank) % range_len
    block_rows = row_owner * range_len + row_pool[p_index, row_owner, row_pos]
    col_owner = col_perm % N_ROW
    col_rank = col_perm // N_ROW
    col_pos = (p_index * col_cap + col_rank) % range_len
    block_cols = col_owner * range_len + col_pool[q_index, col_owner, col_pos]
    return jnp.stack([block_rows, block_cols], axis=-1).astype(jnp.int32)


def draw_counts(key, part):
    key_base, key_pick = jax.random.split(jax.random.fold_in(key, 23))
    used = SLOTS - jax.random.randint(key_base, (N_ROW, N_COL), 0, SLOTS // 2 + 1, dtype=jnp.int32)
    picks = jax.random.permutation(key_pick, N_ROW * N_COL)[:2].astype(jnp.int32)
    numbers = tile_numbers()
    used = jnp.where(numbers == picks[0], SLOTS, jnp.where(numbers == picks[1], SLOTS - SLOTS // 2, used))
    return used.astype(jnp.int32)


def draw_rhs(key, part):
    key_base, key_scale = jax.random.split(jax.random.fold_in(key, 37))
    scales = jnp.exp(jax.random.uniform(key_scale, (RHS, ORDER), jnp.float32) * math.log(10.0))
    base = jnp.clip(jax.random.normal(key_base, (RHS, ORDER), jnp.float32), -5.0, 5.0)
    return (base * scales).astype(jnp.float32)


def level_of(own_key, extent, cuts, smallest, largest):
    level, own = 1.0, jax.random.fold_in(own_key, 6)
    for dim, shards_of in cuts:
        heights = jnp.exp(jax.random.uniform(jax.random.fold_in(own, dim), (shards_of,), jnp.float32, smallest / len(cuts), largest / len(cuts)))
        level = level * jnp.repeat(heights, extent[dim] // shards_of).reshape([-1 if axis == dim else 1 for axis in range(len(extent))])
    return level


def gaussian(stream_key, dims, scale, reach, pieces=(), held_as=jnp.bfloat16):
    values = jax.random.normal(stream_key, dims, jnp.float32) * scale
    if len(pieces) > 0:
        values = level_of(stream_key, dims, pieces, -0.22, 0.18) * values
    return jnp.clip(values, min=-reach, max=reach).astype(held_as)


def setup_inputs(seed: int = 0) -> dict:
    arg_keys = jax.random.split(jax.random.key(seed), 5)
    return {
        "tiles": gaussian(arg_keys[0], (N_ROW, N_COL, SLOTS, BLOCK, BLOCK), (2 * BLOCK) ** -0.5, 0.375, ((0, 32), (1, 16))),
        "coords": draw_coords(jax.random.fold_in(arg_keys[4], 71), 0),
        "counts": draw_counts(jax.random.fold_in(arg_keys[4], 71), 0),
        "rhs": draw_rhs(jax.random.fold_in(arg_keys[4], 71), 0),
    }


EPS = 1e-06

def rounded(values):
    return lax.optimization_barrier(values.astype(jnp.bfloat16))

def norm_of(vector_bf):
    values = vector_bf.astype(jnp.float32)
    return jnp.sqrt(lax.optimization_barrier(jnp.sum(values * values, axis=1)) + EPS)

def tile_forward(tile_data, slot_coords, count, segment):
    valid = (jnp.arange(SLOTS) < count).astype(jnp.float32)
    blocks = segment.reshape(RHS, TILE_COLS, BLOCK).astype(jnp.float32)
    picked = jnp.take(blocks, slot_coords[:, 1], axis=1)
    products = jnp.einsum('rkc,kdc->krd', picked, tile_data.astype(jnp.float32), precision=lax.Precision.HIGHEST)
    products = products * valid[:, None, None]
    summed = jax.ops.segment_sum(products, slot_coords[:, 0], num_segments=TILE_ROWS)
    partial_sum = jnp.transpose(summed, (1, 0, 2)).reshape(RHS, TILE_ROWS * BLOCK)
    return rounded(partial_sum).astype(jnp.float32)

def tile_adjoint(tile_data, slot_coords, count, segment):
    valid = (jnp.arange(SLOTS) < count).astype(jnp.float32)
    blocks = segment.reshape(RHS, TILE_ROWS, BLOCK).astype(jnp.float32)
    picked = jnp.take(blocks, slot_coords[:, 0], axis=1)
    products = jnp.einsum('rkd,kdc->krc', picked, tile_data.astype(jnp.float32), precision=lax.Precision.HIGHEST)
    products = products * valid[:, None, None]
    summed = jax.ops.segment_sum(products, slot_coords[:, 1], num_segments=TILE_COLS)
    partial_sum = jnp.transpose(summed, (1, 0, 2)).reshape(RHS, TILE_COLS * BLOCK)
    return rounded(partial_sum).astype(jnp.float32)

def apply_forward(tiles, coords, counts, vector_bf):
    segments = vector_bf.reshape(RHS, N_COL, TILE_COLS * BLOCK)

    def one_row(row_index):

        def add_tile(total, col_index):
            term = tile_forward(tiles[row_index, col_index], coords[row_index, col_index], counts[row_index, col_index], segments[:, col_index])
            return (total + term, None)
        total, _ = lax.scan(add_tile, jnp.zeros((RHS, TILE_ROWS * BLOCK), jnp.float32), jnp.arange(N_COL))
        return total
    stacked = lax.map(one_row, jnp.arange(N_ROW))
    return jnp.transpose(stacked, (1, 0, 2)).reshape(RHS, ORDER)

def apply_adjoint(tiles, coords, counts, vector_bf):
    segments = vector_bf.reshape(RHS, N_ROW, TILE_ROWS * BLOCK)

    def one_col(col_index):

        def add_tile(total, row_index):
            term = tile_adjoint(tiles[row_index, col_index], coords[row_index, col_index], counts[row_index, col_index], segments[:, row_index])
            return (total + term, None)
        total, _ = lax.scan(add_tile, jnp.zeros((RHS, TILE_COLS * BLOCK), jnp.float32), jnp.arange(N_ROW))
        return total
    stacked = lax.map(one_col, jnp.arange(N_COL))
    return jnp.transpose(stacked, (1, 0, 2)).reshape(RHS, ORDER)

def reference(tiles, coords, counts, rhs):
    u_rounded = rounded(rhs)
    beta_now = norm_of(u_rounded)
    u_unit = u_rounded.astype(jnp.float32) / beta_now[:, None]
    v_rounded = rounded(apply_adjoint(tiles, coords, counts, u_rounded) / beta_now[:, None])
    alpha_now = norm_of(v_rounded)
    v_unit = v_rounded.astype(jnp.float32) / alpha_now[:, None]
    direction = v_unit
    solution = jnp.zeros((RHS, ORDER), jnp.float32)
    phi_bar = beta_now
    rho_bar = alpha_now
    for step in range(ITERS):
        forward = apply_forward(tiles, coords, counts, v_rounded)
        u_rounded = rounded(forward / alpha_now[:, None] - alpha_now[:, None] * u_unit)
        beta_now = norm_of(u_rounded)
        rho_value = jnp.sqrt(rho_bar * rho_bar + beta_now * beta_now)
        cosine = rho_bar / rho_value
        sine = beta_now / rho_value
        phi_value = cosine * phi_bar
        phi_bar = sine * phi_bar
        solution = solution + (phi_value / rho_value)[:, None] * direction
        u_unit = u_rounded.astype(jnp.float32) / beta_now[:, None]
        if step + 1 < ITERS:
            adjoint = apply_adjoint(tiles, coords, counts, u_rounded)
            v_rounded = rounded(adjoint / beta_now[:, None] - beta_now[:, None] * v_unit)
            alpha_now = norm_of(v_rounded)
            theta_value = sine * alpha_now
            rho_bar = -cosine * alpha_now
            v_unit = v_rounded.astype(jnp.float32) / alpha_now[:, None]
            direction = v_unit - (theta_value / rho_value)[:, None] * direction
    return (solution, phi_bar)
```

```python
import functools

import jax
import jax.numpy as jnp
from jax import lax
from jax.experimental import pallas as pl
from jax.experimental.pallas import tpu as pltpu
from jax.sharding import PartitionSpec as P

EPS = 1e-06
F32 = jnp.float32
BF16 = jnp.bfloat16
VMEM = pl.BlockSpec(memory_space=pltpu.VMEM)
SMEM = pl.BlockSpec(memory_space=pltpu.SMEM)


def iota(shape, dim):
    return lax.broadcasted_iota(jnp.int32, shape, dim)


def fill_row_keys(keys_ref, coords_ref, count, axis):
    parity = iota((2, 128), 0)
    for k in range(coords_ref.shape[0]):
        base = jnp.where(k < count, coords_ref[k, axis] * 2, -8)
        keys_ref[2 * k : 2 * k + 2, :] = (base + parity).astype(F32)


def lane_keys(coords_ref, count, axis):
    lane = iota((8, 128), 1)
    slot = (lane % 64) // 2
    keys = jnp.full((8, 128), -2, jnp.int32)
    for k in range(coords_ref.shape[0]):
        base = jnp.where(k < count, coords_ref[k, axis] * 2, -2)
        keys = jnp.where(slot == k, base, keys)
    keys = (keys + lane % 2).astype(F32)
    high = jnp.floor(keys * (1.0 / 64.0))
    low = keys - 64.0 * high
    sub = iota((8, 128), 0)
    return jnp.where(sub == 0, high, jnp.where(sub == 1, low, 0.0)).astype(BF16)


def read_lane_keys(received_ref, map_ref, rows):
    first = iota((8, 128), 1) < 64
    for g in range(received_ref.shape[0] // 2):
        even = received_ref[2 * g, rows : rows + 8, :].astype(F32)
        odd = received_ref[2 * g + 1, rows : rows + 8, :].astype(F32)
        both = jnp.where(first, even, odd)
        map_ref[g : g + 1, :] = both[0:1, :] * 64.0 + both[1:2, :]


def own_sum(received_ref, map_ref, keys_ref, rows):
    keys = keys_ref[...]
    total = jnp.zeros(keys.shape, F32)
    for g in range(received_ref.shape[0] // 2):
        match = (keys == map_ref[g : g + 1, :]).astype(F32).astype(BF16)
        both = jnp.concatenate([received_ref[2 * g, 0:rows, :], received_ref[2 * g + 1, 0:rows, :]], axis=0)
        total = total + jnp.dot(match, both, preferred_element_type=F32)
    return total


def leaders(map_ref, keys_ref, me, groups):
    keys = keys_ref[...]
    half = iota(keys.shape, 1) // 64
    earlier = jnp.zeros(keys.shape, F32)
    for g in range(groups):
        hit = (keys == map_ref[g : g + 1, :]) & (2 * g + half < me)
        earlier = earlier + hit.astype(F32)
    count = jnp.sum(earlier, axis=1, keepdims=True)
    return ((count == 0.0) & (keys >= 0.0)).astype(F32)


def products(held_ref, tile_ref, out_ref, adjoint):
    for k in range(tile_ref.shape[0]):
        rows = held_ref[2 * k : 2 * k + 2, :].astype(BF16)
        dims = (((1,), (0 if adjoint else 1,)), ((), ()))
        out_ref[2 * k : 2 * k + 2, :] = lax.dot_general(rows, tile_ref[k], dims, preferred_element_type=F32)


def send_all(sent_ref, values, extra):
    rows = values.shape[0]
    for peer in range(sent_ref.shape[0]):
        sent_ref[peer, 0:rows, :] = values
        if extra is not None:
            sent_ref[peer, rows : rows + 8, :] = extra


def first_adjoint(coords_ref, counts_ref, u_ref, tile_ref, sent_ref, own_u_ref, wide, held, out):
    wide[...] = u_ref[...].astype(F32)
    count = counts_ref[0, 0]
    for k in range(coords_ref.shape[0]):
        used = (k < count).astype(F32)
        row = pl.multiple_of(coords_ref[k, 0] * 2, 2)
        held[2 * k : 2 * k + 2, :] = wide[pl.ds(row, 2), :] * used
    own_u_ref[...] = held[...].astype(BF16)
    products(held, tile_ref, out, True)
    send_all(sent_ref, out[...].astype(BF16), lane_keys(coords_ref, count, 1))


def first_forward(coords_ref, counts_ref, got_ref, tile_ref, sent_ref, w_ref, map_ref, keys, held, out):
    count = counts_ref[0, 0]
    rows = keys.shape[0]
    fill_row_keys(keys, coords_ref, count, 1)
    read_lane_keys(got_ref, map_ref, rows)
    w = own_sum(got_ref, map_ref, keys, rows).astype(BF16)
    w_ref[...] = w
    held[...] = w.astype(F32)
    products(held, tile_ref, out, False)
    send_all(sent_ref, out[...].astype(BF16), lane_keys(coords_ref, count, 0))


def second_adjoint(coords_ref, counts_ref, got_ref, tile_ref, sent_ref, w_ref, map_ref, keys, held, out):
    rows = keys.shape[0]
    fill_row_keys(keys, coords_ref, counts_ref[0, 0], 0)
    read_lane_keys(got_ref, map_ref, rows)
    w = own_sum(got_ref, map_ref, keys, rows).astype(BF16)
    w_ref[...] = w
    held[...] = w.astype(F32)
    products(held, tile_ref, out, True)
    send_all(sent_ref, out[...].astype(BF16), None)


def by_parity(values):
    folded = jnp.sum(values.reshape(values.shape[0] // 8, 8, 128), axis=0)
    return jnp.sum(folded, axis=1, keepdims=True)


def digits(sums):
    lane = iota((8, 128), 1)
    block = jnp.zeros((8, 128), F32)
    for j, value in enumerate(sums):
        value = jnp.broadcast_to(value, (8, 128))
        high = value.astype(BF16).astype(F32)
        middle = (value - high).astype(BF16).astype(F32)
        low = (value - high - middle).astype(BF16).astype(F32)
        block = jnp.where(lane == j, high, block)
        block = jnp.where(lane == 16 + j, middle, block)
        block = jnp.where(lane == 32 + j, low, block)
    return block


def undigits(block):
    return block + pltpu.roll(block, 112, 1) + pltpu.roll(block, 96, 1)


def second_forward(
    coords_ref, counts_ref, got_ref, tile_ref, v_map_ref, u_map_ref, w1_ref, w2_ref, own_u_ref, piece_ref,
    sent_ref, w3_ref, lead_ref, keys, held, out,
):
    count = counts_ref[0, 0]
    rows = keys.shape[0]
    fill_row_keys(keys, coords_ref, count, 1)
    w3 = own_sum(got_ref, v_map_ref, keys, rows).astype(BF16)
    w3_ref[...] = w3
    held[...] = w3.astype(F32)
    products(held, tile_ref, out, False)
    sent = out[...].astype(BF16)
    lead_v = leaders(v_map_ref, keys, lax.axis_index("row"), got_ref.shape[0] // 2)
    lead_ref[...] = jnp.broadcast_to(lead_v, lead_ref.shape)
    fill_row_keys(keys, coords_ref, count, 0)
    lead_u = leaders(u_map_ref, keys, lax.axis_index("col"), sent_ref.shape[0] // 2)
    w3 = w3.astype(F32)
    w1 = w1_ref[...].astype(F32)
    w2 = w2_ref[...].astype(F32)
    u0 = own_u_ref[...].astype(F32)
    piece = piece_ref[...].astype(F32)
    c4 = sent.astype(F32)
    sums = [
        by_parity(w1 * w1 * lead_v),
        by_parity(w1 * w3 * lead_v),
        by_parity(w3 * w3 * lead_v),
        by_parity(piece * piece),
        by_parity(u0 * w2 * lead_u),
        by_parity(w2 * w2 * lead_u),
        by_parity(c4 * w2),
        by_parity(c4 * u0),
    ]
    send_all(sent_ref, sent, digits(sums).astype(BF16))


def gather_sums(coords_ref, got_ref, u_map_ref, w1_ref, w3_ref, lead_ref, sent_ref, values, square, held1, held3):
    peers = got_ref.shape[0]
    rows = got_ref.shape[1] - 8
    partial = jnp.zeros((8, 128), F32)
    for peer in range(peers):
        partial = partial + got_ref[peer, rows : rows + 8, :].astype(F32)
        values[peer * rows : (peer + 1) * rows, :] = got_ref[peer, 0:rows, :]
    for g in range(peers // 2):
        column = jnp.transpose(jnp.broadcast_to(u_map_ref[g : g + 1, :], (128, 128)))
        total = jnp.zeros((128, 128), F32)
        for h in range(peers // 2):
            match = (column == u_map_ref[h : h + 1, :]).astype(F32).astype(BF16)
            total = total + jnp.dot(match, values[128 * h : 128 * h + 128, :], preferred_element_type=F32)
        own = values[128 * g : 128 * g + 128, :].astype(F32) * total
        folded = jnp.sum(own.reshape(16, 8, 128), axis=0)
        square[...] = folded if g == 0 else square[...] + folded
    last = digits([jnp.zeros((8, 1), F32)] * 8 + [jnp.sum(square[...], axis=1, keepdims=True)])
    block = partial + last
    block = block + pltpu.roll(block, 2, 0)
    block = block + pltpu.roll(block, 4, 0)
    block = digits_again(block)
    held1[...] = w1_ref[...].astype(F32) * lead_ref[...]
    held3[...] = w3_ref[...].astype(F32) * lead_ref[...]
    me = lax.axis_index("row")
    sub = iota((8, 128), 0)
    lane = iota((8, 128), 1)
    label_here = (lane // 8 + 16 * (sub - 6) == me) & (sub >= 6)
    sums = jnp.where((sub == 4) | (sub == 5), block, 0.0)
    for k in range(coords_ref.shape[0]):
        column = coords_ref[k, 1]
        owner = column // 64
        first = held1[2 * k : 2 * k + 2, :]
        second = held3[2 * k : 2 * k + 2, :]
        lead = lead_ref[2 * k : 2 * k + 1, :]
        label = (column % 64 + 1).astype(F32) * jnp.broadcast_to(lead, (8, 128))
        whole = jnp.concatenate([first, second, jnp.zeros((4, 128), F32)], axis=0)
        whole = whole + sums + jnp.where(label_here, label, 0.0)
        sent_ref[owner] = whole.astype(BF16)


def digits_again(block):
    total = undigits(block)
    lane = iota((8, 128), 1)
    total = jnp.where(lane < 16, total, 0.0)
    high = total.astype(BF16).astype(F32)
    middle = (total - high).astype(BF16).astype(F32)
    low = (total - high - middle).astype(BF16).astype(F32)
    return high + pltpu.roll(middle, 16, 1) + pltpu.roll(low, 32, 1)


def finish(got_ref, solution_ref, phi_ref, wide):
    peers = got_ref.shape[0]
    wide[...] = got_ref[...].astype(F32)
    total = jnp.sum(wide[...], axis=0)
    sub = iota((8, 128), 0)
    sums = jnp.where(sub % 2 == 0, jnp.broadcast_to(total[4:5, :], (8, 128)), jnp.broadcast_to(total[5:6, :], (8, 128)))
    sums = undigits(sums)

    def pick(j):
        return jnp.broadcast_to(sums[:, j : j + 1], (8, 128))

    t11, t13, t33, s00, s02, s22, s24, s04, s44 = [pick(j) for j in range(9)]

    def norm(square):
        return jnp.sqrt(jnp.maximum(square, 0.0) + EPS)

    beta0 = norm(s00)
    alpha1 = norm(t11 / (beta0 * beta0))
    x2 = 1.0 / (beta0 * alpha1)
    x0 = -alpha1 / beta0
    beta1 = norm(x2 * x2 * s22 + 2.0 * x2 * x0 * s02 + x0 * x0 * s00)
    y3 = x2 / beta1
    y1 = x0 / beta1 - beta1 * x2
    alpha2 = norm(y3 * y3 * t33 + 2.0 * y3 * y1 * t13 + y1 * y1 * t11)
    ratio = alpha2 / beta1
    z4 = y3 / alpha2
    z2 = y1 / alpha2 - ratio * x2
    z0 = -ratio * x0
    beta2 = norm(
        z4 * z4 * s44 + z2 * z2 * s22 + z0 * z0 * s00 + 2.0 * (z4 * z2 * s24 + z4 * z0 * s04 + z2 * z0 * s02)
    )
    rho1 = jnp.sqrt(alpha1 * alpha1 + beta1 * beta1)
    cosine1 = alpha1 / rho1
    sine1 = beta1 / rho1
    phi1 = cosine1 * beta0
    phi_bar1 = sine1 * beta0
    theta = sine1 * alpha2
    rho_bar2 = -cosine1 * alpha2
    rho2 = jnp.sqrt(rho_bar2 * rho_bar2 + beta2 * beta2)
    cosine2 = rho_bar2 / rho2
    sine2 = beta2 / rho2
    phi2 = cosine2 * phi_bar1
    phi_ref[...] = sine2 * phi_bar1
    share1 = phi1 / rho1
    share2 = phi2 / rho2
    k1 = share1 * x2 + share2 * (y1 / alpha2 - (theta / rho1) * x2)
    k3 = share2 * y3 / alpha2

    out_rows = solution_ref.shape[0]
    place1 = jnp.zeros((out_rows, 128), F32)
    place3 = jnp.zeros((out_rows, 128), F32)
    row = iota((out_rows, 128), 0)
    slot = iota((out_rows, 128), 1) % 8
    for h in range(peers // 16):
        labels = jnp.broadcast_to(total[6 + h : 7 + h, :], (out_rows, 128)).astype(jnp.int32) - 1
        values = wide[16 * h : 16 * h + 16].reshape(128, 128).astype(BF16)
        hit1 = (labels * 2 + slot == row) & (slot < 2) & (labels >= 0)
        hit3 = (labels * 2 + slot - 2 == row) & (slot >= 2) & (slot < 4) & (labels >= 0)
        place1 = place1 + jnp.dot(hit1.astype(F32).astype(BF16), values, preferred_element_type=F32)
        place3 = place3 + jnp.dot(hit3.astype(F32).astype(BF16), values, preferred_element_type=F32)
    shape = (out_rows // 8, 8, 128)
    result = place1.reshape(shape) * k1[None] + place3.reshape(shape) * k3[None]
    solution_ref[...] = result.reshape(out_rows, 128)


def struct(shape, dtype):
    return jax.ShapeDtypeStruct(shape, dtype)


def on_device(tiles, coords, counts, rhs):
    n_row = lax.axis_size("row")
    n_col = lax.axis_size("col")
    tile = tiles[0, 0]
    places = coords[0, 0]
    slots = tile.shape[0]
    rows = 2 * slots
    piece_rows = rhs.shape[1] // 128 * 2

    def call(body, outs, scratch, specs):
        return pl.pallas_call(
            body,
            out_shape=outs,
            in_specs=specs,
            out_specs=[VMEM] * len(outs),
            scratch_shapes=[pltpu.VMEM(shape, dtype) for shape, dtype in scratch],
            compiler_params=pltpu.CompilerParams(vmem_limit_bytes=32 * 1024 * 1024),
        )

    def exchange(sent, axis):
        return lax.all_to_all(sent, axis, split_axis=0, concat_axis=0, tiled=True)

    work = [((rows, 128), F32)] * 3
    two = [SMEM, SMEM]
    piece = rhs.reshape(2, piece_rows // 2, 128).transpose(1, 0, 2).reshape(piece_rows, 128).astype(BF16)
    u_group = lax.all_gather(piece, "col", axis=0, tiled=True)
    sent, own_u = call(
        first_adjoint,
        [struct((n_row, rows + 8, 128), BF16), struct((rows, 128), BF16)],
        [((n_col * piece_rows, 128), F32)] + work[:2],
        two + [VMEM] * 2,
    )(places, counts, u_group, tile)
    got = exchange(sent, "row")
    sent, w1, v_map = call(
        first_forward,
        [struct((n_col, rows + 8, 128), BF16), struct((rows, 128), BF16), struct((n_row // 2, 128), F32)],
        work,
        two + [VMEM] * 2,
    )(places, counts, got, tile)
    got = exchange(sent, "col")
    sent, w2, u_map = call(
        second_adjoint,
        [struct((n_row, rows, 128), BF16), struct((rows, 128), BF16), struct((n_col // 2, 128), F32)],
        work,
        two + [VMEM] * 2,
    )(places, counts, got, tile)
    got = exchange(sent, "row")
    sent, w3, lead = call(
        second_forward,
        [struct((n_col, rows + 8, 128), BF16), struct((rows, 128), BF16), struct((rows, 128), F32)],
        work,
        two + [VMEM] * 8,
    )(places, counts, got, tile, v_map, u_map, w1, w2, own_u, piece)
    got = exchange(sent, "col")
    (sent,) = call(
        gather_sums,
        [struct((n_row, 8, 128), BF16)],
        [((n_col * rows, 128), BF16), ((8, 128), F32)] + work[:2],
        [SMEM] + [VMEM] * 5,
    )(places, got, u_map, w1, w3, lead)
    got = exchange(sent, "row")
    result, phi = call(
        finish,
        [struct((piece_rows, 128), F32), struct((8, 128), F32)],
        [((n_row, 8, 128), F32)],
        [VMEM],
    )(got)
    result = result.reshape(piece_rows // 2, 2, 128).transpose(1, 0, 2).reshape(2, piece_rows * 64)
    return (result, phi[0:2, 0])


def solution(mesh):
    return jax.shard_map(
        on_device,
        mesh=mesh,
        in_specs=(
            P("row", "col", None, None, None),
            P("row", "col", None, None),
            P("row", "col"),
            P(None, ("row", "col")),
        ),
        out_specs=(P(None, ("col", "row")), P()),
        check_vma=False,
    )
```

```python
import jax
import jax.numpy as jnp
from jax import lax
from jax.experimental import pallas as pl
from jax.experimental.pallas import tpu as pltpu
from jax.sharding import Mesh
from jax.sharding import PartitionSpec as P

EPS = 1e-06
F32 = jnp.float32
BF16 = jnp.bfloat16
ROW = ("z", "x")
COL = ("y", "core")
VMEM = pl.BlockSpec(memory_space=pltpu.VMEM)
SMEM = pl.BlockSpec(memory_space=pltpu.SMEM)


def iota(shape, dim):
    return lax.broadcasted_iota(jnp.int32, shape, dim)


def row_index():
    return lax.axis_index("z") * lax.axis_size("x") + lax.axis_index("x")


def col_index():
    return lax.axis_index("y") * lax.axis_size("core") + lax.axis_index("core")


def fill_keys(keys_ref, places_ref, count, axis, me):
    slots = places_ref.shape[1]
    for k in range(slots):
        block = jnp.where(k < count, places_ref[axis, k], -8)
        keys_ref[k : k + 1, :] = jnp.full((1, 128), block, jnp.int32).astype(F32)
    own = keys_ref.shape[0] - slots
    keys_ref[slots:, :] = (me * own + iota((own, 128), 0)).astype(F32)


def lane_keys(places_ref, count, axis):
    slots = places_ref.shape[1]
    slot = iota((8, 128), 1) % slots
    keys = jnp.full((8, 128), -1, jnp.int32)
    for k in range(slots):
        keys = jnp.where(slot == k, jnp.where(k < count, places_ref[axis, k], -1), keys)
    keys = keys.astype(F32)
    high = jnp.floor(keys * (1.0 / 64.0))
    sub = iota((8, 128), 0)
    return jnp.where(sub == 0, high, jnp.where(sub == 1, keys - 64.0 * high, 0.0)).astype(BF16)


def read_keys(got_ref, map_ref):
    rows = got_ref.shape[1] - 8
    quarter = iota((8, 128), 1) // 32
    for g in range(got_ref.shape[0] // 4):
        both = got_ref[4 * g, rows:, :].astype(F32)
        for i in range(1, 4):
            both = jnp.where(quarter == i, got_ref[4 * g + i, rows:, :].astype(F32), both)
        map_ref[g : g + 1, :] = both[0:1, :] * 64.0 + both[1:2, :]


def four_peers(got_ref, g):
    halves = []
    for r in range(2):
        halves.append(jnp.concatenate([got_ref[4 * g + i, 32 * r : 32 * r + 32, :] for i in range(4)], axis=0))
    return jnp.concatenate(halves, axis=1)


def sum_by_key(got_ref, map_ref, keys_ref):
    keys = keys_ref[...]
    total = jnp.zeros((keys.shape[0], 256), F32)
    for g in range(0, got_ref.shape[0] // 4, 2):
        match = jnp.concatenate([(keys == map_ref[g + i : g + i + 1, :]).astype(F32) for i in range(2)], axis=1)
        values = jnp.concatenate([four_peers(got_ref, g + i) for i in range(2)], axis=0)
        total = total + jnp.dot(match.astype(BF16), values, preferred_element_type=F32)
    return total


def products(held_ref, tile_ref, out_ref, adjoint):
    pair = iota((8, 128), 0) // 2
    for j in range(tile_ref.shape[0] // 4):
        rows = held_ref[8 * j : 8 * j + 8, :]
        left = jnp.concatenate([jnp.where(pair == i, rows, 0.0) for i in range(4)], axis=1).astype(BF16)
        blocks = [tile_ref[4 * j + i] for i in range(4)]
        right = jnp.concatenate(blocks, axis=0 if adjoint else 1)
        dims = (((1,), (0 if adjoint else 1,)), ((), ()))
        out_ref[8 * j : 8 * j + 8, :] = lax.dot_general(left, right, dims, preferred_element_type=F32)


def split_rows(ref):
    half = ref.shape[0] // 2
    return jnp.concatenate([ref[pl.ds(r, half, stride=2), :] for r in range(2)], axis=0)


def hold(held_ref, own):
    half = held_ref.shape[0] // 2
    for r in range(2):
        held_ref[pl.ds(r, half, stride=2), :] = own[:, 128 * r : 128 * r + 128].astype(F32)


def send_all(sent_ref, values, extra):
    rows = values.shape[0]
    for peer in range(sent_ref.shape[0]):
        sent_ref[peer, 0:rows, :] = values
        if extra is not None:
            sent_ref[peer, rows:, :] = extra


def begin(rhs_ref, sent_ref, piece_ref, rows):
    for b in range(rows.shape[0] // 2):
        rows[2 * b : 2 * b + 2, :] = rhs_ref[:, 128 * b : 128 * b + 128]
    send_all(sent_ref, rows[...].astype(BF16), None)
    half = rows.shape[0] // 2
    piece_ref[...] = jnp.concatenate([rows[pl.ds(r, half, stride=2), :] for r in range(2)], axis=1).astype(BF16)


def first_adjoint(places_ref, counts_ref, u_ref, tile_ref, sent_ref, own_u_ref, held, out):
    count = counts_ref[0, 0]
    cores = lax.axis_size("core")
    chips = lax.axis_size("y")
    span = u_ref.shape[0] // (cores * chips)
    for k in range(places_ref.shape[1]):
        block = places_ref[0, k]
        owner = block // span
        row = ((owner % cores) * chips + owner // cores) * span + block % span
        held[2 * k : 2 * k + 2, :] = u_ref[row].astype(F32) * (k < count).astype(F32)
    own_u_ref[...] = split_rows(held).astype(BF16)
    products(held, tile_ref, out, True)
    send_all(sent_ref, split_rows(out).astype(BF16), lane_keys(places_ref, count, 1))


def keep(w, w_ref, piece_ref, held):
    slots = held.shape[0] // 2
    w = w.astype(BF16)
    own = w[0:slots, :]
    piece_ref[...] = w[slots:, :]
    hold(held, own)
    if w_ref is not None:
        w_ref[...] = jnp.concatenate([own[:, 0:128], own[:, 128:256]], axis=0)


def first_forward(places_ref, counts_ref, got_ref, tile_ref, sent_ref, piece_ref, map_ref, keys, held, out):
    count = counts_ref[0, 0]
    fill_keys(keys, places_ref, count, 1, row_index())
    read_keys(got_ref, map_ref)
    keep(sum_by_key(got_ref, map_ref, keys), None, piece_ref, held)
    products(held, tile_ref, out, False)
    send_all(sent_ref, split_rows(out).astype(BF16), lane_keys(places_ref, count, 0))


def second_adjoint(places_ref, counts_ref, got_ref, tile_ref, sent_ref, w_ref, piece_ref, map_ref, keys, held, out):
    fill_keys(keys, places_ref, counts_ref[0, 0], 0, col_index())
    read_keys(got_ref, map_ref)
    keep(sum_by_key(got_ref, map_ref, keys), w_ref, piece_ref, held)
    products(held, tile_ref, out, True)
    send_all(sent_ref, split_rows(out).astype(BF16), None)


def sum_halves(first, second):
    folds = []
    for values in (first, second):
        fold = jnp.sum(values.reshape(values.shape[0] // 8, 8, 128), axis=0)
        folds.append(fold + pltpu.roll(fold, 4, 0))
    return jnp.sum(jnp.where(iota((8, 128), 0) < 4, folds[0], folds[1]), axis=1, keepdims=True)


def sum_piece(values):
    return sum_halves(values[:, 0:128], values[:, 128:256])


def sum_slots(values):
    half = values.shape[0] // 2
    return sum_halves(values[0:half, :], values[half:, :])


def three_parts(values):
    values = jnp.where(iota(values.shape, 1) < 16, values, 0.0)
    high = values.astype(BF16).astype(F32)
    middle = (values - high).astype(BF16).astype(F32)
    low = (values - high - middle).astype(BF16).astype(F32)
    return high + pltpu.roll(middle, 16, 1) + pltpu.roll(low, 32, 1)


def whole_sums(parts):
    return parts + pltpu.roll(parts, 112, 1) + pltpu.roll(parts, 96, 1)


def second_forward(
    places_ref, counts_ref, got_ref, tile_ref, map_ref, w1_ref, w2_ref, u0_ref, own_w2_ref, own_u_ref,
    sent_ref, piece_ref, keys, held, out,
):
    fill_keys(keys, places_ref, counts_ref[0, 0], 1, row_index())
    keep(sum_by_key(got_ref, map_ref, keys), None, piece_ref, held)
    products(held, tile_ref, out, False)
    sent = split_rows(out).astype(BF16)
    w1 = w1_ref[...].astype(F32)
    w2 = w2_ref[...].astype(F32)
    u0 = u0_ref[...].astype(F32)
    w3 = piece_ref[...].astype(F32)
    c4 = sent.astype(F32)
    sums = [
        sum_piece(w1 * w1),
        sum_piece(w1 * w3),
        sum_piece(w3 * w3),
        sum_piece(u0 * u0),
        sum_piece(u0 * w2),
        sum_piece(w2 * w2),
        sum_slots(c4 * own_w2_ref[...].astype(F32)),
        sum_slots(c4 * own_u_ref[...].astype(F32)),
    ]
    lane = iota((8, 128), 1)
    block = jnp.zeros((8, 128), F32)
    for j, value in enumerate(sums):
        block = jnp.where(lane == j, value, block)
    send_all(sent_ref, sent, three_parts(block).astype(BF16))


def gather_sums(got_ref, map_ref, sent_ref):
    peers = got_ref.shape[0]
    rows = got_ref.shape[1] - 8
    partial = got_ref[0, rows:, :].astype(F32)
    for peer in range(1, peers):
        partial = partial + got_ref[peer, rows:, :].astype(F32)
    groups = peers // 4
    values = jnp.concatenate([four_peers(got_ref, g) for g in range(groups)], axis=0)
    square = jnp.zeros((8, 256), F32)
    for g in range(groups):
        column = jnp.transpose(jnp.broadcast_to(map_ref[g : g + 1, :], (128, 128)))
        match = [jnp.where(column == map_ref[h : h + 1, :], 1.0 if h == g else 2.0, 0.0) for h in range(g, groups)]
        total = jnp.dot(jnp.concatenate(match, axis=1).astype(BF16), values[128 * g :, :], preferred_element_type=F32)
        square = square + jnp.sum((values[128 * g : 128 * g + 128, :].astype(F32) * total).reshape(16, 8, 256), axis=0)
    last = sum_piece(square)
    lane = iota((8, 128), 1)
    block = jnp.where(lane == 8, last, whole_sums(partial))
    block = block + pltpu.roll(block, 1, 0)
    block = three_parts(block + pltpu.roll(block, 2, 0)).astype(BF16).astype(F32)
    block = jnp.concatenate([block[3:4, :], block[7:8, :]], axis=0).astype(BF16)
    for peer in range(sent_ref.shape[0]):
        sent_ref[peer] = block


def finish(got_ref, w1_ref, w3_ref, solution_ref, phi_ref):
    total = jnp.sum(got_ref[...].astype(F32), axis=0)
    first = iota((8, 128), 0) < 4
    sums = whole_sums(jnp.where(first, total[0:1, :], total[1:2, :]))

    def pick(j):
        return jnp.broadcast_to(sums[:, j : j + 1], (8, 128))

    t11, t13, t33, s00, s02, s22, s24, s04, s44 = [pick(j) for j in range(9)]

    def norm(square):
        return jnp.sqrt(jnp.maximum(square, 0.0) + EPS)

    beta0 = norm(s00)
    alpha1 = norm(t11 / (beta0 * beta0))
    x2 = 1.0 / (beta0 * alpha1)
    x0 = -alpha1 / beta0
    beta1 = norm(x2 * x2 * s22 + 2.0 * x2 * x0 * s02 + x0 * x0 * s00)
    y3 = x2 / beta1
    y1 = x0 / beta1 - beta1 * x2
    alpha2 = norm(y3 * y3 * t33 + 2.0 * y3 * y1 * t13 + y1 * y1 * t11)
    ratio = alpha2 / beta1
    z4 = y3 / alpha2
    z2 = y1 / alpha2 - ratio * x2
    z0 = -ratio * x0
    beta2 = norm(
        z4 * z4 * s44 + z2 * z2 * s22 + z0 * z0 * s00 + 2.0 * (z4 * z2 * s24 + z4 * z0 * s04 + z2 * z0 * s02)
    )
    rho1 = jnp.sqrt(alpha1 * alpha1 + beta1 * beta1)
    cosine1 = alpha1 / rho1
    sine1 = beta1 / rho1
    phi1 = cosine1 * beta0
    phi_bar1 = sine1 * beta0
    theta = sine1 * alpha2
    rho_bar2 = -cosine1 * alpha2
    rho2 = jnp.sqrt(rho_bar2 * rho_bar2 + beta2 * beta2)
    cosine2 = rho_bar2 / rho2
    sine2 = beta2 / rho2
    phi2 = cosine2 * phi_bar1
    phi_bar2 = sine2 * phi_bar1
    share1 = phi1 / rho1
    share2 = phi2 / rho2
    k1 = share1 * x2 + share2 * (y1 / alpha2 - (theta / rho1) * x2)
    k3 = share2 * y3 / alpha2

    phi_ref[...] = jnp.where(iota((1, 128), 1) == 0, phi_bar2[0:1, :], phi_bar2[4:5, :])[:, 0:2]
    half = w1_ref.shape[0]
    for r in range(2):
        w1 = w1_ref[:, 128 * r : 128 * r + 128].astype(F32)
        w3 = w3_ref[:, 128 * r : 128 * r + 128].astype(F32)
        solution_ref[pl.ds(r, half, stride=2), :] = w1 * k1[4 * r : 4 * r + 1, :] + w3 * k3[4 * r : 4 * r + 1, :]


def struct(shape, dtype):
    return jax.ShapeDtypeStruct(shape, dtype)


def on_device(tiles, coords, counts, rhs):
    chips = lax.axis_size("y")
    n_row = lax.axis_size("z") * lax.axis_size("x")
    n_col = chips * lax.axis_size("core")
    slots = tiles.shape[2]
    rows = 2 * slots
    span = rhs.shape[1] // 128
    places = coords[0, 0].T

    def call(body, specs, outs, scratch, *operands):
        return pl.pallas_call(
            body,
            out_shape=outs,
            in_specs=specs,
            out_specs=[VMEM] * len(outs),
            scratch_shapes=scratch,
            compiler_params=pltpu.CompilerParams(vmem_limit_bytes=32 * 1024 * 1024),
        )(*operands)

    def exchange(sent, axis):
        return lax.all_to_all(sent, axis, split_axis=0, concat_axis=0, tiled=True)

    def exchange_col(sent):
        return lax.all_gather(exchange(sent, "y"), "core", axis=0, tiled=True)

    wide = pltpu.VMEM((rows, 128), F32)
    keys = pltpu.VMEM((slots + span, 128), F32)
    two = [SMEM, SMEM]
    piece = struct((span, 256), BF16)
    own = struct((rows, 128), BF16)
    tile = tiles[0, 0]
    sent, u0 = call(
        begin,
        [VMEM],
        [struct((chips, 2 * span, 128), BF16), piece],
        [pltpu.VMEM((2 * span, 128), F32)],
        rhs,
    )
    u_group = exchange_col(sent).reshape(n_col * span, 2, 128)
    sent, own_u = call(
        first_adjoint,
        two + [VMEM] * 2,
        [struct((n_row, rows + 8, 128), BF16), own],
        [wide, wide],
        places, counts, u_group, tile,
    )
    sent, w1, v_map = call(
        first_forward,
        two + [VMEM] * 2,
        [struct((chips, rows + 8, 128), BF16), piece, struct((n_row // 4, 128), F32)],
        [keys, wide, wide],
        places, counts, exchange(sent, ROW), tile,
    )
    sent, own_w2, w2, u_map = call(
        second_adjoint,
        two + [VMEM] * 2,
        [struct((n_row, rows, 128), BF16), own, piece, struct((n_col // 4, 128), F32)],
        [keys, wide, wide],
        places, counts, exchange_col(sent), tile,
    )
    sent, w3 = call(
        second_forward,
        two + [VMEM] * 8,
        [struct((chips, rows + 8, 128), BF16), piece],
        [keys, wide, wide],
        places, counts, exchange(sent, ROW), tile, v_map, w1, w2, u0, own_w2, own_u,
    )
    (sent,) = call(
        gather_sums,
        [VMEM] * 2,
        [struct((n_row, 2, 128), BF16)],
        [],
        exchange_col(sent), u_map,
    )
    result, phi_bar = call(
        finish,
        [VMEM] * 3,
        [struct((2 * span, 128), F32), struct((1, 2), F32)],
        [],
        exchange(sent, ROW), w1, w3,
    )
    result = result.reshape(span, 2, 128).transpose(1, 0, 2).reshape(2, span * 128)
    return (result, phi_bar.reshape(2))


def solution(mesh):
    n_row, n_col = mesh.devices.shape
    fine = Mesh(mesh.devices.reshape(n_row // 4, 4, n_col // 2, 2), ROW + COL)
    return jax.shard_map(
        on_device,
        mesh=fine,
        in_specs=(P(ROW, COL, None, None, None), P(ROW, COL, None, None), P(ROW, COL), P(None, ROW + COL)),
        out_specs=(P(None, COL + ROW), P()),
        check_vma=False,
    )
```

```python
import jax
import jax.numpy as jnp
from jax import lax
from jax.experimental import pallas as pl
from jax.experimental.pallas import tpu as pltpu
from jax.sharding import Mesh
from jax.sharding import PartitionSpec as P

EPS = 1e-06
F32 = jnp.float32
BF16 = jnp.bfloat16
ROW = ("z", "x")
COL = ("y", "core")
VMEM = pl.BlockSpec(memory_space=pltpu.VMEM)
SMEM = pl.BlockSpec(memory_space=pltpu.SMEM)


def iota(shape, dim):
    return lax.broadcasted_iota(jnp.int32, shape, dim)


def row_index():
    return lax.axis_index("z") * lax.axis_size("x") + lax.axis_index("x")


def col_index():
    return lax.axis_index("y") * lax.axis_size("core") + lax.axis_index("core")


def slot_keys(places_ref, count, axis):
    slots = places_ref.shape[1]
    row = iota((slots, 128), 0)
    keys = jnp.full((slots, 128), -8, jnp.int32)
    for k in range(slots):
        keys = jnp.where(row == k, jnp.where(k < count, places_ref[axis, k], -8), keys)
    return keys.astype(F32)


def with_range(slot_ref, me, span):
    return jnp.concatenate([slot_ref[...], (me * span + iota((span, 128), 0)).astype(F32)], axis=0)


def lane_keys(places_ref, count, axis):
    slots = places_ref.shape[1]
    slot = iota((8, 128), 1) % slots
    keys = jnp.full((8, 128), -1, jnp.int32)
    for k in range(slots):
        keys = jnp.where(slot == k, jnp.where(k < count, places_ref[axis, k], -1), keys)
    keys = keys.astype(F32)
    high = jnp.floor(keys * (1.0 / 64.0))
    sub = iota((8, 128), 0)
    return jnp.where(sub == 0, high, jnp.where(sub == 1, keys - 64.0 * high, 0.0)).astype(BF16)


def read_keys(got_ref, map_ref):
    rows = got_ref.shape[1] - 8
    quarter = iota((8, 128), 1) // 32
    for g in range(got_ref.shape[0] // 4):
        both = got_ref[4 * g, rows:, :].astype(F32)
        for i in range(1, 4):
            both = jnp.where(quarter == i, got_ref[4 * g + i, rows:, :].astype(F32), both)
        map_ref[g : g + 1, :] = both[0:1, :] * 64.0 + both[1:2, :]


def four_peers(got_ref, g):
    halves = []
    for r in range(2):
        halves.append(jnp.concatenate([got_ref[4 * g + i, 32 * r : 32 * r + 32, :] for i in range(4)], axis=0))
    return jnp.concatenate(halves, axis=1)


def sum_by_key(got_ref, map_ref, keys):
    total = jnp.zeros((keys.shape[0], 256), F32)
    for g in range(0, got_ref.shape[0] // 4, 2):
        match = jnp.concatenate([(keys == map_ref[g + i : g + i + 1, :]).astype(F32) for i in range(2)], axis=1)
        values = jnp.concatenate([four_peers(got_ref, g + i) for i in range(2)], axis=0)
        total = total + jnp.dot(match.astype(BF16), values, preferred_element_type=F32)
    return total


def products(held_ref, tile_ref, out_ref, adjoint):
    pair = iota((8, 128), 0) // 2
    for j in range(tile_ref.shape[0] // 4):
        rows = held_ref[8 * j : 8 * j + 8, :]
        left = jnp.concatenate([jnp.where(pair == i, rows, 0.0) for i in range(4)], axis=1).astype(BF16)
        blocks = [tile_ref[4 * j + i] for i in range(4)]
        right = jnp.concatenate(blocks, axis=0 if adjoint else 1)
        dims = (((1,), (0 if adjoint else 1,)), ((), ()))
        out_ref[8 * j : 8 * j + 8, :] = lax.dot_general(left, right, dims, preferred_element_type=F32)


def split_rows(ref):
    half = ref.shape[0] // 2
    return jnp.concatenate([ref[pl.ds(r, half, stride=2), :] for r in range(2)], axis=0)


def hold(held_ref, own):
    half = held_ref.shape[0] // 2
    for r in range(2):
        held_ref[pl.ds(r, half, stride=2), :] = own[:, 128 * r : 128 * r + 128].astype(F32)


def send_all(sent_ref, values, extra):
    rows = values.shape[0]
    for peer in range(sent_ref.shape[0]):
        sent_ref[peer, 0:rows, :] = values
        if extra is not None:
            sent_ref[peer, rows:, :] = extra


def begin(places_ref, counts_ref, rhs_ref, sent_ref, piece_ref, slot_v_ref, slot_u_ref, lane_v_ref, lane_u_ref, rows):
    for b in range(rows.shape[0] // 2):
        rows[2 * b : 2 * b + 2, :] = rhs_ref[:, 128 * b : 128 * b + 128]
    send_all(sent_ref, rows[...].astype(BF16), None)
    half = rows.shape[0] // 2
    piece_ref[...] = jnp.concatenate([rows[pl.ds(r, half, stride=2), :] for r in range(2)], axis=1).astype(BF16)
    count = counts_ref[0, 0]
    for axis, slot_ref, lane_ref in ((0, slot_u_ref, lane_u_ref), (1, slot_v_ref, lane_v_ref)):
        slot_ref[...] = slot_keys(places_ref, count, axis)
        lane_ref[...] = lane_keys(places_ref, count, axis)


def first_adjoint(places_ref, counts_ref, lane_ref, u_ref, tile_ref, sent_ref, own_u_ref, held, out):
    count = counts_ref[0, 0]
    cores = lax.axis_size("core")
    chips = lax.axis_size("y")
    span = u_ref.shape[0] // (cores * chips)
    for k in range(places_ref.shape[1]):
        block = places_ref[0, k]
        owner = block // span
        row = ((owner % cores) * chips + owner // cores) * span + block % span
        held[2 * k : 2 * k + 2, :] = u_ref[row].astype(F32) * (k < count).astype(F32)
    own_u_ref[...] = split_rows(held).astype(BF16)
    products(held, tile_ref, out, True)
    send_all(sent_ref, split_rows(out).astype(BF16), lane_ref[...])


def keep(w, w_ref, piece_ref, held):
    slots = held.shape[0] // 2
    w = w.astype(BF16)
    own = w[0:slots, :]
    piece_ref[...] = w[slots:, :]
    hold(held, own)
    w_ref[...] = jnp.concatenate([own[:, 0:128], own[:, 128:256]], axis=0)


def first_forward(slot_ref, lane_ref, got_ref, tile_ref, sent_ref, w_ref, piece_ref, map_ref, held, out):
    read_keys(got_ref, map_ref)
    keys = with_range(slot_ref, row_index(), piece_ref.shape[0])
    keep(sum_by_key(got_ref, map_ref, keys), w_ref, piece_ref, held)
    products(held, tile_ref, out, False)
    send_all(sent_ref, split_rows(out).astype(BF16), lane_ref[...])


def second_adjoint(slot_ref, lane_ref, got_ref, tile_ref, sent_ref, w_ref, piece_ref, map_ref, held, out):
    read_keys(got_ref, map_ref)
    keys = with_range(slot_ref, col_index(), piece_ref.shape[0])
    keep(sum_by_key(got_ref, map_ref, keys), w_ref, piece_ref, held)
    products(held, tile_ref, out, True)
    send_all(sent_ref, split_rows(out).astype(BF16), lane_ref[...])


def regroup(map_ref, got_ref, sent_ref, line_ref):
    read_keys(got_ref, line_ref)
    target = map_ref[pl.ds(lax.axis_index("z"), 1), :]
    column = jnp.transpose(jnp.broadcast_to(target, (128, 128)))
    total = sum_by_key(got_ref, line_ref, column).astype(BF16)
    for peer in range(sent_ref.shape[0]):
        for r in range(2):
            sent_ref[peer, 32 * r : 32 * r + 32, :] = total[32 * peer : 32 * peer + 32, 128 * r : 128 * r + 128]


def leaders(map_ref, slot_ref, me):
    keys = slot_ref[...]
    quarter = iota(keys.shape, 1) // 32
    earlier = jnp.zeros(keys.shape, F32)
    for g in range(map_ref.shape[0]):
        earlier = earlier + ((keys == map_ref[g : g + 1, :]) & (4 * g + quarter < me)).astype(F32)
    count = jnp.sum(earlier, axis=1, keepdims=True)
    return ((count == 0.0) & (keys >= 0.0)).astype(F32)


def sum_halves(first, second):
    folds = []
    for values in (first, second):
        fold = jnp.sum(values.reshape(values.shape[0] // 8, 8, 128), axis=0)
        folds.append(fold + pltpu.roll(fold, 4, 0))
    return jnp.sum(jnp.where(iota((8, 128), 0) < 4, folds[0], folds[1]), axis=1, keepdims=True)


def sum_piece(values):
    return sum_halves(values[:, 0:128], values[:, 128:256])


def sum_slots(values):
    half = values.shape[0] // 2
    return sum_halves(values[0:half, :], values[half:, :])


def three_parts(values):
    values = jnp.where(iota(values.shape, 1) < 16, values, 0.0)
    high = values.astype(BF16).astype(F32)
    middle = (values - high).astype(BF16).astype(F32)
    low = (values - high - middle).astype(BF16).astype(F32)
    return high + pltpu.roll(middle, 16, 1) + pltpu.roll(low, 32, 1)


def whole_sums(parts):
    return parts + pltpu.roll(parts, 112, 1) + pltpu.roll(parts, 96, 1)


def second_forward(
    slot_ref, map_ref, got_ref, tile_ref, own_w1_ref, w2_ref, u0_ref, own_w2_ref, own_u_ref,
    sent_ref, lead_w3_ref, lead_ref, held, out,
):
    w3 = got_ref[0].astype(F32)
    for peer in range(1, got_ref.shape[0]):
        w3 = w3 + got_ref[peer].astype(F32)
    w3 = w3.astype(BF16).astype(F32)
    half = w3.shape[0] // 2
    for r in range(2):
        held[pl.ds(r, half, stride=2), :] = w3[half * r : half * r + half, :]
    products(held, tile_ref, out, False)
    sent = split_rows(out).astype(BF16)
    lead = leaders(map_ref, slot_ref, row_index())
    lead_ref[...] = lead
    lead = jnp.concatenate([lead, lead], axis=0)
    lead_w3 = w3 * lead
    for r in range(2):
        lead_w3_ref[pl.ds(r, half, stride=2), :] = lead_w3[half * r : half * r + half, :]
    w1 = own_w1_ref[...].astype(F32)
    w2 = w2_ref[...].astype(F32)
    u0 = u0_ref[...].astype(F32)
    c4 = sent.astype(F32)
    sums = [
        sum_slots(w1 * w1 * lead),
        sum_slots(w1 * lead_w3),
        sum_slots(w3 * lead_w3),
        sum_piece(u0 * u0),
        sum_piece(u0 * w2),
        sum_piece(w2 * w2),
        sum_slots(c4 * own_w2_ref[...].astype(F32)),
        sum_slots(c4 * own_u_ref[...].astype(F32)),
    ]
    lane = iota((8, 128), 1)
    block = jnp.zeros((8, 128), F32)
    for j, value in enumerate(sums):
        block = jnp.where(lane == j, value, block)
    send_all(sent_ref, sent, three_parts(block).astype(BF16))


def gather_sums(places_ref, got_ref, map_ref, lead_w3_ref, lead_ref, sent_ref):
    peers = got_ref.shape[0]
    rows = got_ref.shape[1] - 8
    partial = got_ref[0, rows:, :].astype(F32)
    for peer in range(1, peers):
        partial = partial + got_ref[peer, rows:, :].astype(F32)
    groups = peers // 4
    values = jnp.concatenate([four_peers(got_ref, g) for g in range(groups)], axis=0)
    square = jnp.zeros((8, 256), F32)
    for g in range(groups):
        column = jnp.transpose(jnp.broadcast_to(map_ref[g : g + 1, :], (128, 128)))
        match = [jnp.where(column == map_ref[h : h + 1, :], 1.0 if h == g else 2.0, 0.0) for h in range(g, groups)]
        total = jnp.dot(jnp.concatenate(match, axis=1).astype(BF16), values[128 * g :, :], preferred_element_type=F32)
        square = square + jnp.sum((values[128 * g : 128 * g + 128, :].astype(F32) * total).reshape(16, 8, 256), axis=0)
    lane = iota((8, 128), 1)
    block = jnp.where(lane == 8, sum_piece(square), whole_sums(partial))
    block = block + pltpu.roll(block, 1, 0)
    block = three_parts(block + pltpu.roll(block, 2, 0))
    block = jnp.concatenate([block[3:4, :], block[7:8, :]], axis=0)
    span = 64
    here = (iota((2, 128), 1) == 64 + row_index()) & (iota((2, 128), 0) == 0)
    for k in range(places_ref.shape[1]):
        place = places_ref[1, k]
        label = (place % span + 1).astype(F32) * lead_ref[k : k + 1, :]
        second = block + jnp.where(here, label, 0.0)
        whole = jnp.concatenate([lead_w3_ref[2 * k : 2 * k + 2, :], second], axis=0)
        sent_ref[place // span] = whole.astype(BF16)


def finish(got_ref, w1_ref, solution_ref, phi_ref, wide):
    wide[...] = got_ref[...].astype(F32)
    peers = got_ref.shape[0] // 4
    parts = [wide[pl.ds(i, peers, stride=4), :] for i in range(4)]
    total = jnp.concatenate([jnp.sum(parts[i], axis=0, keepdims=True) for i in (2, 3)], axis=0)
    half = w1_ref.shape[0]
    labels = pltpu.roll(jnp.broadcast_to(total[0:1, :], (half, 128)), 64, 1)
    match = (labels == (iota((half, 128), 0) + 1).astype(F32)) & (iota((half, 128), 1) < peers)
    values = jnp.concatenate(parts[0:2], axis=1)
    values = jnp.concatenate([values, jnp.zeros((128 - peers, 256), F32)], axis=0).astype(BF16)
    w3 = jnp.dot(match.astype(F32).astype(BF16), values, preferred_element_type=F32)
    first = iota((8, 128), 0) < 4
    sums = whole_sums(jnp.where(first, total[0:1, :], total[1:2, :]))

    def pick(j):
        return jnp.broadcast_to(sums[:, j : j + 1], (8, 128))

    t11, t13, t33, s00, s02, s22, s24, s04, s44 = [pick(j) for j in range(9)]

    def norm(square):
        return jnp.sqrt(jnp.maximum(square, 0.0) + EPS)

    beta0 = norm(s00)
    alpha1 = norm(t11 / (beta0 * beta0))
    x2 = 1.0 / (beta0 * alpha1)
    x0 = -alpha1 / beta0
    beta1 = norm(x2 * x2 * s22 + 2.0 * x2 * x0 * s02 + x0 * x0 * s00)
    y3 = x2 / beta1
    y1 = x0 / beta1 - beta1 * x2
    alpha2 = norm(y3 * y3 * t33 + 2.0 * y3 * y1 * t13 + y1 * y1 * t11)
    ratio = alpha2 / beta1
    z4 = y3 / alpha2
    z2 = y1 / alpha2 - ratio * x2
    z0 = -ratio * x0
    beta2 = norm(
        z4 * z4 * s44 + z2 * z2 * s22 + z0 * z0 * s00 + 2.0 * (z4 * z2 * s24 + z4 * z0 * s04 + z2 * z0 * s02)
    )
    rho1 = jnp.sqrt(alpha1 * alpha1 + beta1 * beta1)
    cosine1 = alpha1 / rho1
    sine1 = beta1 / rho1
    phi1 = cosine1 * beta0
    phi_bar1 = sine1 * beta0
    theta = sine1 * alpha2
    rho_bar2 = -cosine1 * alpha2
    rho2 = jnp.sqrt(rho_bar2 * rho_bar2 + beta2 * beta2)
    cosine2 = rho_bar2 / rho2
    sine2 = beta2 / rho2
    phi2 = cosine2 * phi_bar1
    phi_bar2 = sine2 * phi_bar1
    share1 = phi1 / rho1
    share2 = phi2 / rho2
    k1 = share1 * x2 + share2 * (y1 / alpha2 - (theta / rho1) * x2)
    k3 = share2 * y3 / alpha2

    phi_ref[...] = jnp.where(iota((1, 128), 1) == 0, phi_bar2[0:1, :], phi_bar2[4:5, :])[:, 0:2]
    for r in range(2):
        lanes = slice(128 * r, 128 * r + 128)
        scale1, scale3 = k1[4 * r : 4 * r + 1, :], k3[4 * r : 4 * r + 1, :]
        solution_ref[pl.ds(r, half, stride=2), :] = w1_ref[:, lanes].astype(F32) * scale1 + w3[:, lanes] * scale3


def struct(shape, dtype):
    return jax.ShapeDtypeStruct(shape, dtype)


def on_device(tiles, coords, counts, rhs):
    chips = lax.axis_size("y")
    n_row = lax.axis_size("z") * lax.axis_size("x")
    n_col = chips * lax.axis_size("core")
    slots = tiles.shape[2]
    rows = 2 * slots
    span = rhs.shape[1] // 128
    places = coords[0, 0].T

    def call(body, specs, outs, scratch, *operands):
        return pl.pallas_call(
            body,
            out_shape=outs,
            in_specs=specs,
            out_specs=[VMEM] * len(outs),
            scratch_shapes=scratch,
            compiler_params=pltpu.CompilerParams(vmem_limit_bytes=32 * 1024 * 1024),
        )(*operands)

    def exchange(sent, axis):
        return lax.all_to_all(sent, axis, split_axis=0, concat_axis=0, tiled=True)

    def exchange_col(sent):
        return lax.all_gather(exchange(sent, "y"), "core", axis=0, tiled=True)

    wide = pltpu.VMEM((rows, 128), F32)
    piece = struct((span, 256), BF16)
    own = struct((rows, 128), BF16)
    own_wide = struct((rows, 128), F32)
    slot_table = struct((slots, 128), F32)
    lane_table = struct((8, 128), BF16)
    tile = tiles[0, 0]
    sent, u0, slot_v, slot_u, lane_v, lane_u = call(
        begin,
        [SMEM, SMEM, VMEM],
        [struct((chips, 2 * span, 128), BF16), piece, slot_table, slot_table, lane_table, lane_table],
        [pltpu.VMEM((2 * span, 128), F32)],
        places, counts, rhs,
    )
    u_group = exchange_col(sent).reshape(n_col * span, 2, 128)
    sent, own_u = call(
        first_adjoint,
        [SMEM, SMEM] + [VMEM] * 3,
        [struct((n_row, rows + 8, 128), BF16), own],
        [wide, wide],
        places, counts, lane_v, u_group, tile,
    )
    sent, own_w1, w1, v_map = call(
        first_forward,
        [VMEM] * 4,
        [struct((chips, rows + 8, 128), BF16), own, piece, struct((n_row // 4, 128), F32)],
        [wide, wide],
        slot_v, lane_u, exchange(sent, ROW), tile,
    )
    sent, own_w2, w2, u_map = call(
        second_adjoint,
        [VMEM] * 4,
        [struct((lax.axis_size("z"), rows + 8, 128), BF16), own, piece, struct((n_col // 4, 128), F32)],
        [wide, wide],
        slot_u, lane_v, exchange_col(sent), tile,
    )
    (sent,) = call(
        regroup,
        [VMEM] * 2,
        [struct((lax.axis_size("x"), rows, 128), BF16)],
        [pltpu.VMEM((lax.axis_size("z") // 4, 128), F32)],
        v_map, exchange(sent, "z"),
    )
    sent, lead_w3, lead = call(
        second_forward,
        [VMEM] * 9,
        [struct((chips, rows + 8, 128), BF16), own_wide, slot_table],
        [wide, wide],
        slot_v, v_map, exchange(sent, "x"), tile, own_w1, w2, u0, own_w2, own_u,
    )
    (sent,) = call(
        gather_sums,
        [SMEM] + [VMEM] * 4,
        [struct((n_row, 4, 128), BF16)],
        [],
        places, exchange_col(sent), u_map, lead_w3, lead,
    )
    result, phi_bar = call(
        finish,
        [VMEM] * 2,
        [struct((2 * span, 128), F32), struct((1, 2), F32)],
        [pltpu.VMEM((n_row * 4, 128), F32)],
        exchange(sent, ROW).reshape(n_row * 4, 128), w1,
    )
    result = result.reshape(span, 2, 128).transpose(1, 0, 2).reshape(2, span * 128)
    return (result, phi_bar.reshape(2))


def solution(mesh):
    n_row, n_col = mesh.devices.shape
    fine = Mesh(mesh.devices.reshape(n_row // 4, 4, n_col // 2, 2), ROW + COL)
    return jax.shard_map(
        on_device,
        mesh=fine,
        in_specs=(P(ROW, COL, None, None, None), P(ROW, COL, None, None), P(ROW, COL), P(None, ROW + COL)),
        out_specs=(P(None, COL + ROW), P()),
        check_vma=False,
    )
```

```python
import functools

import jax
import jax.numpy as jnp
from jax import lax
from jax.experimental import pallas as pl
from jax.experimental.pallas import tpu as pltpu
from jax.sharding import Mesh
from jax.sharding import PartitionSpec as P

EPS = 1e-06
F32 = jnp.float32
BF16 = jnp.bfloat16
ROW = ("z", "x")
COL = ("y", "core")
VMEM = pl.BlockSpec(memory_space=pltpu.VMEM)
SMEM = pl.BlockSpec(memory_space=pltpu.SMEM)


def iota(shape, dim):
    return lax.broadcasted_iota(jnp.int32, shape, dim)


def row_index():
    return lax.axis_index("z") * lax.axis_size("x") + lax.axis_index("x")


def col_index():
    return lax.axis_index("y") * lax.axis_size("core") + lax.axis_index("core")


def slot_keys(places_ref, count, axis):
    slots = places_ref.shape[1]
    row = iota((slots, 128), 0)
    keys = jnp.full((slots, 128), -8, jnp.int32)
    for k in range(slots):
        keys = jnp.where(row == k, jnp.where(k < count, places_ref[axis, k], -8), keys)
    return keys.astype(F32)


def with_range(slot_ref, me, span):
    return jnp.concatenate([slot_ref[...], (me * span + iota((span, 128), 0)).astype(F32)], axis=0)


def lane_keys(places_ref, count, axis):
    slots = places_ref.shape[1]
    slot = iota((8, 128), 1) % slots
    keys = jnp.full((8, 128), -1, jnp.int32)
    for k in range(slots):
        keys = jnp.where(slot == k, jnp.where(k < count, places_ref[axis, k], -1), keys)
    keys = keys.astype(F32)
    high = jnp.floor(keys * (1.0 / 64.0))
    sub = iota((8, 128), 0)
    return jnp.where(sub == 0, high, jnp.where(sub == 1, keys - 64.0 * high, 0.0)).astype(BF16)


def read_keys(got_ref, map_ref):
    rows = got_ref.shape[1] - 8
    quarter = iota((8, 128), 1) // 32
    for g in range(got_ref.shape[0] // 4):
        both = got_ref[4 * g, rows:, :].astype(F32)
        for i in range(1, 4):
            both = jnp.where(quarter == i, got_ref[4 * g + i, rows:, :].astype(F32), both)
        map_ref[g : g + 1, :] = both[0:1, :] * 64.0 + both[1:2, :]


def four_peers(got_ref, g):
    halves = []
    for r in range(2):
        halves.append(jnp.concatenate([got_ref[4 * g + i, 32 * r : 32 * r + 32, :] for i in range(4)], axis=0))
    return jnp.concatenate(halves, axis=1)


def sum_by_key(got_ref, map_ref, keys):
    total = jnp.zeros((keys.shape[0], 256), F32)
    for g in range(0, got_ref.shape[0] // 4, 2):
        match = jnp.concatenate([(keys == map_ref[g + i : g + i + 1, :]).astype(F32) for i in range(2)], axis=1)
        values = jnp.concatenate([four_peers(got_ref, g + i) for i in range(2)], axis=0)
        total = total + jnp.dot(match.astype(BF16), values, preferred_element_type=F32)
    return total


def products(held_ref, tile_ref, out_ref, adjoint):
    pair = iota((8, 128), 0) // 2
    for j in range(tile_ref.shape[0] // 4):
        rows = held_ref[8 * j : 8 * j + 8, :]
        left = jnp.concatenate([jnp.where(pair == i, rows, 0.0) for i in range(4)], axis=1).astype(BF16)
        blocks = [tile_ref[4 * j + i] for i in range(4)]
        right = jnp.concatenate(blocks, axis=0 if adjoint else 1)
        dims = (((1,), (0 if adjoint else 1,)), ((), ()))
        out_ref[8 * j : 8 * j + 8, :] = lax.dot_general(left, right, dims, preferred_element_type=F32)


def split_rows(ref):
    half = ref.shape[0] // 2
    return jnp.concatenate([ref[pl.ds(r, half, stride=2), :] for r in range(2)], axis=0)


def hold(held_ref, own):
    half = held_ref.shape[0] // 2
    for r in range(2):
        held_ref[pl.ds(r, half, stride=2), :] = own[:, 128 * r : 128 * r + 128].astype(F32)


def send_all(sent_ref, values, extra):
    rows = values.shape[0]
    for peer in range(sent_ref.shape[0]):
        sent_ref[peer, 0:rows, :] = values
        if extra is not None:
            sent_ref[peer, rows:, :] = extra


def begin(rhs_ref, sent_ref, piece_ref, rows):
    for b in range(rows.shape[0] // 2):
        rows[2 * b : 2 * b + 2, :] = rhs_ref[:, 128 * b : 128 * b + 128]
    send_all(sent_ref, rows[...].astype(BF16), None)
    half = rows.shape[0] // 2
    piece_ref[...] = jnp.concatenate([rows[pl.ds(r, half, stride=2), :] for r in range(2)], axis=1).astype(BF16)


def tables(places_ref, counts_ref, slot_v_ref, slot_u_ref, lane_v_ref, lane_u_ref, fetch_ref, spans):
    count = counts_ref[0, 0]
    for axis, slot_ref, lane_ref in ((0, slot_u_ref, lane_u_ref), (1, slot_v_ref, lane_v_ref)):
        slot_ref[...] = slot_keys(places_ref, count, axis)
        lane_ref[...] = lane_keys(places_ref, count, axis)
    span, chips, cores = spans
    for k in range(places_ref.shape[1]):
        block = places_ref[0, k]
        owner = block // span
        fetch_ref[0, k] = ((owner % cores) * chips + owner // cores) * span + block % span
        fetch_ref[1, k] = (k < count).astype(jnp.int32)


def first_adjoint(fetch_ref, lane_ref, u_ref, tile_ref, sent_ref, own_u_ref, held, out):
    for k in range(fetch_ref.shape[1]):
        held[2 * k : 2 * k + 2, :] = u_ref[fetch_ref[0, k]].astype(F32) * fetch_ref[1, k].astype(F32)
    own_u_ref[...] = split_rows(held).astype(BF16)
    products(held, tile_ref, out, True)
    send_all(sent_ref, split_rows(out).astype(BF16), lane_ref[...])


def keep(w, w_ref, piece_ref, held):
    slots = held.shape[0] // 2
    w = w.astype(BF16)
    own = w[0:slots, :]
    piece_ref[...] = w[slots:, :]
    hold(held, own)
    w_ref[...] = jnp.concatenate([own[:, 0:128], own[:, 128:256]], axis=0)


def first_forward(slot_ref, lane_ref, got_ref, tile_ref, sent_ref, w_ref, piece_ref, map_ref, held, out):
    read_keys(got_ref, map_ref)
    keys = with_range(slot_ref, row_index(), piece_ref.shape[0])
    keep(sum_by_key(got_ref, map_ref, keys), w_ref, piece_ref, held)
    products(held, tile_ref, out, False)
    send_all(sent_ref, split_rows(out).astype(BF16), lane_ref[...])


def second_adjoint(slot_ref, lane_ref, got_ref, tile_ref, sent_ref, w_ref, piece_ref, map_ref, held, out):
    read_keys(got_ref, map_ref)
    keys = with_range(slot_ref, col_index(), piece_ref.shape[0])
    keep(sum_by_key(got_ref, map_ref, keys), w_ref, piece_ref, held)
    products(held, tile_ref, out, True)
    send_all(sent_ref, split_rows(out).astype(BF16), lane_ref[...])


def regroup(map_ref, got_ref, sent_ref, line_ref):
    read_keys(got_ref, line_ref)
    target = map_ref[pl.ds(lax.axis_index("z"), 1), :]
    column = jnp.transpose(jnp.broadcast_to(target, (128, 128)))
    total = sum_by_key(got_ref, line_ref, column).astype(BF16)
    for peer in range(sent_ref.shape[0]):
        for r in range(2):
            sent_ref[peer, 32 * r : 32 * r + 32, :] = total[32 * peer : 32 * peer + 32, 128 * r : 128 * r + 128]


def leaders(map_ref, slot_ref, me):
    keys = slot_ref[...]
    quarter = iota(keys.shape, 1) // 32
    earlier = jnp.zeros(keys.shape, F32)
    for g in range(map_ref.shape[0]):
        earlier = earlier + ((keys == map_ref[g : g + 1, :]) & (4 * g + quarter < me)).astype(F32)
    count = jnp.sum(earlier, axis=1, keepdims=True)
    return ((count == 0.0) & (keys >= 0.0)).astype(F32)


def sum_halves(first, second):
    folds = []
    for values in (first, second):
        fold = jnp.sum(values.reshape(values.shape[0] // 8, 8, 128), axis=0)
        folds.append(fold + pltpu.roll(fold, 4, 0))
    return jnp.sum(jnp.where(iota((8, 128), 0) < 4, folds[0], folds[1]), axis=1, keepdims=True)


def sum_piece(values):
    return sum_halves(values[:, 0:128], values[:, 128:256])


def sum_slots(values):
    half = values.shape[0] // 2
    return sum_halves(values[0:half, :], values[half:, :])


def three_parts(values):
    values = jnp.where(iota(values.shape, 1) < 16, values, 0.0)
    high = values.astype(BF16).astype(F32)
    middle = (values - high).astype(BF16).astype(F32)
    low = (values - high - middle).astype(BF16).astype(F32)
    return high + pltpu.roll(middle, 16, 1) + pltpu.roll(low, 32, 1)


def whole_sums(parts):
    return parts + pltpu.roll(parts, 112, 1) + pltpu.roll(parts, 96, 1)


def second_forward(
    slot_ref, map_ref, got_ref, tile_ref, own_w1_ref, w2_ref, u0_ref, own_w2_ref, own_u_ref,
    sent_ref, lead_w3_ref, lead_ref, held, out,
):
    w3 = got_ref[0].astype(F32)
    for peer in range(1, got_ref.shape[0]):
        w3 = w3 + got_ref[peer].astype(F32)
    w3 = w3.astype(BF16).astype(F32)
    half = w3.shape[0] // 2
    for r in range(2):
        held[pl.ds(r, half, stride=2), :] = w3[half * r : half * r + half, :]
    products(held, tile_ref, out, False)
    sent = split_rows(out).astype(BF16)
    lead = leaders(map_ref, slot_ref, row_index())
    lead_ref[...] = lead
    lead = jnp.concatenate([lead, lead], axis=0)
    lead_w3 = w3 * lead
    lead_w3_ref[...] = lead_w3.astype(BF16)
    w1 = own_w1_ref[...].astype(F32)
    w2 = w2_ref[...].astype(F32)
    u0 = u0_ref[...].astype(F32)
    c4 = sent.astype(F32)
    sums = [
        sum_slots(w1 * w1 * lead),
        sum_slots(w1 * lead_w3),
        sum_slots(w3 * lead_w3),
        sum_piece(u0 * u0),
        sum_piece(u0 * w2),
        sum_piece(w2 * w2),
        sum_slots(c4 * own_w2_ref[...].astype(F32)),
        sum_slots(c4 * own_u_ref[...].astype(F32)),
    ]
    lane = iota((8, 128), 1)
    block = jnp.zeros((8, 128), F32)
    for j, value in enumerate(sums):
        block = jnp.where(lane == j, value, block)
    send_all(sent_ref, sent, three_parts(block).astype(BF16))


def gather_sums(got_ref, map_ref, lane_ref, slot_ref, lead_w3_ref, lead_ref, sent_ref, wide, span):
    peers = got_ref.shape[0]
    rows = got_ref.shape[1] - 8
    partial = got_ref[0, rows:, :].astype(F32)
    for peer in range(1, peers):
        partial = partial + got_ref[peer, rows:, :].astype(F32)
    groups = peers // 4
    values = jnp.concatenate([four_peers(got_ref, g) for g in range(groups)], axis=0)
    square = jnp.zeros((8, 256), F32)
    for g in range(groups):
        column = jnp.transpose(jnp.broadcast_to(map_ref[g : g + 1, :], (128, 128)))
        match = [jnp.where(column == map_ref[h : h + 1, :], 1.0 if h == g else 2.0, 0.0) for h in range(g, groups)]
        total = jnp.dot(jnp.concatenate(match, axis=1).astype(BF16), values[128 * g :, :], preferred_element_type=F32)
        square = square + jnp.sum((values[128 * g : 128 * g + 128, :].astype(F32) * total).reshape(16, 8, 256), axis=0)
    lane = iota((8, 128), 1)
    block = jnp.where(lane == 8, sum_piece(square), whole_sums(partial))
    block = block + pltpu.roll(block, 1, 0)
    block = three_parts(block + pltpu.roll(block, 2, 0))
    owners = sent_ref.shape[0] // 4
    slots = slot_ref.shape[0]
    keys = slot_ref[...]
    label = (keys - span * jnp.floor(keys * (1.0 / span)) + 1.0) * lead_ref[...]
    here = iota((slots, 128), 1) == 64 + row_index()
    values = [lead_w3_ref[0:slots, :], lead_w3_ref[slots:, :], jnp.where(here, label, 0.0).astype(BF16)]
    values = jnp.concatenate(values, axis=1)
    values = jnp.concatenate([values, jnp.zeros((128 - slots, 384), BF16)], axis=0)
    match = (iota((owners, 128), 0) == lane_ref[...].astype(jnp.int32)[0:1, :]) & (iota((owners, 128), 1) < slots)
    placed = jnp.dot(match.astype(F32).astype(BF16), values, preferred_element_type=F32)
    wide[pl.ds(0, owners, stride=4), :] = placed[:, 0:128]
    wide[pl.ds(1, owners, stride=4), :] = placed[:, 128:256]
    wide[pl.ds(2, owners, stride=4), :] = placed[:, 256:384] + block[3:4, :]
    wide[pl.ds(3, owners, stride=4), :] = jnp.broadcast_to(block[7:8, :], (owners, 128))
    sent_ref[...] = wide[...].astype(BF16)


def finish(got_ref, w1_ref, solution_ref, phi_ref, wide):
    wide[...] = got_ref[...].astype(F32)
    peers = got_ref.shape[0] // 4
    parts = [wide[pl.ds(i, peers, stride=4), :] for i in range(4)]
    total = jnp.concatenate([jnp.sum(parts[i], axis=0, keepdims=True) for i in (2, 3)], axis=0)
    half = w1_ref.shape[0]
    labels = pltpu.roll(jnp.broadcast_to(total[0:1, :], (half, 128)), 64, 1)
    match = (labels == (iota((half, 128), 0) + 1).astype(F32)) & (iota((half, 128), 1) < peers)
    values = jnp.concatenate(parts[0:2], axis=1)
    values = jnp.concatenate([values, jnp.zeros((128 - peers, 256), F32)], axis=0).astype(BF16)
    w3 = jnp.dot(match.astype(F32).astype(BF16), values, preferred_element_type=F32)
    first = iota((8, 128), 0) < 4
    sums = whole_sums(jnp.where(first, total[0:1, :], total[1:2, :]))

    def pick(j):
        return jnp.broadcast_to(sums[:, j : j + 1], (8, 128))

    t11, t13, t33, s00, s02, s22, s24, s04, s44 = [pick(j) for j in range(9)]

    def norm(square):
        return jnp.sqrt(jnp.maximum(square, 0.0) + EPS)

    beta0 = norm(s00)
    alpha1 = norm(t11 / (beta0 * beta0))
    x2 = 1.0 / (beta0 * alpha1)
    x0 = -alpha1 / beta0
    beta1 = norm(x2 * x2 * s22 + 2.0 * x2 * x0 * s02 + x0 * x0 * s00)
    y3 = x2 / beta1
    y1 = x0 / beta1 - beta1 * x2
    alpha2 = norm(y3 * y3 * t33 + 2.0 * y3 * y1 * t13 + y1 * y1 * t11)
    ratio = alpha2 / beta1
    z4 = y3 / alpha2
    z2 = y1 / alpha2 - ratio * x2
    z0 = -ratio * x0
    beta2 = norm(
        z4 * z4 * s44 + z2 * z2 * s22 + z0 * z0 * s00 + 2.0 * (z4 * z2 * s24 + z4 * z0 * s04 + z2 * z0 * s02)
    )
    rho1 = jnp.sqrt(alpha1 * alpha1 + beta1 * beta1)
    cosine1 = alpha1 / rho1
    sine1 = beta1 / rho1
    phi1 = cosine1 * beta0
    phi_bar1 = sine1 * beta0
    theta = sine1 * alpha2
    rho_bar2 = -cosine1 * alpha2
    rho2 = jnp.sqrt(rho_bar2 * rho_bar2 + beta2 * beta2)
    cosine2 = rho_bar2 / rho2
    sine2 = beta2 / rho2
    phi2 = cosine2 * phi_bar1
    phi_bar2 = sine2 * phi_bar1
    share1 = phi1 / rho1
    share2 = phi2 / rho2
    k1 = share1 * x2 + share2 * (y1 / alpha2 - (theta / rho1) * x2)
    k3 = share2 * y3 / alpha2

    phi_ref[...] = jnp.where(iota((1, 128), 1) == 0, phi_bar2[0:1, :], phi_bar2[4:5, :])[:, 0:2]
    for r in range(2):
        lanes = slice(128 * r, 128 * r + 128)
        scale1, scale3 = k1[4 * r : 4 * r + 1, :], k3[4 * r : 4 * r + 1, :]
        solution_ref[pl.ds(r, half, stride=2), :] = w1_ref[:, lanes].astype(F32) * scale1 + w3[:, lanes] * scale3


def struct(shape, dtype):
    return jax.ShapeDtypeStruct(shape, dtype)


def on_device(tiles, coords, counts, rhs):
    chips = lax.axis_size("y")
    n_row = lax.axis_size("z") * lax.axis_size("x")
    n_col = chips * lax.axis_size("core")
    slots = tiles.shape[2]
    rows = 2 * slots
    span = rhs.shape[1] // 128
    places = coords[0, 0].T

    def call(body, specs, outs, scratch, *operands, out_specs=None):
        return pl.pallas_call(
            body,
            out_shape=outs,
            in_specs=specs,
            out_specs=[VMEM] * len(outs) if out_specs is None else out_specs,
            scratch_shapes=scratch,
            compiler_params=pltpu.CompilerParams(vmem_limit_bytes=32 * 1024 * 1024),
        )(*operands)

    def exchange(sent, axis):
        return lax.all_to_all(sent, axis, split_axis=0, concat_axis=0, tiled=True)

    def exchange_col(sent):
        return lax.all_gather(exchange(sent, "y"), "core", axis=0, tiled=True)

    wide = pltpu.VMEM((rows, 128), F32)
    piece = struct((span, 256), BF16)
    own = struct((rows, 128), BF16)
    slot_table = struct((slots, 128), F32)
    lane_table = struct((8, 128), BF16)
    tile = tiles[0, 0]
    sent, u0 = call(
        begin,
        [VMEM],
        [struct((chips, 2 * span, 128), BF16), piece],
        [pltpu.VMEM((2 * span, 128), F32)],
        rhs,
    )
    slot_v, slot_u, lane_v, lane_u, fetch = call(
        functools.partial(tables, spans=(span, chips, lax.axis_size("core"))),
        [SMEM, SMEM],
        [slot_table, slot_table, lane_table, lane_table, struct((2, slots), jnp.int32)],
        [],
        places, counts,
        out_specs=[VMEM] * 4 + [SMEM],
    )
    u_group = exchange_col(sent).reshape(n_col * span, 2, 128)
    sent, own_u = call(
        first_adjoint,
        [SMEM] + [VMEM] * 3,
        [struct((n_row, rows + 8, 128), BF16), own],
        [wide, wide],
        fetch, lane_v, u_group, tile,
    )
    sent, own_w1, w1, v_map = call(
        first_forward,
        [VMEM] * 4,
        [struct((chips, rows + 8, 128), BF16), own, piece, struct((n_row // 4, 128), F32)],
        [wide, wide],
        slot_v, lane_u, exchange(sent, ROW), tile,
    )
    sent, own_w2, w2, u_map = call(
        second_adjoint,
        [VMEM] * 4,
        [struct((lax.axis_size("z"), rows + 8, 128), BF16), own, piece, struct((n_col // 4, 128), F32)],
        [wide, wide],
        slot_u, lane_v, exchange_col(sent), tile,
    )
    (sent,) = call(
        regroup,
        [VMEM] * 2,
        [struct((lax.axis_size("x"), rows, 128), BF16)],
        [pltpu.VMEM((lax.axis_size("z") // 4, 128), F32)],
        v_map, exchange(sent, "z"),
    )
    sent, lead_w3, lead = call(
        second_forward,
        [VMEM] * 9,
        [struct((chips, rows + 8, 128), BF16), own, slot_table],
        [wide, wide],
        slot_v, v_map, exchange(sent, "x"), tile, own_w1, w2, u0, own_w2, own_u,
    )
    (sent,) = call(
        functools.partial(gather_sums, span=span),
        [VMEM] * 6,
        [struct((n_row * 4, 128), BF16)],
        [pltpu.VMEM((n_row * 4, 128), F32)],
        exchange_col(sent), u_map, lane_v, slot_v, lead_w3, lead,
    )
    result, phi_bar = call(
        finish,
        [VMEM] * 2,
        [struct((2 * span, 128), F32), struct((1, 2), F32)],
        [pltpu.VMEM((n_row * 4, 128), F32)],
        exchange(sent.reshape(n_row, 4, 128), ROW).reshape(n_row * 4, 128), w1,
    )
    result = result.reshape(span, 2, 128).transpose(1, 0, 2).reshape(2, span * 128)
    return (result, phi_bar.reshape(2))


def solution(mesh):
    n_row, n_col = mesh.devices.shape
    fine = Mesh(mesh.devices.reshape(n_row // 4, 4, n_col // 2, 2), ROW + COL)
    return jax.shard_map(
        on_device,
        mesh=fine,
        in_specs=(P(ROW, COL, None, None, None), P(ROW, COL, None, None), P(ROW, COL), P(None, ROW + COL)),
        out_specs=(P(None, COL + ROW), P()),
        check_vma=False,
    )
```

```python
import functools

import jax
import jax.numpy as jnp
from jax import lax
from jax.experimental import pallas as pl
from jax.experimental.pallas import tpu as pltpu
from jax.sharding import Mesh
from jax.sharding import PartitionSpec as P

EPS = 1e-06
F32 = jnp.float32
BF16 = jnp.bfloat16
ROW = ("z", "x")
COL = ("y", "core")
VMEM = pl.BlockSpec(memory_space=pltpu.VMEM)
SMEM = pl.BlockSpec(memory_space=pltpu.SMEM)


def iota(shape, dim):
    return lax.broadcasted_iota(jnp.int32, shape, dim)


def row_index():
    return lax.axis_index("z") * lax.axis_size("x") + lax.axis_index("x")


def col_index():
    return lax.axis_index("y") * lax.axis_size("core") + lax.axis_index("core")


def slot_keys(places_ref, count, axis):
    slots = places_ref.shape[1]
    row = iota((slots, 128), 0)
    keys = jnp.full((slots, 128), -8, jnp.int32)
    for k in range(slots):
        keys = jnp.where(row == k, jnp.where(k < count, places_ref[axis, k], -8), keys)
    return keys.astype(F32)


def with_range(slot_ref, me, span):
    return jnp.concatenate([slot_ref[...], (me * span + iota((span, 128), 0)).astype(F32)], axis=0)


def lane_keys(places_ref, count, axis):
    slots = places_ref.shape[1]
    slot = iota((8, 128), 1) % slots
    keys = jnp.full((8, 128), -1, jnp.int32)
    for k in range(slots):
        keys = jnp.where(slot == k, jnp.where(k < count, places_ref[axis, k], -1), keys)
    keys = keys.astype(F32)
    high = jnp.floor(keys * (1.0 / 64.0))
    sub = iota((8, 128), 0)
    return jnp.where(sub == 0, high, jnp.where(sub == 1, keys - 64.0 * high, 0.0)).astype(BF16)


def read_keys(got_ref, map_ref):
    rows = got_ref.shape[1] - 8
    quarter = iota((8, 128), 1) // 32
    for g in range(got_ref.shape[0] // 4):
        both = got_ref[4 * g, rows:, :].astype(F32)
        for i in range(1, 4):
            both = jnp.where(quarter == i, got_ref[4 * g + i, rows:, :].astype(F32), both)
        map_ref[g : g + 1, :] = both[0:1, :] * 64.0 + both[1:2, :]


def four_peers(got_ref, g):
    halves = []
    for r in range(2):
        halves.append(jnp.concatenate([got_ref[4 * g + i, 32 * r : 32 * r + 32, :] for i in range(4)], axis=0))
    return jnp.concatenate(halves, axis=1)


def sum_by_key(got_ref, map_ref, keys):
    total = jnp.zeros((keys.shape[0], 256), F32)
    for g in range(0, got_ref.shape[0] // 4, 2):
        match = jnp.concatenate([(keys == map_ref[g + i : g + i + 1, :]).astype(F32) for i in range(2)], axis=1)
        values = jnp.concatenate([four_peers(got_ref, g + i) for i in range(2)], axis=0)
        total = total + jnp.dot(match.astype(BF16), values, preferred_element_type=F32)
    return total


def products(held_ref, tile_ref, out_ref, adjoint):
    pair = iota((8, 128), 0) // 2
    for j in range(tile_ref.shape[0] // 4):
        rows = held_ref[8 * j : 8 * j + 8, :]
        left = jnp.concatenate([jnp.where(pair == i, rows, 0.0) for i in range(4)], axis=1).astype(BF16)
        blocks = [tile_ref[4 * j + i] for i in range(4)]
        right = jnp.concatenate(blocks, axis=0 if adjoint else 1)
        dims = (((1,), (0 if adjoint else 1,)), ((), ()))
        out_ref[8 * j : 8 * j + 8, :] = lax.dot_general(left, right, dims, preferred_element_type=F32)


def split_rows(ref):
    half = ref.shape[0] // 2
    return jnp.concatenate([ref[pl.ds(r, half, stride=2), :] for r in range(2)], axis=0)


def hold(held_ref, own):
    half = held_ref.shape[0] // 2
    for r in range(2):
        held_ref[pl.ds(r, half, stride=2), :] = own[:, 128 * r : 128 * r + 128].astype(F32)


def send_all(sent_ref, values, extra):
    rows = values.shape[0]
    for peer in range(sent_ref.shape[0]):
        sent_ref[peer, 0:rows, :] = values
        if extra is not None:
            sent_ref[peer, rows:, :] = extra


def tables(
    places_ref, counts_ref, piece_ref, slot_v_ref, slot_u_ref, lane_v_ref, lane_u_ref, u0_ref, fetch_ref, rows, spans
):
    rows[...] = piece_ref[...].astype(F32)
    half = rows.shape[0] // 2
    u0_ref[...] = jnp.concatenate([rows[pl.ds(r, half, stride=2), :] for r in range(2)], axis=1).astype(BF16)
    count = counts_ref[0, 0]
    for axis, slot_ref, lane_ref in ((0, slot_u_ref, lane_u_ref), (1, slot_v_ref, lane_v_ref)):
        slot_ref[...] = slot_keys(places_ref, count, axis)
        lane_ref[...] = lane_keys(places_ref, count, axis)
    span, chips, cores = spans
    for k in range(places_ref.shape[1]):
        block = places_ref[0, k]
        owner = block // span
        fetch_ref[0, k] = ((owner % cores) * chips + owner // cores) * span + block % span
        fetch_ref[1, k] = (k < count).astype(jnp.int32)


def first_adjoint(fetch_ref, lane_ref, u_ref, tile_ref, sent_ref, own_u_ref, held, out):
    for k in range(fetch_ref.shape[1]):
        held[2 * k : 2 * k + 2, :] = u_ref[fetch_ref[0, k]].astype(F32) * fetch_ref[1, k].astype(F32)
    own_u_ref[...] = split_rows(held).astype(BF16)
    products(held, tile_ref, out, True)
    send_all(sent_ref, split_rows(out).astype(BF16), lane_ref[...])


def keep(w, w_ref, piece_ref, held):
    slots = held.shape[0] // 2
    w = w.astype(BF16)
    own = w[0:slots, :]
    piece_ref[...] = w[slots:, :]
    hold(held, own)
    w_ref[...] = jnp.concatenate([own[:, 0:128], own[:, 128:256]], axis=0)


def first_forward(slot_ref, lane_ref, got_ref, tile_ref, sent_ref, w_ref, piece_ref, map_ref, held, out):
    read_keys(got_ref, map_ref)
    keys = with_range(slot_ref, row_index(), piece_ref.shape[0])
    keep(sum_by_key(got_ref, map_ref, keys), w_ref, piece_ref, held)
    products(held, tile_ref, out, False)
    send_all(sent_ref, split_rows(out).astype(BF16), lane_ref[...])


def second_adjoint(slot_ref, lane_ref, got_ref, tile_ref, sent_ref, w_ref, piece_ref, map_ref, held, out):
    read_keys(got_ref, map_ref)
    keys = with_range(slot_ref, col_index(), piece_ref.shape[0])
    keep(sum_by_key(got_ref, map_ref, keys), w_ref, piece_ref, held)
    products(held, tile_ref, out, True)
    send_all(sent_ref, split_rows(out).astype(BF16), lane_ref[...])


def regroup(map_ref, got_ref, sent_ref, line_ref):
    read_keys(got_ref, line_ref)
    target = map_ref[pl.ds(lax.axis_index("z"), 1), :]
    column = jnp.transpose(jnp.broadcast_to(target, (128, 128)))
    total = sum_by_key(got_ref, line_ref, column).astype(BF16)
    for peer in range(sent_ref.shape[0]):
        for r in range(2):
            sent_ref[peer, 32 * r : 32 * r + 32, :] = total[32 * peer : 32 * peer + 32, 128 * r : 128 * r + 128]


def leaders(map_ref, slot_ref, me):
    keys = slot_ref[...]
    quarter = iota(keys.shape, 1) // 32
    earlier = jnp.zeros(keys.shape, F32)
    for g in range(map_ref.shape[0]):
        earlier = earlier + ((keys == map_ref[g : g + 1, :]) & (4 * g + quarter < me)).astype(F32)
    count = jnp.sum(earlier, axis=1, keepdims=True)
    return ((count == 0.0) & (keys >= 0.0)).astype(F32)


def sum_halves(first, second):
    folds = []
    for values in (first, second):
        fold = jnp.sum(values.reshape(values.shape[0] // 8, 8, 128), axis=0)
        folds.append(fold + pltpu.roll(fold, 4, 0))
    return jnp.sum(jnp.where(iota((8, 128), 0) < 4, folds[0], folds[1]), axis=1, keepdims=True)


def sum_piece(values):
    return sum_halves(values[:, 0:128], values[:, 128:256])


def sum_slots(values):
    half = values.shape[0] // 2
    return sum_halves(values[0:half, :], values[half:, :])


def three_parts(values):
    values = jnp.where(iota(values.shape, 1) < 16, values, 0.0)
    high = values.astype(BF16).astype(F32)
    middle = (values - high).astype(BF16).astype(F32)
    low = (values - high - middle).astype(BF16).astype(F32)
    return high + pltpu.roll(middle, 16, 1) + pltpu.roll(low, 32, 1)


def whole_sums(parts):
    return parts + pltpu.roll(parts, 112, 1) + pltpu.roll(parts, 96, 1)


def second_forward(
    slot_ref, map_ref, got_ref, tile_ref, own_w1_ref, w2_ref, u0_ref, own_w2_ref, own_u_ref,
    sent_ref, lead_w3_ref, lead_ref, held, out,
):
    w3 = got_ref[0].astype(F32)
    for peer in range(1, got_ref.shape[0]):
        w3 = w3 + got_ref[peer].astype(F32)
    w3 = w3.astype(BF16).astype(F32)
    half = w3.shape[0] // 2
    for r in range(2):
        held[pl.ds(r, half, stride=2), :] = w3[half * r : half * r + half, :]
    products(held, tile_ref, out, False)
    sent = split_rows(out).astype(BF16)
    lead = leaders(map_ref, slot_ref, row_index())
    lead_ref[...] = lead
    lead = jnp.concatenate([lead, lead], axis=0)
    lead_w3 = w3 * lead
    lead_w3_ref[...] = lead_w3.astype(BF16)
    w1 = own_w1_ref[...].astype(F32)
    w2 = w2_ref[...].astype(F32)
    u0 = u0_ref[...].astype(F32)
    c4 = sent.astype(F32)
    sums = [
        sum_slots(w1 * w1 * lead),
        sum_slots(w1 * lead_w3),
        sum_slots(w3 * lead_w3),
        sum_piece(u0 * u0),
        sum_piece(u0 * w2),
        sum_piece(w2 * w2),
        sum_slots(c4 * own_w2_ref[...].astype(F32)),
        sum_slots(c4 * own_u_ref[...].astype(F32)),
    ]
    lane = iota((8, 128), 1)
    block = jnp.zeros((8, 128), F32)
    for j, value in enumerate(sums):
        block = jnp.where(lane == j, value, block)
    send_all(sent_ref, sent, three_parts(block).astype(BF16))


def gather_sums(got_ref, map_ref, lane_ref, slot_ref, lead_w3_ref, lead_ref, sent_ref, wide, span):
    peers = got_ref.shape[0]
    rows = got_ref.shape[1] - 8
    partial = got_ref[0, rows:, :].astype(F32)
    for peer in range(1, peers):
        partial = partial + got_ref[peer, rows:, :].astype(F32)
    groups = peers // 4
    values = jnp.concatenate([four_peers(got_ref, g) for g in range(groups)], axis=0)
    square = jnp.zeros((8, 256), F32)
    for g in range(groups):
        column = jnp.transpose(jnp.broadcast_to(map_ref[g : g + 1, :], (128, 128)))
        match = [jnp.where(column == map_ref[h : h + 1, :], 1.0 if h == g else 2.0, 0.0) for h in range(g, groups)]
        total = jnp.dot(jnp.concatenate(match, axis=1).astype(BF16), values[128 * g :, :], preferred_element_type=F32)
        square = square + jnp.sum((values[128 * g : 128 * g + 128, :].astype(F32) * total).reshape(16, 8, 256), axis=0)
    lane = iota((8, 128), 1)
    block = jnp.where(lane == 8, sum_piece(square), whole_sums(partial))
    block = block + pltpu.roll(block, 1, 0)
    block = three_parts(block + pltpu.roll(block, 2, 0))
    owners = sent_ref.shape[0] // 4
    slots = slot_ref.shape[0]
    keys = slot_ref[...]
    label = (keys - span * jnp.floor(keys * (1.0 / span)) + 1.0) * lead_ref[...]
    here = iota((slots, 128), 1) == 64 + row_index()
    values = [lead_w3_ref[0:slots, :], lead_w3_ref[slots:, :], jnp.where(here, label, 0.0).astype(BF16)]
    values = jnp.concatenate(values, axis=1)
    values = jnp.concatenate([values, jnp.zeros((128 - slots, 384), BF16)], axis=0)
    match = (iota((owners, 128), 0) == lane_ref[...].astype(jnp.int32)[0:1, :]) & (iota((owners, 128), 1) < slots)
    placed = jnp.dot(match.astype(F32).astype(BF16), values, preferred_element_type=F32)
    wide[pl.ds(0, owners, stride=4), :] = placed[:, 0:128]
    wide[pl.ds(1, owners, stride=4), :] = placed[:, 128:256]
    wide[pl.ds(2, owners, stride=4), :] = placed[:, 256:384] + block[3:4, :]
    wide[pl.ds(3, owners, stride=4), :] = jnp.broadcast_to(block[7:8, :], (owners, 128))
    sent_ref[...] = wide[...].astype(BF16)


def finish(got_ref, w1_ref, solution_ref, phi_ref, wide):
    wide[...] = got_ref[...].astype(F32)
    peers = got_ref.shape[0] // 4
    parts = [wide[pl.ds(i, peers, stride=4), :] for i in range(4)]
    total = jnp.concatenate([jnp.sum(parts[i], axis=0, keepdims=True) for i in (2, 3)], axis=0)
    half = w1_ref.shape[0]
    labels = pltpu.roll(jnp.broadcast_to(total[0:1, :], (half, 128)), 64, 1)
    match = (labels == (iota((half, 128), 0) + 1).astype(F32)) & (iota((half, 128), 1) < peers)
    values = jnp.concatenate(parts[0:2], axis=1)
    values = jnp.concatenate([values, jnp.zeros((128 - peers, 256), F32)], axis=0).astype(BF16)
    w3 = jnp.dot(match.astype(F32).astype(BF16), values, preferred_element_type=F32)
    first = iota((8, 128), 0) < 4
    sums = whole_sums(jnp.where(first, total[0:1, :], total[1:2, :]))

    def pick(j):
        return jnp.broadcast_to(sums[:, j : j + 1], (8, 128))

    t11, t13, t33, s00, s02, s22, s24, s04, s44 = [pick(j) for j in range(9)]

    def norm(square):
        return jnp.maximum(square, 0.0) + EPS

    b0 = norm(s00)
    ib0 = 1.0 / b0
    a1 = norm(t11 * ib0)
    x22 = ib0 / a1
    x20 = -ib0
    x00 = a1 * ib0
    b1 = norm(x22 * s22 + 2.0 * x20 * s02 + x00 * s00)
    ib1 = 1.0 / b1
    y33 = x22 * ib1
    y31 = x20 * ib1 - x22
    y11 = x00 * ib1 - 2.0 * x20 + b1 * x22
    a2 = norm(y33 * t33 + 2.0 * y31 * t13 + y11 * t11)
    ia2 = 1.0 / a2
    ratio = a2 * ib1
    z44 = y33 * ia2
    z22 = y11 * ia2 - 2.0 * y31 + ratio * x22
    z00 = ratio * x00
    z42 = y31 * ia2 - y33
    z40 = -x20 * ib1
    z20 = x20 + (a2 * x20 - x00) * ib1
    b2 = norm(z44 * s44 + z22 * s22 + z00 * s00 + 2.0 * (z42 * s24 + z40 * s04 + z20 * s02))
    ir1 = 1.0 / (a1 + b1)
    ir2 = 1.0 / (a1 * a2 * ir1 + b2)
    k1 = ir1 + (1.0 + a2 * ir1 * (b1 * ir1)) * ir2
    k3 = -ir1 * ir2
    phi_bar2 = jnp.sqrt(b0 * (b1 * ir1) * (b2 * ir2))

    phi_ref[...] = jnp.where(iota((1, 128), 1) == 0, phi_bar2[0:1, :], phi_bar2[4:5, :])[:, 0:2]
    for r in range(2):
        lanes = slice(128 * r, 128 * r + 128)
        scale1, scale3 = k1[4 * r : 4 * r + 1, :], k3[4 * r : 4 * r + 1, :]
        solution_ref[pl.ds(r, half, stride=2), :] = w1_ref[:, lanes].astype(F32) * scale1 + w3[:, lanes] * scale3


def struct(shape, dtype):
    return jax.ShapeDtypeStruct(shape, dtype)


def on_device(tiles, coords, counts, rhs):
    chips = lax.axis_size("y")
    n_row = lax.axis_size("z") * lax.axis_size("x")
    n_col = chips * lax.axis_size("core")
    slots = tiles.shape[2]
    rows = 2 * slots
    span = rhs.shape[1] // 128
    places = coords[0, 0].T

    def call(body, specs, outs, scratch, *operands, out_specs=None):
        return pl.pallas_call(
            body,
            out_shape=outs,
            in_specs=specs,
            out_specs=[VMEM] * len(outs) if out_specs is None else out_specs,
            scratch_shapes=scratch,
            compiler_params=pltpu.CompilerParams(vmem_limit_bytes=32 * 1024 * 1024),
        )(*operands)

    def exchange(sent, axis):
        return lax.all_to_all(sent, axis, split_axis=0, concat_axis=0, tiled=True)

    def exchange_col(sent):
        return lax.all_gather(exchange(sent, "y"), "core", axis=0, tiled=True)

    wide = pltpu.VMEM((rows, 128), F32)
    piece = struct((span, 256), BF16)
    own = struct((rows, 128), BF16)
    slot_table = struct((slots, 128), F32)
    lane_table = struct((8, 128), BF16)
    tile = tiles[0, 0]
    pairs = rhs.reshape(2, span, 128).transpose(1, 0, 2).reshape(2 * span, 128).astype(BF16)
    slot_v, slot_u, lane_v, lane_u, u0, fetch = call(
        functools.partial(tables, spans=(span, chips, lax.axis_size("core"))),
        [SMEM, SMEM, VMEM],
        [slot_table, slot_table, lane_table, lane_table, piece, struct((2, slots), jnp.int32)],
        [pltpu.VMEM((2 * span, 128), F32)],
        places, counts, pairs,
        out_specs=[VMEM] * 5 + [SMEM],
    )
    sent = jnp.broadcast_to(pairs[None], (chips, 2 * span, 128))
    u_group = exchange_col(sent).reshape(n_col * span, 2, 128)
    sent, own_u = call(
        first_adjoint,
        [SMEM] + [VMEM] * 3,
        [struct((n_row, rows + 8, 128), BF16), own],
        [wide, wide],
        fetch, lane_v, u_group, tile,
    )
    sent, own_w1, w1, v_map = call(
        first_forward,
        [VMEM] * 4,
        [struct((chips, rows + 8, 128), BF16), own, piece, struct((n_row // 4, 128), F32)],
        [wide, wide],
        slot_v, lane_u, exchange(sent, ROW), tile,
    )
    sent, own_w2, w2, u_map = call(
        second_adjoint,
        [VMEM] * 4,
        [struct((lax.axis_size("z"), rows + 8, 128), BF16), own, piece, struct((n_col // 4, 128), F32)],
        [wide, wide],
        slot_u, lane_v, exchange_col(sent), tile,
    )
    (sent,) = call(
        regroup,
        [VMEM] * 2,
        [struct((lax.axis_size("x"), rows, 128), BF16)],
        [pltpu.VMEM((lax.axis_size("z") // 4, 128), F32)],
        v_map, exchange(sent, "z"),
    )
    sent, lead_w3, lead = call(
        second_forward,
        [VMEM] * 9,
        [struct((chips, rows + 8, 128), BF16), own, slot_table],
        [wide, wide],
        slot_v, v_map, exchange(sent, "x"), tile, own_w1, w2, u0, own_w2, own_u,
    )
    (sent,) = call(
        functools.partial(gather_sums, span=span),
        [VMEM] * 6,
        [struct((n_row * 4, 128), BF16)],
        [pltpu.VMEM((n_row * 4, 128), F32)],
        exchange_col(sent), u_map, lane_v, slot_v, lead_w3, lead,
    )
    result, phi_bar = call(
        finish,
        [VMEM] * 2,
        [struct((2 * span, 128), F32), struct((1, 2), F32)],
        [pltpu.VMEM((n_row * 4, 128), F32)],
        exchange(sent.reshape(n_row, 4, 128), ROW).reshape(n_row * 4, 128), w1,
    )
    result = result.reshape(span, 2, 128).transpose(1, 0, 2).reshape(2, span * 128)
    return (result, phi_bar.reshape(2))


def solution(mesh):
    n_row, n_col = mesh.devices.shape
    fine = Mesh(mesh.devices.reshape(n_row // 4, 4, n_col // 2, 2), ROW + COL)
    return jax.shard_map(
        on_device,
        mesh=fine,
        in_specs=(P(ROW, COL, None, None, None), P(ROW, COL, None, None), P(ROW, COL), P(None, ROW + COL)),
        out_specs=(P(None, COL + ROW), P()),
        check_vma=False,
    )
```

```python
import functools

import jax
import jax.numpy as jnp
from jax import lax
from jax.experimental import pallas as pl
from jax.experimental.pallas import tpu as pltpu
from jax.sharding import Mesh
from jax.sharding import PartitionSpec as P

EPS = 1e-06
F32 = jnp.float32
BF16 = jnp.bfloat16
ROW = ("z", "x")
COL = ("y", "core")
VMEM = pl.BlockSpec(memory_space=pltpu.VMEM)
SMEM = pl.BlockSpec(memory_space=pltpu.SMEM)


def iota(shape, dim):
    return lax.broadcasted_iota(jnp.int32, shape, dim)


def row_index():
    return lax.axis_index("z") * lax.axis_size("x") + lax.axis_index("x")


def col_index():
    return lax.axis_index("y") * lax.axis_size("core") + lax.axis_index("core")


def slot_keys(places_ref, count, axis):
    slots = places_ref.shape[1]
    row = iota((slots, 128), 0)
    keys = jnp.full((slots, 128), -8, jnp.int32)
    for k in range(slots):
        keys = jnp.where(row == k, jnp.where(k < count, places_ref[axis, k], -8), keys)
    return keys.astype(F32)


def with_range(slot_ref, me, span):
    return jnp.concatenate([slot_ref[...], (me * span + iota((span, 128), 0)).astype(F32)], axis=0)


def lane_keys(places_ref, count, axis):
    slots = places_ref.shape[1]
    slot = iota((8, 128), 1) % slots
    keys = jnp.full((8, 128), -1, jnp.int32)
    for k in range(slots):
        keys = jnp.where(slot == k, jnp.where(k < count, places_ref[axis, k], -1), keys)
    keys = keys.astype(F32)
    high = jnp.floor(keys * (1.0 / 64.0))
    sub = iota((8, 128), 0)
    return jnp.where(sub == 0, high, jnp.where(sub == 1, keys - 64.0 * high, 0.0)).astype(BF16)


def read_keys(got_ref, map_ref):
    rows = got_ref.shape[1] - 8
    quarter = iota((8, 128), 1) // 32
    for g in range(got_ref.shape[0] // 4):
        both = got_ref[4 * g, rows:, :].astype(F32)
        for i in range(1, 4):
            both = jnp.where(quarter == i, got_ref[4 * g + i, rows:, :].astype(F32), both)
        map_ref[g : g + 1, :] = both[0:1, :] * 64.0 + both[1:2, :]


def four_peers(got_ref, g):
    halves = []
    for r in range(2):
        halves.append(jnp.concatenate([got_ref[4 * g + i, 32 * r : 32 * r + 32, :] for i in range(4)], axis=0))
    return jnp.concatenate(halves, axis=1)


def sum_by_key(got_ref, map_ref, keys):
    total = jnp.zeros((keys.shape[0], 256), F32)
    for g in range(0, got_ref.shape[0] // 4, 2):
        match = jnp.concatenate([(keys == map_ref[g + i : g + i + 1, :]).astype(F32) for i in range(2)], axis=1)
        values = jnp.concatenate([four_peers(got_ref, g + i) for i in range(2)], axis=0)
        total = total + jnp.dot(match.astype(BF16), values, preferred_element_type=F32)
    return total


def products(held_ref, tile_ref, out_ref, adjoint):
    pair = iota((8, 128), 0) // 2
    for j in range(tile_ref.shape[0] // 4):
        rows = held_ref[8 * j : 8 * j + 8, :]
        left = jnp.concatenate([jnp.where(pair == i, rows, 0.0) for i in range(4)], axis=1).astype(BF16)
        blocks = [tile_ref[4 * j + i] for i in range(4)]
        right = jnp.concatenate(blocks, axis=0 if adjoint else 1)
        dims = (((1,), (0 if adjoint else 1,)), ((), ()))
        out_ref[8 * j : 8 * j + 8, :] = lax.dot_general(left, right, dims, preferred_element_type=F32)


def split_rows(ref):
    half = ref.shape[0] // 2
    return jnp.concatenate([ref[pl.ds(r, half, stride=2), :] for r in range(2)], axis=0)


def hold(held_ref, own):
    half = held_ref.shape[0] // 2
    for r in range(2):
        held_ref[pl.ds(r, half, stride=2), :] = own[:, 128 * r : 128 * r + 128].astype(F32)


def send_all(sent_ref, values, extra):
    rows = values.shape[0]
    for peer in range(sent_ref.shape[0]):
        sent_ref[peer, 0:rows, :] = values
        if extra is not None:
            sent_ref[peer, rows:, :] = extra


def begin(rhs_ref, sent_ref, piece_ref, rows):
    for b in range(rows.shape[0] // 2):
        rows[2 * b : 2 * b + 2, :] = rhs_ref[:, 128 * b : 128 * b + 128]
    send_all(sent_ref, rows[...].astype(BF16), None)
    half = rows.shape[0] // 2
    piece_ref[...] = jnp.concatenate([rows[pl.ds(r, half, stride=2), :] for r in range(2)], axis=1).astype(BF16)


def own_lanes(places_ref, counts_ref, lane_ref):
    lane_ref[...] = lane_keys(places_ref, counts_ref[0, 0], 1)


def tables(places_ref, counts_ref, slot_v_ref, slot_u_ref, lane_u_ref, fetch_ref, spans):
    count = counts_ref[0, 0]
    slot_u_ref[...] = slot_keys(places_ref, count, 0)
    slot_v_ref[...] = slot_keys(places_ref, count, 1)
    lane_u_ref[...] = lane_keys(places_ref, count, 0)
    span, chips, cores = spans
    for k in range(places_ref.shape[1]):
        block = places_ref[0, k]
        owner = block // span
        fetch_ref[0, k] = ((owner % cores) * chips + owner // cores) * span + block % span
        fetch_ref[1, k] = (k < count).astype(jnp.int32)


def first_adjoint(fetch_ref, lane_ref, u_ref, tile_ref, sent_ref, own_u_ref, held, out):
    for k in range(fetch_ref.shape[1]):
        held[2 * k : 2 * k + 2, :] = u_ref[fetch_ref[0, k]].astype(F32) * fetch_ref[1, k].astype(F32)
    own_u_ref[...] = split_rows(held).astype(BF16)
    products(held, tile_ref, out, True)
    send_all(sent_ref, split_rows(out).astype(BF16), lane_ref[...])


def keep(w, w_ref, piece_ref, held):
    slots = held.shape[0] // 2
    w = w.astype(BF16)
    own = w[0:slots, :]
    piece_ref[...] = w[slots:, :]
    hold(held, own)
    w_ref[...] = jnp.concatenate([own[:, 0:128], own[:, 128:256]], axis=0)


def peers_sum(got_ref, rows):
    total = got_ref[0, 0:rows, :].astype(F32)
    for peer in range(1, got_ref.shape[0]):
        total = total + got_ref[peer, 0:rows, :].astype(F32)
    return total.astype(BF16)


def hold_rows(held_ref, own):
    half = own.shape[0] // 2
    for r in range(2):
        held_ref[pl.ds(r, half, stride=2), :] = own[half * r : half * r + half, :].astype(F32)


def first_forward(lane_ref, got_ref, tile_ref, sent_ref, w_ref, map_ref, held, out):
    rows = w_ref.shape[0]
    for peer in range(got_ref.shape[0]):
        digits = got_ref[peer, rows:, :].astype(F32)
        for g in range(2):
            map_ref[2 * peer + g : 2 * peer + g + 1, :] = digits[2 * g : 2 * g + 1, :] * 64.0 + digits[2 * g + 1 : 2 * g + 2, :]
    w = peers_sum(got_ref, rows)
    w_ref[...] = w
    hold_rows(held, w)
    products(held, tile_ref, out, False)
    send_all(sent_ref, split_rows(out).astype(BF16), lane_ref[...])


def second_adjoint(slot_ref, lane_ref, got_ref, tile_ref, sent_ref, w_ref, piece_ref, map_ref, held, out):
    read_keys(got_ref, map_ref)
    keys = with_range(slot_ref, col_index(), piece_ref.shape[0])
    keep(sum_by_key(got_ref, map_ref, keys), w_ref, piece_ref, held)
    products(held, tile_ref, out, True)
    send_all(sent_ref, split_rows(out).astype(BF16), lane_ref[...])


def regroup(target, got_ref, sent_ref, line_ref):
    read_keys(got_ref, line_ref)
    column = jnp.transpose(jnp.broadcast_to(target, (128, 128)))
    total = sum_by_key(got_ref, line_ref, column).astype(BF16)
    for peer in range(sent_ref.shape[0]):
        for r in range(2):
            sent_ref[peer, 32 * r : 32 * r + 32, :] = total[32 * peer : 32 * peer + 32, 128 * r : 128 * r + 128]


def first_regroup(lane_ref, near1_ref, near2_ref, near3_ref, got_ref, sent_ref, target_ref, line_ref):
    peers = sent_ref.shape[0]
    me = lax.axis_index("x")
    quarter = iota((8, 128), 1) // 32
    digits = lane_ref[...].astype(F32)
    for shift, near_ref in enumerate((near1_ref, near2_ref, near3_ref), 1):
        digits = jnp.where(quarter == (me + peers - shift) % peers, near_ref[...].astype(F32), digits)
    target = digits[0:1, :] * 64.0 + digits[1:2, :]
    target_ref[...] = jnp.broadcast_to(target, target_ref.shape)
    regroup(target, got_ref, sent_ref, line_ref)
    line = line_ref[...]
    high = jnp.floor(line * (1.0 / 64.0))
    low = line - 64.0 * high
    extra = jnp.concatenate([high[0:1], low[0:1], high[1:2], low[1:2], jnp.zeros((4, 128), F32)], axis=0).astype(BF16)
    for peer in range(peers):
        sent_ref[peer, 64:, :] = extra


def second_regroup(target_ref, got_ref, sent_ref, line_ref):
    regroup(target_ref[0:1, :], got_ref, sent_ref, line_ref)


def leaders(map_ref, slot_ref, me):
    keys = slot_ref[...]
    quarter = iota(keys.shape, 1) // 32
    earlier = jnp.zeros(keys.shape, F32)
    for g in range(map_ref.shape[0]):
        earlier = earlier + ((keys == map_ref[g : g + 1, :]) & (4 * g + quarter < me)).astype(F32)
    count = jnp.sum(earlier, axis=1, keepdims=True)
    return ((count == 0.0) & (keys >= 0.0)).astype(F32)


def sum_halves(first, second):
    folds = []
    for values in (first, second):
        fold = jnp.sum(values.reshape(values.shape[0] // 8, 8, 128), axis=0)
        folds.append(fold + pltpu.roll(fold, 4, 0))
    return jnp.sum(jnp.where(iota((8, 128), 0) < 4, folds[0], folds[1]), axis=1, keepdims=True)


def sum_piece(values):
    return sum_halves(values[:, 0:128], values[:, 128:256])


def sum_slots(values):
    half = values.shape[0] // 2
    return sum_halves(values[0:half, :], values[half:, :])


def three_parts(values):
    values = jnp.where(iota(values.shape, 1) < 16, values, 0.0)
    high = values.astype(BF16).astype(F32)
    middle = (values - high).astype(BF16).astype(F32)
    low = (values - high - middle).astype(BF16).astype(F32)
    return high + pltpu.roll(middle, 16, 1) + pltpu.roll(low, 32, 1)


def whole_sums(parts):
    return parts + pltpu.roll(parts, 112, 1) + pltpu.roll(parts, 96, 1)


def second_forward(
    slot_ref, map_ref, got_ref, tile_ref, own_w1_ref, w2_ref, u0_ref, own_w2_ref, own_u_ref,
    sent_ref, lead_w1_ref, lead_w3_ref, lead_ref, held, out,
):
    w3 = peers_sum(got_ref, own_w1_ref.shape[0])
    hold_rows(held, w3)
    products(held, tile_ref, out, False)
    sent = split_rows(out).astype(BF16)
    lead = leaders(map_ref, slot_ref, lax.axis_index("x") * lax.axis_size("z") + lax.axis_index("z"))
    lead_ref[...] = lead
    lead = jnp.concatenate([lead, lead], axis=0)
    w3 = w3.astype(F32)
    lead_w3 = w3 * lead
    lead_w3_ref[...] = lead_w3.astype(BF16)
    w1 = own_w1_ref[...].astype(F32)
    lead_w1 = w1 * lead
    lead_w1_ref[...] = lead_w1.astype(BF16)
    w2 = w2_ref[...].astype(F32)
    u0 = u0_ref[...].astype(F32)
    c4 = sent.astype(F32)
    sums = [
        sum_slots(w1 * lead_w1),
        sum_slots(w1 * lead_w3),
        sum_slots(w3 * lead_w3),
        sum_piece(u0 * u0),
        sum_piece(u0 * w2),
        sum_piece(w2 * w2),
        sum_slots(c4 * own_w2_ref[...].astype(F32)),
        sum_slots(c4 * own_u_ref[...].astype(F32)),
    ]
    lane = iota((8, 128), 1)
    block = jnp.zeros((8, 128), F32)
    for j, value in enumerate(sums):
        block = jnp.where(lane == j, value, block)
    send_all(sent_ref, sent, three_parts(block).astype(BF16))


def gather_sums(got_ref, map_ref, lane_ref, slot_ref, lead_w1_ref, lead_w3_ref, lead_ref, sent_ref, wide, span):
    peers = got_ref.shape[0]
    rows = got_ref.shape[1] - 8
    partial = got_ref[0, rows:, :].astype(F32)
    for peer in range(1, peers):
        partial = partial + got_ref[peer, rows:, :].astype(F32)
    groups = peers // 4
    values = jnp.concatenate([four_peers(got_ref, g) for g in range(groups)], axis=0)
    square = jnp.zeros((8, 256), F32)
    for g in range(groups):
        column = jnp.transpose(jnp.broadcast_to(map_ref[g : g + 1, :], (128, 128)))
        match = [jnp.where(column == map_ref[h : h + 1, :], 1.0 if h == g else 2.0, 0.0) for h in range(g, groups)]
        total = jnp.dot(jnp.concatenate(match, axis=1).astype(BF16), values[128 * g :, :], preferred_element_type=F32)
        square = square + jnp.sum((values[128 * g : 128 * g + 128, :].astype(F32) * total).reshape(16, 8, 256), axis=0)
    lane = iota((8, 128), 1)
    block = jnp.where(lane == 8, sum_piece(square), whole_sums(partial))
    block = block + pltpu.roll(block, 1, 0)
    block = three_parts(block + pltpu.roll(block, 2, 0))
    owners = sent_ref.shape[0] // 8
    slots = slot_ref.shape[0]
    keys = slot_ref[...]
    label = (keys - span * jnp.floor(keys * (1.0 / span)) + 1.0) * lead_ref[...]
    here = iota((slots, 128), 1) == 64 + row_index()
    values = [ref[slots * r : slots * r + slots, :] for ref in (lead_w1_ref, lead_w3_ref) for r in range(2)]
    values = jnp.concatenate(values + [jnp.where(here, label, 0.0).astype(BF16)], axis=1)
    values = jnp.concatenate([values, jnp.zeros((128 - slots, 640), BF16)], axis=0)
    match = (iota((owners, 128), 0) == lane_ref[...].astype(jnp.int32)[0:1, :]) & (iota((owners, 128), 1) < slots)
    placed = jnp.dot(match.astype(F32).astype(BF16), values, preferred_element_type=F32)
    for i in range(4):
        wide[pl.ds(i, owners, stride=8), :] = placed[:, 128 * i : 128 * i + 128]
    wide[pl.ds(4, owners, stride=8), :] = placed[:, 512:640] + block[3:4, :]
    wide[pl.ds(5, owners, stride=8), :] = jnp.broadcast_to(block[7:8, :], (owners, 128))
    for i in (6, 7):
        wide[pl.ds(i, owners, stride=8), :] = jnp.zeros((owners, 128), F32)
    sent_ref[...] = wide[...].astype(BF16)


def finish(got_ref, solution_ref, phi_ref, wide):
    wide[...] = got_ref[...].astype(F32)
    peers = got_ref.shape[0] // 8
    parts = [wide[pl.ds(i, peers, stride=8), :] for i in range(6)]
    total = jnp.concatenate([jnp.sum(parts[i], axis=0, keepdims=True) for i in (4, 5)], axis=0)
    half = solution_ref.shape[0] // 2
    labels = pltpu.roll(jnp.broadcast_to(total[0:1, :], (half, 128)), 64, 1)
    match = (labels == (iota((half, 128), 0) + 1).astype(F32)) & (iota((half, 128), 1) < peers)
    values = jnp.concatenate(parts[0:4], axis=1)
    values = jnp.concatenate([values, jnp.zeros((128 - peers, 512), F32)], axis=0).astype(BF16)
    placed = jnp.dot(match.astype(F32).astype(BF16), values, preferred_element_type=F32)
    first = iota((8, 128), 0) < 4
    sums = whole_sums(jnp.where(first, total[0:1, :], total[1:2, :]))

    def pick(j):
        return jnp.broadcast_to(sums[:, j : j + 1], (8, 128))

    t11, t13, t33, s00, s02, s22, s24, s04, s44 = [pick(j) for j in range(9)]

    def norm(square):
        return jnp.maximum(square, 0.0) + EPS

    b0 = norm(s00)
    ib0 = 1.0 / b0
    a1 = norm(t11 * ib0)
    x22 = ib0 / a1
    x20 = -ib0
    x00 = a1 * ib0
    b1 = norm(x22 * s22 + 2.0 * x20 * s02 + x00 * s00)
    ib1 = 1.0 / b1
    y33 = x22 * ib1
    y31 = x20 * ib1 - x22
    y11 = x00 * ib1 - 2.0 * x20 + b1 * x22
    a2 = norm(y33 * t33 + 2.0 * y31 * t13 + y11 * t11)
    ia2 = 1.0 / a2
    ratio = a2 * ib1
    z44 = y33 * ia2
    z22 = y11 * ia2 - 2.0 * y31 + ratio * x22
    z00 = ratio * x00
    z42 = y31 * ia2 - y33
    z40 = -x20 * ib1
    z20 = x20 + (a2 * x20 - x00) * ib1
    b2 = norm(z44 * s44 + z22 * s22 + z00 * s00 + 2.0 * (z42 * s24 + z40 * s04 + z20 * s02))
    ir1 = 1.0 / (a1 + b1)
    ir2 = 1.0 / (a1 * a2 * ir1 + b2)
    k1 = ir1 + (1.0 + a2 * ir1 * (b1 * ir1)) * ir2
    k3 = -ir1 * ir2
    phi_bar2 = jnp.sqrt(b0 * (b1 * ir1) * (b2 * ir2))

    phi_ref[...] = jnp.where(iota((1, 128), 1) == 0, phi_bar2[0:1, :], phi_bar2[4:5, :])[:, 0:2]
    for r in range(2):
        scale1, scale3 = k1[4 * r : 4 * r + 1, :], k3[4 * r : 4 * r + 1, :]
        w1 = placed[:, 128 * r : 128 * r + 128]
        w3 = placed[:, 256 + 128 * r : 384 + 128 * r]
        solution_ref[pl.ds(r, half, stride=2), :] = w1 * scale1 + w3 * scale3


def struct(shape, dtype):
    return jax.ShapeDtypeStruct(shape, dtype)


def on_device(tiles, coords, counts, rhs):
    chips = lax.axis_size("y")
    n_row = lax.axis_size("z") * lax.axis_size("x")
    n_col = chips * lax.axis_size("core")
    slots = tiles.shape[2]
    rows = 2 * slots
    span = rhs.shape[1] // 128
    places = coords[0, 0].T

    def call(body, specs, outs, scratch, *operands, out_specs=None):
        return pl.pallas_call(
            body,
            out_shape=outs,
            in_specs=specs,
            out_specs=[VMEM] * len(outs) if out_specs is None else out_specs,
            scratch_shapes=scratch,
            compiler_params=pltpu.CompilerParams(vmem_limit_bytes=32 * 1024 * 1024),
        )(*operands)

    def exchange(sent, axis):
        return lax.all_to_all(sent, axis, split_axis=0, concat_axis=0, tiled=True)

    def exchange_col(sent):
        return lax.all_gather(exchange(sent, "y"), "core", axis=0, tiled=True)

    wide = pltpu.VMEM((rows, 128), F32)
    piece = struct((span, 256), BF16)
    own = struct((rows, 128), BF16)
    slot_table = struct((slots, 128), F32)
    lane_table = struct((8, 128), BF16)
    tile = tiles[0, 0]
    sent, u0 = call(
        begin,
        [VMEM],
        [struct((chips, 2 * span, 128), BF16), piece],
        [pltpu.VMEM((2 * span, 128), F32)],
        rhs,
    )
    (lane_v,) = call(own_lanes, [SMEM, SMEM], [lane_table], [], places, counts)
    n_x, n_z = lax.axis_size("x"), lax.axis_size("z")
    near = [lax.ppermute(lane_v, "x", [(i, (i + shift) % n_x) for i in range(n_x)]) for shift in range(1, n_x)]
    slot_v, slot_u, lane_u, fetch = call(
        functools.partial(tables, spans=(span, chips, lax.axis_size("core"))),
        [SMEM, SMEM],
        [slot_table, slot_table, lane_table, struct((2, slots), jnp.int32)],
        [],
        places, counts,
        out_specs=[VMEM] * 3 + [SMEM],
    )
    u_group = exchange_col(sent).reshape(n_col * span, 2, 128)
    line = [pltpu.VMEM((n_z // 4, 128), F32)]
    sent, own_u = call(
        first_adjoint,
        [SMEM] + [VMEM] * 3,
        [struct((n_z, rows + 8, 128), BF16), own],
        [wide, wide],
        fetch, lane_v, u_group, tile,
    )
    sent, target = call(
        first_regroup,
        [VMEM] * 5,
        [struct((n_x, rows + 8, 128), BF16), struct((8, 128), F32)],
        line,
        lane_v, *near, exchange(sent, "z"),
    )
    sent, own_w1, v_map = call(
        first_forward,
        [VMEM] * 3,
        [struct((chips, rows + 8, 128), BF16), own, struct((n_row // 4, 128), F32)],
        [wide, wide],
        lane_u, exchange(sent, "x"), tile,
    )
    sent, own_w2, w2, u_map = call(
        second_adjoint,
        [VMEM] * 4,
        [struct((n_z, rows + 8, 128), BF16), own, piece, struct((n_col // 4, 128), F32)],
        [wide, wide],
        slot_u, lane_v, exchange_col(sent), tile,
    )
    (sent,) = call(
        second_regroup,
        [VMEM] * 2,
        [struct((n_x, rows, 128), BF16)],
        line,
        target, exchange(sent, "z"),
    )
    sent, lead_w1, lead_w3, lead = call(
        second_forward,
        [VMEM] * 9,
        [struct((chips, rows + 8, 128), BF16), own, own, slot_table],
        [wide, wide],
        slot_v, v_map, exchange(sent, "x"), tile, own_w1, w2, u0, own_w2, own_u,
    )
    (sent,) = call(
        functools.partial(gather_sums, span=span),
        [VMEM] * 7,
        [struct((n_row * 8, 128), BF16)],
        [pltpu.VMEM((n_row * 8, 128), F32)],
        exchange_col(sent), u_map, lane_v, slot_v, lead_w1, lead_w3, lead,
    )
    result, phi_bar = call(
        finish,
        [VMEM],
        [struct((2 * span, 128), F32), struct((1, 2), F32)],
        [pltpu.VMEM((n_row * 8, 128), F32)],
        exchange(sent.reshape(n_row, 8, 128), ROW).reshape(n_row * 8, 128),
    )
    result = result.reshape(span, 2, 128).transpose(1, 0, 2).reshape(2, span * 128)
    return (result, phi_bar.reshape(2))


def solution(mesh):
    n_row, n_col = mesh.devices.shape
    fine = Mesh(mesh.devices.reshape(n_row // 4, 4, n_col // 2, 2), ROW + COL)
    return jax.shard_map(
        on_device,
        mesh=fine,
        in_specs=(P(ROW, COL, None, None, None), P(ROW, COL, None, None), P(ROW, COL), P(None, ROW + COL)),
        out_specs=(P(None, COL + ROW), P()),
        check_vma=False,
    )
```

```python
import functools

import jax
import jax.numpy as jnp
from jax import lax
from jax.experimental import pallas as pl
from jax.experimental.pallas import tpu as pltpu
from jax.sharding import Mesh
from jax.sharding import PartitionSpec as P

EPS = 1e-06
F32 = jnp.float32
BF16 = jnp.bfloat16
ROW = ("z", "x")
COL = ("y", "core")
VMEM = pl.BlockSpec(memory_space=pltpu.VMEM)
SMEM = pl.BlockSpec(memory_space=pltpu.SMEM)
HBM = pl.BlockSpec(memory_space=pltpu.HBM)


def iota(shape, dim):
    return lax.broadcasted_iota(jnp.int32, shape, dim)


def row_index():
    return lax.axis_index("z") * lax.axis_size("x") + lax.axis_index("x")


def col_index():
    return lax.axis_index("y") * lax.axis_size("core") + lax.axis_index("core")


def slot_keys(places_ref, count, axis):
    slots = places_ref.shape[1]
    row = iota((slots, 128), 0)
    keys = jnp.full((slots, 128), -8, jnp.int32)
    for k in range(slots):
        keys = jnp.where(row == k, jnp.where(k < count, places_ref[axis, k], -8), keys)
    return keys.astype(F32)


def range_keys(me, span):
    return (me * span + iota((span, 128), 0)).astype(F32)


def lane_keys(places_ref, count, axis):
    slots = places_ref.shape[1]
    slot = iota((8, 128), 1) % slots
    keys = jnp.full((8, 128), -1, jnp.int32)
    for k in range(slots):
        keys = jnp.where(slot == k, jnp.where(k < count, places_ref[axis, k], -1), keys)
    keys = keys.astype(F32)
    high = jnp.floor(keys * (1.0 / 64.0))
    sub = iota((8, 128), 0)
    return jnp.where(sub == 0, high, jnp.where(sub == 1, keys - 64.0 * high, 0.0)).astype(BF16)


def read_keys(got_ref, map_ref):
    rows = got_ref.shape[1] - 8
    quarter = iota((8, 128), 1) // 32
    for g in range(got_ref.shape[0] // 4):
        both = got_ref[4 * g, rows:, :].astype(F32)
        for i in range(1, 4):
            both = jnp.where(quarter == i, got_ref[4 * g + i, rows:, :].astype(F32), both)
        map_ref[g : g + 1, :] = both[0:1, :] * 64.0 + both[1:2, :]


def four_peers(got_ref, g):
    halves = []
    for r in range(2):
        halves.append(jnp.concatenate([got_ref[4 * g + i, 32 * r : 32 * r + 32, :] for i in range(4)], axis=0))
    return jnp.concatenate(halves, axis=1)


def sum_by_key(got_ref, map_ref, keys):
    total = jnp.zeros((keys.shape[0], 256), F32)
    for g in range(0, got_ref.shape[0] // 4, 2):
        match = jnp.concatenate([(keys == map_ref[g + i : g + i + 1, :]).astype(F32) for i in range(2)], axis=1)
        values = jnp.concatenate([four_peers(got_ref, g + i) for i in range(2)], axis=0)
        total = total + jnp.dot(match.astype(BF16), values, preferred_element_type=F32)
    return total


def products(held_ref, tile_ref, out_ref, adjoint):
    pair = iota((8, 128), 0) // 2
    for j in range(tile_ref.shape[0] // 4):
        rows = held_ref[8 * j : 8 * j + 8, :]
        left = jnp.concatenate([jnp.where(pair == i, rows, 0.0) for i in range(4)], axis=1).astype(BF16)
        blocks = [tile_ref[4 * j + i] for i in range(4)]
        right = jnp.concatenate(blocks, axis=0 if adjoint else 1)
        dims = (((1,), (0 if adjoint else 1,)), ((), ()))
        out_ref[8 * j : 8 * j + 8, :] = lax.dot_general(left, right, dims, preferred_element_type=F32)


def split_rows(ref):
    half = ref.shape[0] // 2
    return jnp.concatenate([ref[pl.ds(r, half, stride=2), :] for r in range(2)], axis=0)


def hold(held_ref, own):
    half = held_ref.shape[0] // 2
    for r in range(2):
        held_ref[pl.ds(r, half, stride=2), :] = own[:, 128 * r : 128 * r + 128].astype(F32)


def send_all(sent_ref, values, extra):
    rows = values.shape[0]
    for peer in range(sent_ref.shape[0]):
        sent_ref[peer, 0:rows, :] = values
        if extra is not None:
            sent_ref[peer, rows:, :] = extra


def begin(rhs_hbm, sent_hbm, piece_ref, rhs_ref, rows, packed, in_sem, out_sems):
    copy = pltpu.make_async_copy(rhs_hbm, rhs_ref, in_sem)
    copy.start()
    copy.wait()
    for b in range(rows.shape[0] // 2):
        rows[2 * b : 2 * b + 2, :] = rhs_ref[:, 128 * b : 128 * b + 128]
    packed[...] = rows[...].astype(BF16)
    copies = [pltpu.make_async_copy(packed, sent_hbm.at[i], out_sems.at[i]) for i in range(sent_hbm.shape[0])]
    for copy in copies:
        copy.start()
    half = rows.shape[0] // 2
    piece_ref[...] = jnp.concatenate([rows[pl.ds(r, half, stride=2), :] for r in range(2)], axis=1).astype(BF16)
    for copy in copies:
        copy.wait()


def tables(places_ref, counts_ref, slot_v_ref, slot_u_ref, lane_v_ref, lane_u_ref, fetch_ref, spans):
    count = counts_ref[0, 0]
    for axis, slot_ref, lane_ref in ((0, slot_u_ref, lane_u_ref), (1, slot_v_ref, lane_v_ref)):
        slot_ref[...] = slot_keys(places_ref, count, axis)
        lane_ref[...] = lane_keys(places_ref, count, axis)
    span, chips, cores = spans
    for k in range(places_ref.shape[1]):
        block = places_ref[0, k]
        owner = block // span
        fetch_ref[0, k] = ((owner % cores) * chips + owner // cores) * span + block % span
        fetch_ref[1, k] = (k < count).astype(jnp.int32)


def first_adjoint(fetch_ref, lane_ref, u_ref, tile_ref, sent_ref, own_u_ref, held, out):
    for k in range(fetch_ref.shape[1]):
        held[2 * k : 2 * k + 2, :] = u_ref[fetch_ref[0, k]].astype(F32) * fetch_ref[1, k].astype(F32)
    own_u_ref[...] = split_rows(held).astype(BF16)
    products(held, tile_ref, out, True)
    send_all(sent_ref, split_rows(out).astype(BF16), lane_ref[...])


def keep(w, w_ref, held):
    w = w.astype(BF16)
    hold(held, w)
    w_ref[...] = jnp.concatenate([w[:, 0:128], w[:, 128:256]], axis=0)


def first_forward(slot_ref, lane_ref, got_ref, tile_ref, sent_ref, w_ref, map_ref, held, out):
    read_keys(got_ref, map_ref)
    keep(sum_by_key(got_ref, map_ref, slot_ref[...]), w_ref, held)
    products(held, tile_ref, out, False)
    send_all(sent_ref, split_rows(out).astype(BF16), lane_ref[...])


def second_adjoint(slot_ref, lane_ref, got_ref, tile_ref, sent_ref, w_ref, map_ref, held, out):
    read_keys(got_ref, map_ref)
    keep(sum_by_key(got_ref, map_ref, slot_ref[...]), w_ref, held)
    products(held, tile_ref, out, True)
    send_all(sent_ref, split_rows(out).astype(BF16), lane_ref[...])


def regroup(map_ref, got_ref, sent_ref, line_ref):
    read_keys(got_ref, line_ref)
    target = map_ref[pl.ds(lax.axis_index("z"), 1), :]
    column = jnp.transpose(jnp.broadcast_to(target, (128, 128)))
    total = sum_by_key(got_ref, line_ref, column).astype(BF16)
    for peer in range(sent_ref.shape[0]):
        for r in range(2):
            sent_ref[peer, 32 * r : 32 * r + 32, :] = total[32 * peer : 32 * peer + 32, 128 * r : 128 * r + 128]


def leaders(map_ref, slot_ref, me):
    keys = slot_ref[...]
    quarter = iota(keys.shape, 1) // 32
    earlier = jnp.zeros(keys.shape, F32)
    for g in range(map_ref.shape[0]):
        earlier = earlier + ((keys == map_ref[g : g + 1, :]) & (4 * g + quarter < me)).astype(F32)
    count = jnp.sum(earlier, axis=1, keepdims=True)
    return ((count == 0.0) & (keys >= 0.0)).astype(F32)


def sum_halves(first, second):
    folds = []
    for values in (first, second):
        fold = jnp.sum(values.reshape(values.shape[0] // 8, 8, 128), axis=0)
        folds.append(fold + pltpu.roll(fold, 4, 0))
    return jnp.sum(jnp.where(iota((8, 128), 0) < 4, folds[0], folds[1]), axis=1, keepdims=True)


def sum_piece(values):
    return sum_halves(values[:, 0:128], values[:, 128:256])


def sum_slots(values):
    half = values.shape[0] // 2
    return sum_halves(values[0:half, :], values[half:, :])


def three_parts(values):
    values = jnp.where(iota(values.shape, 1) < 16, values, 0.0)
    high = values.astype(BF16).astype(F32)
    middle = (values - high).astype(BF16).astype(F32)
    low = (values - high - middle).astype(BF16).astype(F32)
    return high + pltpu.roll(middle, 16, 1) + pltpu.roll(low, 32, 1)


def whole_sums(parts):
    return parts + pltpu.roll(parts, 112, 1) + pltpu.roll(parts, 96, 1)


def lay_out(sums):
    lane = iota((8, 128), 1)
    block = jnp.zeros((8, 128), F32)
    for j, value in sums.items():
        block = jnp.where(lane == j, value, block)
    return block


def aside_v(got_ref, map_ref, slot_ref, piece_ref, lead_ref):
    piece_ref[...] = sum_by_key(got_ref, map_ref, range_keys(row_index(), piece_ref.shape[0])).astype(BF16)
    lead_ref[...] = leaders(map_ref, slot_ref, row_index())


def aside_u(got_ref, map_ref, w1_ref, u0_ref, early_ref, match_ref):
    w2 = sum_by_key(got_ref, map_ref, range_keys(col_index(), u0_ref.shape[0])).astype(BF16).astype(F32)
    w1 = w1_ref[...].astype(F32)
    u0 = u0_ref[...].astype(F32)
    early_ref[...] = lay_out({0: sum_piece(w1 * w1), 3: sum_piece(u0 * u0), 4: sum_piece(u0 * w2), 5: sum_piece(w2 * w2)})
    groups = map_ref.shape[0]
    for g in range(groups):
        column = jnp.transpose(jnp.broadcast_to(map_ref[g : g + 1, :], (128, 128)))
        for h in range(g, groups):
            match = jnp.where(column == map_ref[h : h + 1, :], 1.0 if h == g else 2.0, 0.0)
            match_ref[128 * g : 128 * g + 128, 128 * h : 128 * h + 128] = match.astype(BF16)


def second_forward(
    lead_ref, got_ref, tile_ref, early_ref, own_w1_ref, own_w2_ref, own_u_ref, sent_ref, lead_w3_ref, held, out
):
    w3 = got_ref[0].astype(F32)
    for peer in range(1, got_ref.shape[0]):
        w3 = w3 + got_ref[peer].astype(F32)
    w3 = w3.astype(BF16).astype(F32)
    half = w3.shape[0] // 2
    for r in range(2):
        held[pl.ds(r, half, stride=2), :] = w3[half * r : half * r + half, :]
    products(held, tile_ref, out, False)
    sent = split_rows(out).astype(BF16)
    lead = lead_ref[...]
    lead_w3 = w3 * jnp.concatenate([lead, lead], axis=0)
    lead_w3_ref[...] = lead_w3.astype(BF16)
    c4 = sent.astype(F32)
    sums = {
        1: sum_slots(own_w1_ref[...].astype(F32) * lead_w3),
        2: sum_slots(w3 * lead_w3),
        6: sum_slots(c4 * own_w2_ref[...].astype(F32)),
        7: sum_slots(c4 * own_u_ref[...].astype(F32)),
    }
    send_all(sent_ref, sent, three_parts(early_ref[...] + lay_out(sums)).astype(BF16))


def aside_w3(lane_ref, slot_ref, lead_ref, lead_w3_ref, placed_ref, span):
    owners = placed_ref.shape[0] // 4
    slots = slot_ref.shape[0]
    keys = slot_ref[...]
    label = (keys - span * jnp.floor(keys * (1.0 / span)) + 1.0) * lead_ref[...]
    here = iota((slots, 128), 1) == 64 + row_index()
    values = [lead_w3_ref[0:slots, :], lead_w3_ref[slots:, :], jnp.where(here, label, 0.0).astype(BF16)]
    values = jnp.concatenate(values, axis=1)
    values = jnp.concatenate([values, jnp.zeros((128 - slots, 384), BF16)], axis=0)
    match = (iota((owners, 128), 0) == lane_ref[...].astype(jnp.int32)[0:1, :]) & (iota((owners, 128), 1) < slots)
    placed = jnp.dot(match.astype(F32).astype(BF16), values, preferred_element_type=F32)
    for i in range(3):
        placed_ref[pl.ds(i, owners, stride=4), :] = placed[:, 128 * i : 128 * i + 128]
    placed_ref[pl.ds(3, owners, stride=4), :] = jnp.zeros((owners, 128), F32)


def gather_sums(got_ref, match_ref, placed_ref, sent_ref):
    peers = got_ref.shape[0]
    rows = got_ref.shape[1] - 8
    partial = got_ref[0, rows:, :].astype(F32)
    for peer in range(1, peers):
        partial = partial + got_ref[peer, rows:, :].astype(F32)
    groups = peers // 4
    values = jnp.concatenate([four_peers(got_ref, g) for g in range(groups)], axis=0)
    square = jnp.zeros((8, 256), F32)
    for g in range(groups):
        here = slice(128 * g, 128 * g + 128)
        total = jnp.dot(match_ref[here, 128 * g :], values[128 * g :, :], preferred_element_type=F32)
        square = square + jnp.sum((values[here, :].astype(F32) * total).reshape(16, 8, 256), axis=0)
    block = jnp.where(iota((8, 128), 1) == 8, sum_piece(square), whole_sums(partial))
    block = block + pltpu.roll(block, 1, 0)
    block = three_parts(block + pltpu.roll(block, 2, 0))
    place = iota((8, 128), 0) % 4
    block = jnp.where(place == 2, block[3:4, :], jnp.where(place == 3, block[7:8, :], 0.0))
    placed = placed_ref[...].reshape(placed_ref.shape[0] // 8, 8, 128) + block[None]
    sent_ref[...] = placed.reshape(placed_ref.shape).astype(BF16)


def finish(got_ref, w1_ref, solution_ref, phi_ref, wide):
    wide[...] = got_ref[...].astype(F32)
    peers = got_ref.shape[0] // 4
    parts = [wide[pl.ds(i, peers, stride=4), :] for i in range(4)]
    total = jnp.concatenate([jnp.sum(parts[i], axis=0, keepdims=True) for i in (2, 3)], axis=0)
    half = w1_ref.shape[0]
    labels = pltpu.roll(jnp.broadcast_to(total[0:1, :], (half, 128)), 64, 1)
    match = (labels == (iota((half, 128), 0) + 1).astype(F32)) & (iota((half, 128), 1) < peers)
    values = jnp.concatenate(parts[0:2], axis=1)
    values = jnp.concatenate([values, jnp.zeros((128 - peers, 256), F32)], axis=0).astype(BF16)
    w3 = jnp.dot(match.astype(F32).astype(BF16), values, preferred_element_type=F32)
    first = iota((8, 128), 0) < 4
    sums = whole_sums(jnp.where(first, total[0:1, :], total[1:2, :]))

    def pick(j):
        return jnp.broadcast_to(sums[:, j : j + 1], (8, 128))

    t11, t13, t33, s00, s02, s22, s24, s04, s44 = [pick(j) for j in range(9)]

    def norm(square):
        return jnp.maximum(square, 0.0) + EPS

    b0 = norm(s00)
    ib0 = 1.0 / b0
    a1 = norm(t11 * ib0)
    x22 = ib0 / a1
    x20 = -ib0
    x00 = a1 * ib0
    b1 = norm(x22 * s22 + 2.0 * x20 * s02 + x00 * s00)
    ib1 = 1.0 / b1
    y33 = x22 * ib1
    y31 = x20 * ib1 - x22
    y11 = x00 * ib1 - 2.0 * x20 + b1 * x22
    a2 = norm(y33 * t33 + 2.0 * y31 * t13 + y11 * t11)
    ia2 = 1.0 / a2
    ratio = a2 * ib1
    z44 = y33 * ia2
    z22 = y11 * ia2 - 2.0 * y31 + ratio * x22
    z00 = ratio * x00
    z42 = y31 * ia2 - y33
    z40 = -x20 * ib1
    z20 = x20 + (a2 * x20 - x00) * ib1
    b2 = norm(z44 * s44 + z22 * s22 + z00 * s00 + 2.0 * (z42 * s24 + z40 * s04 + z20 * s02))
    ir1 = 1.0 / (a1 + b1)
    ir2 = 1.0 / (a1 * a2 * ir1 + b2)
    k1 = ir1 + (1.0 + a2 * ir1 * (b1 * ir1)) * ir2
    k3 = -ir1 * ir2
    phi_bar2 = jnp.sqrt(b0 * (b1 * ir1) * (b2 * ir2))

    phi_ref[...] = jnp.where(iota((1, 128), 1) == 0, phi_bar2[0:1, :], phi_bar2[4:5, :])[:, 0:2]
    for r in range(2):
        lanes = slice(128 * r, 128 * r + 128)
        scale1, scale3 = k1[4 * r : 4 * r + 1, :], k3[4 * r : 4 * r + 1, :]
        solution_ref[pl.ds(r, half, stride=2), :] = w1_ref[:, lanes].astype(F32) * scale1 + w3[:, lanes] * scale3


def struct(shape, dtype):
    return jax.ShapeDtypeStruct(shape, dtype)


def on_device(tiles, coords, counts, rhs):
    chips = lax.axis_size("y")
    n_row = lax.axis_size("z") * lax.axis_size("x")
    n_col = chips * lax.axis_size("core")
    slots = tiles.shape[2]
    rows = 2 * slots
    span = rhs.shape[1] // 128
    places = coords[0, 0].T

    def call(body, specs, outs, scratch, *operands, out_specs=None):
        return pl.pallas_call(
            body,
            out_shape=outs,
            in_specs=specs,
            out_specs=[VMEM] * len(outs) if out_specs is None else out_specs,
            scratch_shapes=scratch,
            compiler_params=pltpu.CompilerParams(vmem_limit_bytes=32 * 1024 * 1024),
        )(*operands)

    def exchange(sent, axis):
        return lax.all_to_all(sent, axis, split_axis=0, concat_axis=0, tiled=True)

    def exchange_col(sent):
        return lax.all_gather(exchange(sent, "y"), "core", axis=0, tiled=True)

    wide = pltpu.VMEM((rows, 128), F32)
    piece = struct((span, 256), BF16)
    own = struct((rows, 128), BF16)
    slot_table = struct((slots, 128), F32)
    lane_table = struct((8, 128), BF16)
    tile = tiles[0, 0]
    sent, u0 = call(
        begin,
        [HBM],
        [struct((chips, 2 * span, 128), BF16), piece],
        [
            pltpu.VMEM(rhs.shape, F32),
            pltpu.VMEM((2 * span, 128), F32),
            pltpu.VMEM((2 * span, 128), BF16),
            pltpu.SemaphoreType.DMA(()),
            pltpu.SemaphoreType.DMA((chips,)),
        ],
        pltpu.with_memory_space_constraint(rhs, pltpu.HBM),
        out_specs=[HBM, VMEM],
    )
    slot_v, slot_u, lane_v, lane_u, fetch = call(
        functools.partial(tables, spans=(span, chips, lax.axis_size("core"))),
        [SMEM, SMEM],
        [slot_table, slot_table, lane_table, lane_table, struct((2, slots), jnp.int32)],
        [],
        places, counts,
        out_specs=[VMEM] * 4 + [SMEM],
    )
    u_group = exchange_col(sent).reshape(n_col * span, 2, 128)
    sent, own_u = call(
        first_adjoint,
        [SMEM] + [VMEM] * 3,
        [struct((n_row, rows + 8, 128), BF16), own],
        [wide, wide],
        fetch, lane_v, u_group, tile,
    )
    got = exchange(sent, ROW)
    sent, own_w1, v_map = call(
        first_forward,
        [VMEM] * 4,
        [struct((chips, rows + 8, 128), BF16), own, struct((n_row // 4, 128), F32)],
        [wide, wide],
        slot_v, lane_u, got, tile,
    )
    w1, lead = call(aside_v, [VMEM] * 3, [piece, slot_table], [], got, v_map, slot_v)
    got = exchange_col(sent)
    sent, own_w2, u_map = call(
        second_adjoint,
        [VMEM] * 4,
        [struct((lax.axis_size("z"), rows + 8, 128), BF16), own, struct((n_col // 4, 128), F32)],
        [wide, wide],
        slot_u, lane_v, got, tile,
    )
    early, match = call(
        aside_u,
        [VMEM] * 4,
        [struct((8, 128), F32), struct((n_col * slots, n_col * slots), BF16)],
        [],
        got, u_map, w1, u0,
    )
    (sent,) = call(
        regroup,
        [VMEM] * 2,
        [struct((lax.axis_size("x"), rows, 128), BF16)],
        [pltpu.VMEM((lax.axis_size("z") // 4, 128), F32)],
        v_map, exchange(sent, "z"),
    )
    sent, lead_w3 = call(
        second_forward,
        [VMEM] * 7,
        [struct((chips, rows + 8, 128), BF16), own],
        [wide, wide],
        lead, exchange(sent, "x"), tile, early, own_w1, own_w2, own_u,
    )
    (placed,) = call(
        functools.partial(aside_w3, span=span),
        [VMEM] * 4,
        [struct((n_row * 4, 128), F32)],
        [],
        lane_v, slot_v, lead, lead_w3,
    )
    (sent,) = call(
        gather_sums,
        [VMEM] * 3,
        [struct((n_row * 4, 128), BF16)],
        [],
        exchange_col(sent), match, placed,
    )
    result, phi_bar = call(
        finish,
        [VMEM] * 2,
        [struct((2 * span, 128), F32), struct((1, 2), F32)],
        [pltpu.VMEM((n_row * 4, 128), F32)],
        exchange(sent.reshape(n_row, 4, 128), ROW).reshape(n_row * 4, 128), w1,
    )
    result = result.reshape(span, 2, 128).transpose(1, 0, 2).reshape(2, span * 128)
    return (result, phi_bar.reshape(2))


def solution(mesh):
    n_row, n_col = mesh.devices.shape
    fine = Mesh(mesh.devices.reshape(n_row // 4, 4, n_col // 2, 2), ROW + COL)
    return jax.shard_map(
        on_device,
        mesh=fine,
        in_specs=(P(ROW, COL, None, None, None), P(ROW, COL, None, None), P(ROW, COL), P(None, ROW + COL)),
        out_specs=(P(None, COL + ROW), P()),
        check_vma=False,
    )
```

```python
import functools

import jax
import jax.numpy as jnp
from jax import lax
from jax.experimental import pallas as pl
from jax.experimental.pallas import tpu as pltpu
from jax.sharding import Mesh
from jax.sharding import PartitionSpec as P

EPS = 1e-06
F32 = jnp.float32
BF16 = jnp.bfloat16
ROW = ("z", "x")
COL = ("y", "core")
VMEM = pl.BlockSpec(memory_space=pltpu.VMEM)
SMEM = pl.BlockSpec(memory_space=pltpu.SMEM)


def iota(shape, dim):
    return lax.broadcasted_iota(jnp.int32, shape, dim)


def row_index():
    return lax.axis_index("z") * lax.axis_size("x") + lax.axis_index("x")


def col_index():
    return lax.axis_index("y") * lax.axis_size("core") + lax.axis_index("core")


def slot_keys(places_ref, count, axis):
    slots = places_ref.shape[1]
    row = iota((slots, 128), 0)
    keys = jnp.full((slots, 128), -8, jnp.int32)
    for k in range(slots):
        keys = jnp.where(row == k, jnp.where(k < count, places_ref[axis, k], -8), keys)
    return keys.astype(F32)


def with_range(slot_ref, me, span):
    return jnp.concatenate([slot_ref[...], (me * span + iota((span, 128), 0)).astype(F32)], axis=0)


def lane_keys(places_ref, count, axis):
    slots = places_ref.shape[1]
    slot = iota((8, 128), 1) % slots
    keys = jnp.full((8, 128), -1, jnp.int32)
    for k in range(slots):
        keys = jnp.where(slot == k, jnp.where(k < count, places_ref[axis, k], -1), keys)
    keys = keys.astype(F32)
    high = jnp.floor(keys * (1.0 / 64.0))
    sub = iota((8, 128), 0)
    return jnp.where(sub == 0, high, jnp.where(sub == 1, keys - 64.0 * high, 0.0)).astype(BF16)


def read_keys(got_ref, map_ref):
    rows = got_ref.shape[1] - 8
    quarter = iota((8, 128), 1) // 32
    for g in range(got_ref.shape[0] // 4):
        both = got_ref[4 * g, rows:, :].astype(F32)
        for i in range(1, 4):
            both = jnp.where(quarter == i, got_ref[4 * g + i, rows:, :].astype(F32), both)
        map_ref[g : g + 1, :] = both[0:1, :] * 64.0 + both[1:2, :]


def four_peers(got_ref, g):
    halves = []
    for r in range(2):
        halves.append(jnp.concatenate([got_ref[4 * g + i, 32 * r : 32 * r + 32, :] for i in range(4)], axis=0))
    return jnp.concatenate(halves, axis=1)


def sum_by_key(got_ref, map_ref, keys):
    total = jnp.zeros((keys.shape[0], 256), F32)
    for g in range(0, got_ref.shape[0] // 4, 2):
        match = jnp.concatenate([(keys == map_ref[g + i : g + i + 1, :]).astype(F32) for i in range(2)], axis=1)
        values = jnp.concatenate([four_peers(got_ref, g + i) for i in range(2)], axis=0)
        total = total + jnp.dot(match.astype(BF16), values, preferred_element_type=F32)
    return total


def products(held_ref, tile_ref, out_ref):
    pair = iota((8, 128), 0) // 2
    for j in range(tile_ref.shape[0] // 4):
        rows = held_ref[8 * j : 8 * j + 8, :]
        left = jnp.concatenate([jnp.where(pair == i, rows, 0.0) for i in range(4)], axis=1).astype(BF16)
        right = jnp.concatenate([tile_ref[4 * j + i] for i in range(4)], axis=0)
        out_ref[8 * j : 8 * j + 8, :] = jnp.dot(left, right, preferred_element_type=F32)


def split_rows(ref):
    half = ref.shape[0] // 2
    return jnp.concatenate([ref[pl.ds(r, half, stride=2), :] for r in range(2)], axis=0)


def hold(held_ref, own):
    half = held_ref.shape[0] // 2
    for r in range(2):
        held_ref[pl.ds(r, half, stride=2), :] = own[:, 128 * r : 128 * r + 128].astype(F32)


def send_all(sent_ref, values, extra):
    rows = values.shape[0]
    for peer in range(sent_ref.shape[0]):
        sent_ref[peer, 0:rows, :] = values
        if extra is not None:
            sent_ref[peer, rows:, :] = extra


def begin(rhs_ref, sent_ref, piece_ref, rows):
    for b in range(rows.shape[0] // 2):
        rows[2 * b : 2 * b + 2, :] = rhs_ref[:, 128 * b : 128 * b + 128]
    send_all(sent_ref, rows[...].astype(BF16), None)
    half = rows.shape[0] // 2
    piece_ref[...] = jnp.concatenate([rows[pl.ds(r, half, stride=2), :] for r in range(2)], axis=1).astype(BF16)


def tables(
    places_ref, counts_ref, tile_ref, slot_v_ref, slot_u_ref, lane_v_ref, lane_u_ref, turned_ref, fetch_ref, spans
):
    for k in range(tile_ref.shape[0]):
        turned_ref[k] = jnp.transpose(tile_ref[k])
    count = counts_ref[0, 0]
    for axis, slot_ref, lane_ref in ((0, slot_u_ref, lane_u_ref), (1, slot_v_ref, lane_v_ref)):
        slot_ref[...] = slot_keys(places_ref, count, axis)
        lane_ref[...] = lane_keys(places_ref, count, axis)
    span, chips, cores = spans
    for k in range(places_ref.shape[1]):
        block = places_ref[0, k]
        owner = block // span
        fetch_ref[0, k] = ((owner % cores) * chips + owner // cores) * span + block % span
        fetch_ref[1, k] = (k < count).astype(jnp.int32)


def first_adjoint(fetch_ref, lane_ref, u_ref, tile_ref, sent_ref, own_u_ref, held, out):
    for k in range(fetch_ref.shape[1]):
        held[2 * k : 2 * k + 2, :] = u_ref[fetch_ref[0, k]].astype(F32) * fetch_ref[1, k].astype(F32)
    own_u_ref[...] = split_rows(held).astype(BF16)
    products(held, tile_ref, out)
    send_all(sent_ref, split_rows(out).astype(BF16), lane_ref[...])


def keep(w, w_ref, piece_ref, held):
    slots = held.shape[0] // 2
    w = w.astype(BF16)
    own = w[0:slots, :]
    piece_ref[...] = w[slots:, :]
    hold(held, own)
    w_ref[...] = jnp.concatenate([own[:, 0:128], own[:, 128:256]], axis=0)


def first_forward(slot_ref, lane_ref, got_ref, turned_ref, sent_ref, w_ref, piece_ref, map_ref, held, out):
    read_keys(got_ref, map_ref)
    keys = with_range(slot_ref, row_index(), piece_ref.shape[0])
    keep(sum_by_key(got_ref, map_ref, keys), w_ref, piece_ref, held)
    products(held, turned_ref, out)
    send_all(sent_ref, split_rows(out).astype(BF16), lane_ref[...])


def second_adjoint(slot_ref, lane_ref, got_ref, tile_ref, sent_ref, w_ref, piece_ref, map_ref, held, out):
    read_keys(got_ref, map_ref)
    keys = with_range(slot_ref, col_index(), piece_ref.shape[0])
    keep(sum_by_key(got_ref, map_ref, keys), w_ref, piece_ref, held)
    products(held, tile_ref, out)
    send_all(sent_ref, split_rows(out).astype(BF16), lane_ref[...])


def regroup(map_ref, got_ref, sent_ref, line_ref):
    read_keys(got_ref, line_ref)
    target = map_ref[pl.ds(lax.axis_index("z"), 1), :]
    column = jnp.transpose(jnp.broadcast_to(target, (128, 128)))
    total = sum_by_key(got_ref, line_ref, column).astype(BF16)
    for peer in range(sent_ref.shape[0]):
        for r in range(2):
            sent_ref[peer, 32 * r : 32 * r + 32, :] = total[32 * peer : 32 * peer + 32, 128 * r : 128 * r + 128]


def leaders(map_ref, slot_ref, me):
    keys = slot_ref[...]
    quarter = iota(keys.shape, 1) // 32
    earlier = jnp.zeros(keys.shape, F32)
    for g in range(map_ref.shape[0]):
        earlier = earlier + ((keys == map_ref[g : g + 1, :]) & (4 * g + quarter < me)).astype(F32)
    count = jnp.sum(earlier, axis=1, keepdims=True)
    return ((count == 0.0) & (keys >= 0.0)).astype(F32)


def sum_halves(first, second):
    folds = []
    for values in (first, second):
        fold = jnp.sum(values.reshape(values.shape[0] // 8, 8, 128), axis=0)
        folds.append(fold + pltpu.roll(fold, 4, 0))
    return jnp.sum(jnp.where(iota((8, 128), 0) < 4, folds[0], folds[1]), axis=1, keepdims=True)


def sum_piece(values):
    return sum_halves(values[:, 0:128], values[:, 128:256])


def sum_slots(values):
    half = values.shape[0] // 2
    return sum_halves(values[0:half, :], values[half:, :])


def three_parts(values):
    values = jnp.where(iota(values.shape, 1) < 16, values, 0.0)
    high = values.astype(BF16).astype(F32)
    middle = (values - high).astype(BF16).astype(F32)
    low = (values - high - middle).astype(BF16).astype(F32)
    return high + pltpu.roll(middle, 16, 1) + pltpu.roll(low, 32, 1)


def whole_sums(parts):
    return parts + pltpu.roll(parts, 112, 1) + pltpu.roll(parts, 96, 1)


def second_forward(
    slot_ref, map_ref, got_ref, turned_ref, own_w1_ref, w2_ref, u0_ref, own_w2_ref, own_u_ref,
    sent_ref, lead_w3_ref, lead_ref, held, out,
):
    w3 = got_ref[0].astype(F32)
    for peer in range(1, got_ref.shape[0]):
        w3 = w3 + got_ref[peer].astype(F32)
    w3 = w3.astype(BF16).astype(F32)
    half = w3.shape[0] // 2
    for r in range(2):
        held[pl.ds(r, half, stride=2), :] = w3[half * r : half * r + half, :]
    products(held, turned_ref, out)
    sent = split_rows(out).astype(BF16)
    lead = leaders(map_ref, slot_ref, row_index())
    lead_ref[...] = lead
    lead = jnp.concatenate([lead, lead], axis=0)
    lead_w3 = w3 * lead
    lead_w3_ref[...] = lead_w3.astype(BF16)
    w1 = own_w1_ref[...].astype(F32)
    w2 = w2_ref[...].astype(F32)
    u0 = u0_ref[...].astype(F32)
    c4 = sent.astype(F32)
    sums = [
        sum_slots(w1 * w1 * lead),
        sum_slots(w1 * lead_w3),
        sum_slots(w3 * lead_w3),
        sum_piece(u0 * u0),
        sum_piece(u0 * w2),
        sum_piece(w2 * w2),
        sum_slots(c4 * own_w2_ref[...].astype(F32)),
        sum_slots(c4 * own_u_ref[...].astype(F32)),
    ]
    lane = iota((8, 128), 1)
    block = jnp.zeros((8, 128), F32)
    for j, value in enumerate(sums):
        block = jnp.where(lane == j, value, block)
    send_all(sent_ref, sent, three_parts(block).astype(BF16))


def gather_sums(got_ref, map_ref, lane_ref, slot_ref, lead_w3_ref, lead_ref, sent_ref, wide, span):
    peers = got_ref.shape[0]
    rows = got_ref.shape[1] - 8
    partial = got_ref[0, rows:, :].astype(F32)
    for peer in range(1, peers):
        partial = partial + got_ref[peer, rows:, :].astype(F32)
    groups = peers // 4
    values = jnp.concatenate([four_peers(got_ref, g) for g in range(groups)], axis=0)
    square = jnp.zeros((8, 256), F32)
    for g in range(groups):
        column = jnp.transpose(jnp.broadcast_to(map_ref[g : g + 1, :], (128, 128)))
        match = [jnp.where(column == map_ref[h : h + 1, :], 1.0 if h == g else 2.0, 0.0) for h in range(g, groups)]
        total = jnp.dot(jnp.concatenate(match, axis=1).astype(BF16), values[128 * g :, :], preferred_element_type=F32)
        square = square + jnp.sum((values[128 * g : 128 * g + 128, :].astype(F32) * total).reshape(16, 8, 256), axis=0)
    lane = iota((8, 128), 1)
    block = jnp.where(lane == 8, sum_piece(square), whole_sums(partial))
    block = block + pltpu.roll(block, 1, 0)
    block = three_parts(block + pltpu.roll(block, 2, 0))
    owners = sent_ref.shape[0] // 4
    slots = slot_ref.shape[0]
    keys = slot_ref[...]
    label = (keys - span * jnp.floor(keys * (1.0 / span)) + 1.0) * lead_ref[...]
    here = iota((slots, 128), 1) == 64 + row_index()
    values = [lead_w3_ref[0:slots, :], lead_w3_ref[slots:, :], jnp.where(here, label, 0.0).astype(BF16)]
    values = jnp.concatenate(values, axis=1)
    values = jnp.concatenate([values, jnp.zeros((128 - slots, 384), BF16)], axis=0)
    match = (iota((owners, 128), 0) == lane_ref[...].astype(jnp.int32)[0:1, :]) & (iota((owners, 128), 1) < slots)
    placed = jnp.dot(match.astype(F32).astype(BF16), values, preferred_element_type=F32)
    wide[pl.ds(0, owners, stride=4), :] = placed[:, 0:128]
    wide[pl.ds(1, owners, stride=4), :] = placed[:, 128:256]
    wide[pl.ds(2, owners, stride=4), :] = placed[:, 256:384] + block[3:4, :]
    wide[pl.ds(3, owners, stride=4), :] = jnp.broadcast_to(block[7:8, :], (owners, 128))
    sent_ref[...] = wide[...].astype(BF16)


def finish(got_ref, w1_ref, solution_ref, phi_ref, wide):
    wide[...] = got_ref[...].astype(F32)
    peers = got_ref.shape[0] // 4
    parts = [wide[pl.ds(i, peers, stride=4), :] for i in range(4)]
    total = jnp.concatenate([jnp.sum(parts[i], axis=0, keepdims=True) for i in (2, 3)], axis=0)
    half = w1_ref.shape[0]
    labels = pltpu.roll(jnp.broadcast_to(total[0:1, :], (half, 128)), 64, 1)
    match = (labels == (iota((half, 128), 0) + 1).astype(F32)) & (iota((half, 128), 1) < peers)
    values = jnp.concatenate(parts[0:2], axis=1)
    values = jnp.concatenate([values, jnp.zeros((128 - peers, 256), F32)], axis=0).astype(BF16)
    w3 = jnp.dot(match.astype(F32).astype(BF16), values, preferred_element_type=F32)
    first = iota((8, 128), 0) < 4
    sums = whole_sums(jnp.where(first, total[0:1, :], total[1:2, :]))

    def pick(j):
        return jnp.broadcast_to(sums[:, j : j + 1], (8, 128))

    t11, t13, t33, s00, s02, s22, s24, s04, s44 = [pick(j) for j in range(9)]

    def norm(square):
        return jnp.maximum(square, 0.0) + EPS

    b0 = norm(s00)
    ib0 = 1.0 / b0
    a1 = norm(t11 * ib0)
    x22 = ib0 / a1
    x20 = -ib0
    x00 = a1 * ib0
    b1 = norm(x22 * s22 + 2.0 * x20 * s02 + x00 * s00)
    ib1 = 1.0 / b1
    y33 = x22 * ib1
    y31 = x20 * ib1 - x22
    y11 = x00 * ib1 - 2.0 * x20 + b1 * x22
    a2 = norm(y33 * t33 + 2.0 * y31 * t13 + y11 * t11)
    ia2 = 1.0 / a2
    ratio = a2 * ib1
    z44 = y33 * ia2
    z22 = y11 * ia2 - 2.0 * y31 + ratio * x22
    z00 = ratio * x00
    z42 = y31 * ia2 - y33
    z40 = -x20 * ib1
    z20 = x20 + (a2 * x20 - x00) * ib1
    b2 = norm(z44 * s44 + z22 * s22 + z00 * s00 + 2.0 * (z42 * s24 + z40 * s04 + z20 * s02))
    ir1 = 1.0 / (a1 + b1)
    ir2 = 1.0 / (a1 * a2 * ir1 + b2)
    k1 = ir1 + (1.0 + a2 * ir1 * (b1 * ir1)) * ir2
    k3 = -ir1 * ir2
    phi_bar2 = jnp.sqrt(b0 * (b1 * ir1) * (b2 * ir2))

    phi_ref[...] = jnp.where(iota((1, 128), 1) == 0, phi_bar2[0:1, :], phi_bar2[4:5, :])[:, 0:2]
    for r in range(2):
        lanes = slice(128 * r, 128 * r + 128)
        scale1, scale3 = k1[4 * r : 4 * r + 1, :], k3[4 * r : 4 * r + 1, :]
        solution_ref[pl.ds(r, half, stride=2), :] = w1_ref[:, lanes].astype(F32) * scale1 + w3[:, lanes] * scale3


def struct(shape, dtype):
    return jax.ShapeDtypeStruct(shape, dtype)


def on_device(tiles, coords, counts, rhs):
    chips = lax.axis_size("y")
    n_row = lax.axis_size("z") * lax.axis_size("x")
    n_col = chips * lax.axis_size("core")
    slots = tiles.shape[2]
    rows = 2 * slots
    span = rhs.shape[1] // 128
    places = coords[0, 0].T

    def call(body, specs, outs, scratch, *operands, out_specs=None):
        return pl.pallas_call(
            body,
            out_shape=outs,
            in_specs=specs,
            out_specs=[VMEM] * len(outs) if out_specs is None else out_specs,
            scratch_shapes=scratch,
            compiler_params=pltpu.CompilerParams(vmem_limit_bytes=32 * 1024 * 1024),
        )(*operands)

    def exchange(sent, axis):
        return lax.all_to_all(sent, axis, split_axis=0, concat_axis=0, tiled=True)

    def exchange_col(sent):
        return lax.all_gather(exchange(sent, "y"), "core", axis=0, tiled=True)

    wide = pltpu.VMEM((rows, 128), F32)
    piece = struct((span, 256), BF16)
    own = struct((rows, 128), BF16)
    slot_table = struct((slots, 128), F32)
    lane_table = struct((8, 128), BF16)
    tile = tiles[0, 0]
    sent, u0 = call(
        begin,
        [VMEM],
        [struct((chips, 2 * span, 128), BF16), piece],
        [pltpu.VMEM((2 * span, 128), F32)],
        rhs,
    )
    slot_v, slot_u, lane_v, lane_u, turned, fetch = call(
        functools.partial(tables, spans=(span, chips, lax.axis_size("core"))),
        [SMEM, SMEM, VMEM],
        [slot_table, slot_table, lane_table, lane_table, struct(tile.shape, BF16), struct((2, slots), jnp.int32)],
        [],
        places, counts, tile,
        out_specs=[VMEM] * 5 + [SMEM],
    )
    u_group = exchange_col(sent).reshape(n_col * span, 2, 128)
    sent, own_u = call(
        first_adjoint,
        [SMEM] + [VMEM] * 3,
        [struct((n_row, rows + 8, 128), BF16), own],
        [wide, wide],
        fetch, lane_v, u_group, tile,
    )
    sent, own_w1, w1, v_map = call(
        first_forward,
        [VMEM] * 4,
        [struct((chips, rows + 8, 128), BF16), own, piece, struct((n_row // 4, 128), F32)],
        [wide, wide],
        slot_v, lane_u, exchange(sent, ROW), turned,
    )
    sent, own_w2, w2, u_map = call(
        second_adjoint,
        [VMEM] * 4,
        [struct((lax.axis_size("z"), rows + 8, 128), BF16), own, piece, struct((n_col // 4, 128), F32)],
        [wide, wide],
        slot_u, lane_v, exchange_col(sent), tile,
    )
    (sent,) = call(
        regroup,
        [VMEM] * 2,
        [struct((lax.axis_size("x"), rows, 128), BF16)],
        [pltpu.VMEM((lax.axis_size("z") // 4, 128), F32)],
        v_map, exchange(sent, "z"),
    )
    sent, lead_w3, lead = call(
        second_forward,
        [VMEM] * 9,
        [struct((chips, rows + 8, 128), BF16), own, slot_table],
        [wide, wide],
        slot_v, v_map, exchange(sent, "x"), turned, own_w1, w2, u0, own_w2, own_u,
    )
    (sent,) = call(
        functools.partial(gather_sums, span=span),
        [VMEM] * 6,
        [struct((n_row * 4, 128), BF16)],
        [pltpu.VMEM((n_row * 4, 128), F32)],
        exchange_col(sent), u_map, lane_v, slot_v, lead_w3, lead,
    )
    result, phi_bar = call(
        finish,
        [VMEM] * 2,
        [struct((2 * span, 128), F32), struct((1, 2), F32)],
        [pltpu.VMEM((n_row * 4, 128), F32)],
        exchange(sent.reshape(n_row, 4, 128), ROW).reshape(n_row * 4, 128), w1,
    )
    result = result.reshape(span, 2, 128).transpose(1, 0, 2).reshape(2, span * 128)
    return (result, phi_bar.reshape(2))


def solution(mesh):
    n_row, n_col = mesh.devices.shape
    fine = Mesh(mesh.devices.reshape(n_row // 4, 4, n_col // 2, 2), ROW + COL)
    return jax.shard_map(
        on_device,
        mesh=fine,
        in_specs=(P(ROW, COL, None, None, None), P(ROW, COL, None, None), P(ROW, COL), P(None, ROW + COL)),
        out_specs=(P(None, COL + ROW), P()),
        check_vma=False,
    )
```

```python
import functools

import jax
import jax.numpy as jnp
from jax import lax
from jax.experimental import pallas as pl
from jax.experimental.pallas import tpu as pltpu
from jax.sharding import Mesh
from jax.sharding import PartitionSpec as P

EPS = 1e-06
F32 = jnp.float32
BF16 = jnp.bfloat16
ROW = ("z", "x")
COL = ("y", "core")
VMEM = pl.BlockSpec(memory_space=pltpu.VMEM)
SMEM = pl.BlockSpec(memory_space=pltpu.SMEM)


def iota(shape, dim):
    return lax.broadcasted_iota(jnp.int32, shape, dim)


def row_index():
    return lax.axis_index("z") * lax.axis_size("x") + lax.axis_index("x")


def col_index():
    return lax.axis_index("y") * lax.axis_size("core") + lax.axis_index("core")


def slot_keys(sorted_ref, axis):
    slots = sorted_ref.shape[1]
    row = iota((slots, 128), 0)
    keys = jnp.full((slots, 128), -8, jnp.int32)
    for k in range(slots):
        block = sorted_ref[axis, k]
        keys = jnp.where(row == k, jnp.where(block < 0, -8, block), keys)
    return keys.astype(F32)


def with_range(slot_ref, me, span):
    return jnp.concatenate([slot_ref[...], (me * span + iota((span, 128), 0)).astype(F32)], axis=0)


def lane_keys(sorted_ref, axis):
    slots = sorted_ref.shape[1]
    slot = iota((8, 128), 1) % slots
    keys = jnp.full((8, 128), -1, jnp.int32)
    for k in range(slots):
        keys = jnp.where(slot == k, sorted_ref[axis, k], keys)
    keys = keys.astype(F32)
    high = jnp.floor(keys * (1.0 / 64.0))
    sub = iota((8, 128), 0)
    return jnp.where(sub == 0, high, jnp.where(sub == 1, keys - 64.0 * high, 0.0)).astype(BF16)


def read_keys(got_ref, map_ref):
    rows = got_ref.shape[1] - 8
    quarter = iota((8, 128), 1) // 32
    for g in range(got_ref.shape[0] // 4):
        both = got_ref[4 * g, rows:, :].astype(F32)
        for i in range(1, 4):
            both = jnp.where(quarter == i, got_ref[4 * g + i, rows:, :].astype(F32), both)
        map_ref[g : g + 1, :] = both[0:1, :] * 64.0 + both[1:2, :]


def four_peers(got_ref, g):
    halves = []
    for r in range(2):
        halves.append(jnp.concatenate([got_ref[4 * g + i, 32 * r : 32 * r + 32, :] for i in range(4)], axis=0))
    return jnp.concatenate(halves, axis=1)


def sum_by_key(got_ref, map_ref, keys):
    total = jnp.zeros((keys.shape[0], 256), F32)
    for g in range(0, got_ref.shape[0] // 4, 2):
        match = jnp.concatenate([(keys == map_ref[g + i : g + i + 1, :]).astype(F32) for i in range(2)], axis=1)
        values = jnp.concatenate([four_peers(got_ref, g + i) for i in range(2)], axis=0)
        total = total + jnp.dot(match.astype(BF16), values, preferred_element_type=F32)
    return total


def products(held_ref, tile_ref, out_ref):
    pair = iota((8, 128), 0) // 2
    for j in range(tile_ref.shape[0] // 4):
        rows = held_ref[8 * j : 8 * j + 8, :]
        left = jnp.concatenate([jnp.where(pair == i, rows, 0.0) for i in range(4)], axis=1).astype(BF16)
        right = jnp.concatenate([tile_ref[4 * j + i] for i in range(4)], axis=0)
        out_ref[8 * j : 8 * j + 8, :] = jnp.dot(left, right, preferred_element_type=F32)


def split_rows(ref):
    half = ref.shape[0] // 2
    return jnp.concatenate([ref[pl.ds(r, half, stride=2), :] for r in range(2)], axis=0)


def hold(held_ref, own):
    half = held_ref.shape[0] // 2
    for r in range(2):
        held_ref[pl.ds(r, half, stride=2), :] = own[:, 128 * r : 128 * r + 128].astype(F32)


def send_all(sent_ref, values, extra):
    rows = values.shape[0]
    for peer in range(sent_ref.shape[0]):
        sent_ref[peer, 0:rows, :] = values
        if extra is not None:
            sent_ref[peer, rows:, :] = extra


def begin(rhs_ref, sent_ref, piece_ref, rows):
    for b in range(rows.shape[0] // 2):
        rows[2 * b : 2 * b + 2, :] = rhs_ref[:, 128 * b : 128 * b + 128]
    send_all(sent_ref, rows[...].astype(BF16), None)
    half = rows.shape[0] // 2
    piece_ref[...] = jnp.concatenate([rows[pl.ds(r, half, stride=2), :] for r in range(2)], axis=1).astype(BF16)


def tables(
    places_ref, counts_ref, tile_ref,
    slot_v_ref, slot_u_ref, lane_v_ref, lane_u_ref, held_ref, turned_ref, fetch_ref, order_ref, sorted_ref, spans,
):
    count = counts_ref[0, 0]
    span, chips, cores = spans
    slots = places_ref.shape[1]
    seen = jnp.int32(0)
    for k in range(slots):
        odd = (places_ref[0, k] // span) % 2
        order_ref[jnp.where(odd == 1, slots // 2 + seen, k - seen)] = k
        seen = seen + odd
    for i in range(slots):
        k = order_ref[i]
        held_ref[i] = tile_ref[k]
        turned_ref[i] = jnp.transpose(tile_ref[k])
        block = places_ref[0, k]
        owner = block // span
        used = k < count
        sorted_ref[0, i] = jnp.where(used, block, -1)
        sorted_ref[1, i] = jnp.where(used, places_ref[1, k], -1)
        fetch_ref[0, i] = ((owner % cores) * chips + owner // cores) * span + block % span
        fetch_ref[1, i] = used.astype(jnp.int32)
    slot_u_ref[...] = slot_keys(sorted_ref, 0)
    slot_v_ref[...] = slot_keys(sorted_ref, 1)
    lane_u_ref[...] = lane_keys(sorted_ref, 0)
    lane_v_ref[...] = lane_keys(sorted_ref, 1)


def first_adjoint(fetch_ref, lane_ref, u_ref, tile_ref, sent_ref, own_u_ref, held, out):
    for k in range(fetch_ref.shape[1]):
        held[2 * k : 2 * k + 2, :] = u_ref[fetch_ref[0, k]].astype(F32) * fetch_ref[1, k].astype(F32)
    own_u_ref[...] = split_rows(held).astype(BF16)
    products(held, tile_ref, out)
    send_all(sent_ref, split_rows(out).astype(BF16), lane_ref[...])


def keep(w, w_ref, piece_ref, held):
    slots = held.shape[0] // 2
    w = w.astype(BF16)
    own = w[0:slots, :]
    piece_ref[...] = w[slots:, :]
    hold(held, own)
    w_ref[...] = jnp.concatenate([own[:, 0:128], own[:, 128:256]], axis=0)


def first_forward(slot_ref, lane_ref, got_ref, turned_ref, sent_ref, w_ref, piece_ref, map_ref, held, out):
    read_keys(got_ref, map_ref)
    keys = with_range(slot_ref, row_index(), piece_ref.shape[0])
    keep(sum_by_key(got_ref, map_ref, keys), w_ref, piece_ref, held)
    products(held, turned_ref, out)
    send_all(sent_ref, split_rows(out).astype(BF16), lane_ref[...])


def second_adjoint(slot_ref, lane_ref, got_ref, tile_ref, sent_ref, w_ref, piece_ref, map_ref, held, out):
    read_keys(got_ref, map_ref)
    keys = with_range(slot_ref, col_index(), piece_ref.shape[0])
    keep(sum_by_key(got_ref, map_ref, keys), w_ref, piece_ref, held)
    products(held, tile_ref, out)
    send_all(sent_ref, split_rows(out).astype(BF16), lane_ref[...])


def regroup(map_ref, got_ref, sent_ref, line_ref):
    read_keys(got_ref, line_ref)
    target = map_ref[pl.ds(lax.axis_index("z"), 1), :]
    column = jnp.transpose(jnp.broadcast_to(target, (128, 128)))
    total = sum_by_key(got_ref, line_ref, column).astype(BF16)
    for peer in range(sent_ref.shape[0]):
        for r in range(2):
            sent_ref[peer, 32 * r : 32 * r + 32, :] = total[32 * peer : 32 * peer + 32, 128 * r : 128 * r + 128]


def leaders(map_ref, slot_ref, me):
    keys = slot_ref[...]
    quarter = iota(keys.shape, 1) // 32
    earlier = jnp.zeros(keys.shape, F32)
    for g in range(map_ref.shape[0]):
        earlier = earlier + ((keys == map_ref[g : g + 1, :]) & (4 * g + quarter < me)).astype(F32)
    count = jnp.sum(earlier, axis=1, keepdims=True)
    return ((count == 0.0) & (keys >= 0.0)).astype(F32)


def sum_halves(first, second):
    folds = []
    for values in (first, second):
        fold = jnp.sum(values.reshape(values.shape[0] // 8, 8, 128), axis=0)
        folds.append(fold + pltpu.roll(fold, 4, 0))
    return jnp.sum(jnp.where(iota((8, 128), 0) < 4, folds[0], folds[1]), axis=1, keepdims=True)


def sum_piece(values):
    return sum_halves(values[:, 0:128], values[:, 128:256])


def sum_slots(values):
    half = values.shape[0] // 2
    return sum_halves(values[0:half, :], values[half:, :])


def three_parts(values):
    values = jnp.where(iota(values.shape, 1) < 16, values, 0.0)
    high = values.astype(BF16).astype(F32)
    middle = (values - high).astype(BF16).astype(F32)
    low = (values - high - middle).astype(BF16).astype(F32)
    return high + pltpu.roll(middle, 16, 1) + pltpu.roll(low, 32, 1)


def whole_sums(parts):
    return parts + pltpu.roll(parts, 112, 1) + pltpu.roll(parts, 96, 1)


def second_forward(
    slot_ref, map_ref, got_ref, turned_ref, own_w1_ref, w2_ref, u0_ref, own_w2_ref, own_u_ref,
    sent_ref, lead_w3_ref, lead_ref, held, out,
):
    w3 = got_ref[0].astype(F32)
    for peer in range(1, got_ref.shape[0]):
        w3 = w3 + got_ref[peer].astype(F32)
    w3 = w3.astype(BF16).astype(F32)
    half = w3.shape[0] // 2
    for r in range(2):
        held[pl.ds(r, half, stride=2), :] = w3[half * r : half * r + half, :]
    products(held, turned_ref, out)
    sent = split_rows(out).astype(BF16)
    lead = leaders(map_ref, slot_ref, row_index())
    lead_ref[...] = lead
    lead = jnp.concatenate([lead, lead], axis=0)
    lead_w3 = w3 * lead
    lead_w3_ref[...] = lead_w3.astype(BF16)
    w1 = own_w1_ref[...].astype(F32)
    w2 = w2_ref[...].astype(F32)
    u0 = u0_ref[...].astype(F32)
    c4 = sent.astype(F32)
    sums = [
        sum_slots(w1 * w1 * lead),
        sum_slots(w1 * lead_w3),
        sum_slots(w3 * lead_w3),
        sum_piece(u0 * u0),
        sum_piece(u0 * w2),
        sum_piece(w2 * w2),
        sum_slots(c4 * own_w2_ref[...].astype(F32)),
        sum_slots(c4 * own_u_ref[...].astype(F32)),
    ]
    lane = iota((8, 128), 1)
    block = jnp.zeros((8, 128), F32)
    for j, value in enumerate(sums):
        block = jnp.where(lane == j, value, block)
    block = three_parts(block).astype(BF16)
    chips = sent_ref.shape[0] // 2
    for core in range(2):
        for r in range(2):
            values = sent[half * r + half // 2 * core : half * r + half // 2 * core + half // 2, :]
            for chip in range(chips):
                sent_ref[core * chips + chip, half // 2 * r : half // 2 * r + half // 2, :] = values
        for chip in range(chips):
            sent_ref[core * chips + chip, half:, :] = block


def half_slots(got_ref, g):
    core = lax.axis_index("core")
    halves = []
    for r in range(2):
        for i in range(4):
            values = got_ref[4 * g + i, 16 * r : 16 * r + 16, :]
            zeros = jnp.zeros_like(values)
            halves += [jnp.where(core == 0, values, zeros), jnp.where(core == 0, zeros, values)]
    return jnp.concatenate([jnp.concatenate(halves[0:8], axis=0), jnp.concatenate(halves[8:16], axis=0)], axis=1)


def gather_sums(got_ref, map_ref, lane_ref, slot_ref, lead_w3_ref, lead_ref, sent_ref, wide, span):
    peers = got_ref.shape[0]
    rows = got_ref.shape[1] - 8
    core = lax.axis_index("core")
    partial = got_ref[0, rows:, :].astype(F32)
    for peer in range(1, peers):
        partial = partial + got_ref[peer, rows:, :].astype(F32)
    partial = jnp.where(core == 0, partial, 0.0)
    groups = peers // 4
    values = jnp.concatenate([half_slots(got_ref, g) for g in range(groups)], axis=0)
    square = jnp.zeros((8, 256), F32)
    for g in range(groups):
        column = jnp.transpose(jnp.broadcast_to(map_ref[g : g + 1, :], (128, 128)))
        match = [jnp.where(column == map_ref[h : h + 1, :], 1.0 if h == g else 2.0, 0.0) for h in range(g, groups)]
        total = jnp.dot(jnp.concatenate(match, axis=1).astype(BF16), values[128 * g :, :], preferred_element_type=F32)
        square = square + jnp.sum((values[128 * g : 128 * g + 128, :].astype(F32) * total).reshape(16, 8, 256), axis=0)
    lane = iota((8, 128), 1)
    block = jnp.where(lane == 8, sum_piece(square), whole_sums(partial))
    block = block + pltpu.roll(block, 1, 0)
    block = three_parts(block + pltpu.roll(block, 2, 0))
    owners = sent_ref.shape[0] // 8
    slots = slot_ref.shape[0]
    keys = slot_ref[...]
    label = (keys - span * jnp.floor(keys * (1.0 / span)) + 1.0) * lead_ref[...]
    here = iota((slots, 128), 1) == 64 + row_index()
    values = [lead_w3_ref[0:slots, :], lead_w3_ref[slots:, :], jnp.where(here, label, 0.0).astype(BF16)]
    values = jnp.concatenate(values, axis=1)
    values = jnp.concatenate([values, jnp.zeros((128 - slots, 384), BF16)], axis=0)
    match = (iota((owners, 128), 0) == lane_ref[...].astype(jnp.int32)[0:1, :]) & (iota((owners, 128), 1) < slots)
    placed = jnp.dot(match.astype(F32).astype(BF16), values, preferred_element_type=F32)
    for to in range(2):
        mine = [jnp.where(core == to, placed[:, 128 * i : 128 * i + 128], 0.0) for i in range(3)]
        wide[pl.ds(4 * to, owners, stride=8), :] = mine[0]
        wide[pl.ds(4 * to + 1, owners, stride=8), :] = mine[1]
        wide[pl.ds(4 * to + 2, owners, stride=8), :] = mine[2] + block[3:4, :]
        wide[pl.ds(4 * to + 3, owners, stride=8), :] = jnp.broadcast_to(block[7:8, :], (owners, 128))
    sent_ref[...] = wide[...].astype(BF16)


def finish(got_ref, w1_ref, solution_ref, phi_ref, wide):
    wide[...] = got_ref[...].astype(F32)
    peers = got_ref.shape[0] // 8
    parts = [wide[pl.ds(i, peers, stride=8), :] + wide[pl.ds(4 + i, peers, stride=8), :] for i in range(4)]
    total = jnp.concatenate([jnp.sum(parts[i], axis=0, keepdims=True) for i in (2, 3)], axis=0)
    half = w1_ref.shape[0]
    labels = pltpu.roll(jnp.broadcast_to(total[0:1, :], (half, 128)), 64, 1)
    match = (labels == (iota((half, 128), 0) + 1).astype(F32)) & (iota((half, 128), 1) < peers)
    values = jnp.concatenate(parts[0:2], axis=1)
    values = jnp.concatenate([values, jnp.zeros((128 - peers, 256), F32)], axis=0).astype(BF16)
    w3 = jnp.dot(match.astype(F32).astype(BF16), values, preferred_element_type=F32)
    first = iota((8, 128), 0) < 4
    sums = whole_sums(jnp.where(first, total[0:1, :], total[1:2, :]))

    def pick(j):
        return jnp.broadcast_to(sums[:, j : j + 1], (8, 128))

    t11, t13, t33, s00, s02, s22, s24, s04, s44 = [pick(j) for j in range(9)]

    def norm(square):
        return jnp.maximum(square, 0.0) + EPS

    b0 = norm(s00)
    ib0 = 1.0 / b0
    a1 = norm(t11 * ib0)
    x22 = ib0 / a1
    x20 = -ib0
    x00 = a1 * ib0
    b1 = norm(x22 * s22 + 2.0 * x20 * s02 + x00 * s00)
    ib1 = 1.0 / b1
    y33 = x22 * ib1
    y31 = x20 * ib1 - x22
    y11 = x00 * ib1 - 2.0 * x20 + b1 * x22
    a2 = norm(y33 * t33 + 2.0 * y31 * t13 + y11 * t11)
    ia2 = 1.0 / a2
    ratio = a2 * ib1
    z44 = y33 * ia2
    z22 = y11 * ia2 - 2.0 * y31 + ratio * x22
    z00 = ratio * x00
    z42 = y31 * ia2 - y33
    z40 = -x20 * ib1
    z20 = x20 + (a2 * x20 - x00) * ib1
    b2 = norm(z44 * s44 + z22 * s22 + z00 * s00 + 2.0 * (z42 * s24 + z40 * s04 + z20 * s02))
    ir1 = 1.0 / (a1 + b1)
    ir2 = 1.0 / (a1 * a2 * ir1 + b2)
    k1 = ir1 + (1.0 + a2 * ir1 * (b1 * ir1)) * ir2
    k3 = -ir1 * ir2
    phi_bar2 = jnp.sqrt(b0 * (b1 * ir1) * (b2 * ir2))

    phi_ref[...] = jnp.where(iota((1, 128), 1) == 0, phi_bar2[0:1, :], phi_bar2[4:5, :])[:, 0:2]
    for r in range(2):
        lanes = slice(128 * r, 128 * r + 128)
        scale1, scale3 = k1[4 * r : 4 * r + 1, :], k3[4 * r : 4 * r + 1, :]
        solution_ref[pl.ds(r, half, stride=2), :] = w1_ref[:, lanes].astype(F32) * scale1 + w3[:, lanes] * scale3


def struct(shape, dtype):
    return jax.ShapeDtypeStruct(shape, dtype)


def on_device(tiles, coords, counts, rhs):
    chips = lax.axis_size("y")
    n_row = lax.axis_size("z") * lax.axis_size("x")
    n_col = chips * lax.axis_size("core")
    slots = tiles.shape[2]
    rows = 2 * slots
    span = rhs.shape[1] // 128
    places = coords[0, 0].T

    def call(body, specs, outs, scratch, *operands, out_specs=None):
        return pl.pallas_call(
            body,
            out_shape=outs,
            in_specs=specs,
            out_specs=[VMEM] * len(outs) if out_specs is None else out_specs,
            scratch_shapes=scratch,
            compiler_params=pltpu.CompilerParams(vmem_limit_bytes=32 * 1024 * 1024),
        )(*operands)

    def exchange(sent, axis):
        return lax.all_to_all(sent, axis, split_axis=0, concat_axis=0, tiled=True)

    def exchange_col(sent):
        return lax.all_gather(exchange(sent, "y"), "core", axis=0, tiled=True)

    wide = pltpu.VMEM((rows, 128), F32)
    piece = struct((span, 256), BF16)
    own = struct((rows, 128), BF16)
    slot_table = struct((slots, 128), F32)
    lane_table = struct((8, 128), BF16)
    tile = tiles[0, 0]
    sent, u0 = call(
        begin,
        [VMEM],
        [struct((chips, 2 * span, 128), BF16), piece],
        [pltpu.VMEM((2 * span, 128), F32)],
        rhs,
    )
    slot_v, slot_u, lane_v, lane_u, held, turned, fetch = call(
        functools.partial(tables, spans=(span, chips, lax.axis_size("core"))),
        [SMEM, SMEM, VMEM],
        [slot_table] * 2 + [lane_table] * 2 + [struct(tile.shape, BF16)] * 2 + [struct((2, slots), jnp.int32)],
        [pltpu.SMEM((slots,), jnp.int32), pltpu.SMEM((2, slots), jnp.int32)],
        places, counts, tile,
        out_specs=[VMEM] * 6 + [SMEM],
    )
    u_group = exchange_col(sent).reshape(n_col * span, 2, 128)
    sent, own_u = call(
        first_adjoint,
        [SMEM] + [VMEM] * 3,
        [struct((n_row, rows + 8, 128), BF16), own],
        [wide, wide],
        fetch, lane_v, u_group, held,
    )
    sent, own_w1, w1, v_map = call(
        first_forward,
        [VMEM] * 4,
        [struct((chips, rows + 8, 128), BF16), own, piece, struct((n_row // 4, 128), F32)],
        [wide, wide],
        slot_v, lane_u, exchange(sent, ROW), turned,
    )
    sent, own_w2, w2, u_map = call(
        second_adjoint,
        [VMEM] * 4,
        [struct((lax.axis_size("z"), rows + 8, 128), BF16), own, piece, struct((n_col // 4, 128), F32)],
        [wide, wide],
        slot_u, lane_v, exchange_col(sent), held,
    )
    (sent,) = call(
        regroup,
        [VMEM] * 2,
        [struct((lax.axis_size("x"), rows, 128), BF16)],
        [pltpu.VMEM((lax.axis_size("z") // 4, 128), F32)],
        v_map, exchange(sent, "z"),
    )
    sent, lead_w3, lead = call(
        second_forward,
        [VMEM] * 9,
        [struct((n_col, slots + 8, 128), BF16), own, slot_table],
        [wide, wide],
        slot_v, v_map, exchange(sent, "x"), turned, own_w1, w2, u0, own_w2, own_u,
    )
    (sent,) = call(
        functools.partial(gather_sums, span=span),
        [VMEM] * 6,
        [struct((n_row * 8, 128), BF16)],
        [pltpu.VMEM((n_row * 8, 128), F32)],
        exchange(sent, ("core", "y")), u_map, lane_v, slot_v, lead_w3, lead,
    )
    result, phi_bar = call(
        finish,
        [VMEM] * 2,
        [struct((2 * span, 128), F32), struct((1, 2), F32)],
        [pltpu.VMEM((n_row * 8, 128), F32)],
        exchange(sent.reshape(n_row * 2, 4, 128), ROW + ("core",)).reshape(n_row * 8, 128), w1,
    )
    result = result.reshape(span, 2, 128).transpose(1, 0, 2).reshape(2, span * 128)
    return (result, phi_bar.reshape(2))


def solution(mesh):
    n_row, n_col = mesh.devices.shape
    fine = Mesh(mesh.devices.reshape(n_row // 4, 4, n_col // 2, 2), ROW + COL)
    return jax.shard_map(
        on_device,
        mesh=fine,
        in_specs=(P(ROW, COL, None, None, None), P(ROW, COL, None, None), P(ROW, COL), P(None, ROW + COL)),
        out_specs=(P(None, COL + ROW), P()),
        check_vma=False,
    )
```

```python
import functools

import jax
import jax.numpy as jnp
from jax import lax
from jax.experimental import pallas as pl
from jax.experimental.pallas import tpu as pltpu
from jax.sharding import Mesh
from jax.sharding import PartitionSpec as P

EPS = 1e-06
F32 = jnp.float32
BF16 = jnp.bfloat16
ROW = ("z", "x")
COL = ("y", "core")
VMEM = pl.BlockSpec(memory_space=pltpu.VMEM)
SMEM = pl.BlockSpec(memory_space=pltpu.SMEM)


def iota(shape, dim):
    return lax.broadcasted_iota(jnp.int32, shape, dim)


def row_index():
    return lax.axis_index("z") * lax.axis_size("x") + lax.axis_index("x")


def col_index():
    return lax.axis_index("y") * lax.axis_size("core") + lax.axis_index("core")


def slot_keys(sorted_ref, axis):
    slots = sorted_ref.shape[1]
    row = iota((slots, 128), 0)
    keys = jnp.full((slots, 128), -8, jnp.int32)
    for k in range(slots):
        block = sorted_ref[axis, k]
        keys = jnp.where(row == k, jnp.where(block < 0, -8, block), keys)
    return keys.astype(F32)


def with_range(slot_ref, me, span):
    return jnp.concatenate([slot_ref[...], (me * span + iota((span, 128), 0)).astype(F32)], axis=0)


def lane_keys(sorted_ref, axis):
    slots = sorted_ref.shape[1]
    slot = iota((8, 128), 1) % slots
    keys = jnp.full((8, 128), -1, jnp.int32)
    for k in range(slots):
        keys = jnp.where(slot == k, sorted_ref[axis, k], keys)
    keys = keys.astype(F32)
    high = jnp.floor(keys * (1.0 / 64.0))
    sub = iota((8, 128), 0)
    return jnp.where(sub == 0, high, jnp.where(sub == 1, keys - 64.0 * high, 0.0)).astype(BF16)


def read_keys(got_ref, map_ref):
    rows = got_ref.shape[1] - 8
    quarter = iota((8, 128), 1) // 32
    for g in range(got_ref.shape[0] // 4):
        both = got_ref[4 * g, rows:, :].astype(F32)
        for i in range(1, 4):
            both = jnp.where(quarter == i, got_ref[4 * g + i, rows:, :].astype(F32), both)
        map_ref[g : g + 1, :] = both[0:1, :] * 64.0 + both[1:2, :]


def four_peers(got_ref, g):
    halves = []
    for r in range(2):
        halves.append(jnp.concatenate([got_ref[4 * g + i, 32 * r : 32 * r + 32, :] for i in range(4)], axis=0))
    return jnp.concatenate(halves, axis=1)


def sum_by_key(got_ref, map_ref, keys):
    total = jnp.zeros((keys.shape[0], 256), F32)
    for g in range(0, got_ref.shape[0] // 4, 2):
        match = jnp.concatenate([(keys == map_ref[g + i : g + i + 1, :]).astype(F32) for i in range(2)], axis=1)
        values = jnp.concatenate([four_peers(got_ref, g + i) for i in range(2)], axis=0)
        total = total + jnp.dot(match.astype(BF16), values, preferred_element_type=F32)
    return total


def products(held_ref, tile_ref, out_ref):
    pair = iota((8, 128), 0) // 2
    for j in range(tile_ref.shape[0] // 4):
        rows = held_ref[8 * j : 8 * j + 8, :]
        left = jnp.concatenate([jnp.where(pair == i, rows, 0.0) for i in range(4)], axis=1).astype(BF16)
        right = jnp.concatenate([tile_ref[4 * j + i] for i in range(4)], axis=0)
        out_ref[8 * j : 8 * j + 8, :] = jnp.dot(left, right, preferred_element_type=F32)


def split_rows(ref):
    half = ref.shape[0] // 2
    return jnp.concatenate([ref[pl.ds(r, half, stride=2), :] for r in range(2)], axis=0)


def hold(held_ref, own):
    half = held_ref.shape[0] // 2
    for r in range(2):
        held_ref[pl.ds(r, half, stride=2), :] = own[:, 128 * r : 128 * r + 128].astype(F32)


def send_all(sent_ref, values, extra):
    rows = values.shape[0]
    for peer in range(sent_ref.shape[0]):
        sent_ref[peer, 0:rows, :] = values
        if extra is not None:
            sent_ref[peer, rows:, :] = extra


def begin(rhs_ref, sent_ref, piece_ref, rows):
    for b in range(rows.shape[0] // 2):
        rows[2 * b : 2 * b + 2, :] = rhs_ref[:, 128 * b : 128 * b + 128]
    send_all(sent_ref, rows[...].astype(BF16), None)
    half = rows.shape[0] // 2
    piece_ref[...] = jnp.concatenate([rows[pl.ds(r, half, stride=2), :] for r in range(2)], axis=1).astype(BF16)


def tables(
    places_ref, counts_ref, tile_ref,
    slot_v_ref, slot_u_ref, lane_v_ref, lane_u_ref, held_ref, turned_ref, fetch_ref, order_ref, sorted_ref, spans,
):
    count = counts_ref[0, 0]
    span, chips, cores = spans
    slots = places_ref.shape[1]
    seen = jnp.int32(0)
    for k in range(slots):
        odd = (places_ref[0, k] // span) % 2
        order_ref[jnp.where(odd == 1, slots // 2 + seen, k - seen)] = k
        seen = seen + odd
    for i in range(slots):
        k = order_ref[i]
        held_ref[i] = tile_ref[k]
        turned_ref[i] = jnp.transpose(tile_ref[k])
        block = places_ref[0, k]
        owner = block // span
        used = k < count
        sorted_ref[0, i] = jnp.where(used, block, -1)
        sorted_ref[1, i] = jnp.where(used, places_ref[1, k], -1)
        fetch_ref[0, i] = ((owner % cores) * chips + owner // cores) * span + block % span
        fetch_ref[1, i] = used.astype(jnp.int32)
    slot_u_ref[...] = slot_keys(sorted_ref, 0)
    slot_v_ref[...] = slot_keys(sorted_ref, 1)
    lane_u_ref[...] = lane_keys(sorted_ref, 0)
    lane_v_ref[...] = lane_keys(sorted_ref, 1)


def first_adjoint(fetch_ref, lane_ref, u_ref, tile_ref, sent_ref, own_u_ref, held, out):
    for k in range(fetch_ref.shape[1]):
        held[2 * k : 2 * k + 2, :] = u_ref[fetch_ref[0, k]].astype(F32) * fetch_ref[1, k].astype(F32)
    own_u_ref[...] = split_rows(held).astype(BF16)
    products(held, tile_ref, out)
    send_all(sent_ref, split_rows(out).astype(BF16), lane_ref[...])


def keep(w, w_ref, piece_ref, held):
    slots = held.shape[0] // 2
    w = w.astype(BF16)
    own = w[0:slots, :]
    piece_ref[...] = w[slots:, :]
    hold(held, own)
    w_ref[...] = jnp.concatenate([own[:, 0:128], own[:, 128:256]], axis=0)


def first_forward(slot_ref, lane_ref, got_ref, turned_ref, sent_ref, w_ref, piece_ref, map_ref, held, out):
    read_keys(got_ref, map_ref)
    keys = with_range(slot_ref, row_index(), piece_ref.shape[0])
    keep(sum_by_key(got_ref, map_ref, keys), w_ref, piece_ref, held)
    products(held, turned_ref, out)
    send_all(sent_ref, split_rows(out).astype(BF16), lane_ref[...])


def second_adjoint(slot_ref, lane_ref, got_ref, tile_ref, sent_ref, w_ref, piece_ref, map_ref, held, out):
    read_keys(got_ref, map_ref)
    keys = with_range(slot_ref, col_index(), piece_ref.shape[0])
    keep(sum_by_key(got_ref, map_ref, keys), w_ref, piece_ref, held)
    products(held, tile_ref, out)
    send_all(sent_ref, split_rows(out).astype(BF16), lane_ref[...])


def regroup(map_ref, got_ref, sent_ref, line_ref):
    read_keys(got_ref, line_ref)
    target = map_ref[pl.ds(lax.axis_index("z"), 1), :]
    column = jnp.transpose(jnp.broadcast_to(target, (128, 128)))
    total = sum_by_key(got_ref, line_ref, column).astype(BF16)
    for peer in range(sent_ref.shape[0]):
        for r in range(2):
            sent_ref[peer, 32 * r : 32 * r + 32, :] = total[32 * peer : 32 * peer + 32, 128 * r : 128 * r + 128]


def leaders(map_ref, slot_ref, me):
    keys = slot_ref[...]
    quarter = iota(keys.shape, 1) // 32
    earlier = jnp.zeros(keys.shape, F32)
    for g in range(map_ref.shape[0]):
        earlier = earlier + ((keys == map_ref[g : g + 1, :]) & (4 * g + quarter < me)).astype(F32)
    count = jnp.sum(earlier, axis=1, keepdims=True)
    return ((count == 0.0) & (keys >= 0.0)).astype(F32)


def sum_halves(first, second):
    folds = []
    for values in (first, second):
        fold = jnp.sum(values.reshape(values.shape[0] // 8, 8, 128), axis=0)
        folds.append(fold + pltpu.roll(fold, 4, 0))
    return jnp.sum(jnp.where(iota((8, 128), 0) < 4, folds[0], folds[1]), axis=1, keepdims=True)


def sum_piece(values):
    return sum_halves(values[:, 0:128], values[:, 128:256])


def sum_slots(values):
    half = values.shape[0] // 2
    return sum_halves(values[0:half, :], values[half:, :])


def three_parts(values):
    values = jnp.where(iota(values.shape, 1) < 16, values, 0.0)
    high = values.astype(BF16).astype(F32)
    middle = (values - high).astype(BF16).astype(F32)
    low = (values - high - middle).astype(BF16).astype(F32)
    return high + pltpu.roll(middle, 16, 1) + pltpu.roll(low, 32, 1)


def whole_sums(parts):
    return parts + pltpu.roll(parts, 112, 1) + pltpu.roll(parts, 96, 1)


def second_forward(
    slot_ref, map_ref, got_ref, turned_ref, own_w1_ref, w2_ref, u0_ref, own_w2_ref, own_u_ref,
    sent_ref, lead_w3_ref, lead_ref, held, out,
):
    w3 = got_ref[0].astype(F32)
    for peer in range(1, got_ref.shape[0]):
        w3 = w3 + got_ref[peer].astype(F32)
    w3 = w3.astype(BF16).astype(F32)
    half = w3.shape[0] // 2
    for r in range(2):
        held[pl.ds(r, half, stride=2), :] = w3[half * r : half * r + half, :]
    products(held, turned_ref, out)
    sent = split_rows(out).astype(BF16)
    lead = leaders(map_ref, slot_ref, row_index())
    lead_ref[...] = lead
    lead = jnp.concatenate([lead, lead], axis=0)
    lead_w3 = w3 * lead
    lead_w3_ref[...] = lead_w3.astype(BF16)
    w1 = own_w1_ref[...].astype(F32)
    w2 = w2_ref[...].astype(F32)
    u0 = u0_ref[...].astype(F32)
    c4 = sent.astype(F32)
    sums = [
        sum_slots(w1 * w1 * lead),
        sum_slots(w1 * lead_w3),
        sum_slots(w3 * lead_w3),
        sum_piece(u0 * u0),
        sum_piece(u0 * w2),
        sum_piece(w2 * w2),
        sum_slots(c4 * own_w2_ref[...].astype(F32)),
        sum_slots(c4 * own_u_ref[...].astype(F32)),
    ]
    lane = iota((8, 128), 1)
    block = jnp.zeros((8, 128), F32)
    for j, value in enumerate(sums):
        block = jnp.where(lane == j, value, block)
    block = three_parts(block).astype(BF16)
    chips = sent_ref.shape[0] // 2
    for core in range(2):
        for r in range(2):
            values = sent[half * r + half // 2 * core : half * r + half // 2 * core + half // 2, :]
            for chip in range(chips):
                sent_ref[core * chips + chip, half // 2 * r : half // 2 * r + half // 2, :] = values
        for chip in range(chips):
            sent_ref[core * chips + chip, half:, :] = block


def half_slots(got_ref, g):
    core = lax.axis_index("core")
    halves = []
    for r in range(2):
        for i in range(4):
            values = got_ref[4 * g + i, 16 * r : 16 * r + 16, :]
            zeros = jnp.zeros_like(values)
            halves += [jnp.where(core == 0, values, zeros), jnp.where(core == 0, zeros, values)]
    return jnp.concatenate([jnp.concatenate(halves[0:8], axis=0), jnp.concatenate(halves[8:16], axis=0)], axis=1)


def gather_sums(got_ref, map_ref, lane_ref, slot_ref, lead_w3_ref, lead_ref, sent_ref, wide, span):
    peers = got_ref.shape[0]
    rows = got_ref.shape[1] - 8
    core = lax.axis_index("core")
    partial = got_ref[0, rows:, :].astype(F32)
    for peer in range(1, peers):
        partial = partial + got_ref[peer, rows:, :].astype(F32)
    partial = jnp.where(core == 0, partial, 0.0)
    groups = peers // 4
    values = jnp.concatenate([half_slots(got_ref, g) for g in range(groups)], axis=0)
    square = jnp.zeros((8, 256), F32)
    for g in range(groups):
        column = jnp.transpose(jnp.broadcast_to(map_ref[g : g + 1, :], (128, 128)))
        match = [jnp.where(column == map_ref[h : h + 1, :], 1.0 if h == g else 2.0, 0.0) for h in range(g, groups)]
        total = jnp.dot(jnp.concatenate(match, axis=1).astype(BF16), values[128 * g :, :], preferred_element_type=F32)
        square = square + jnp.sum((values[128 * g : 128 * g + 128, :].astype(F32) * total).reshape(16, 8, 256), axis=0)
    lane = iota((8, 128), 1)
    block = jnp.where(lane == 8, sum_piece(square), whole_sums(partial))
    block = block + pltpu.roll(block, 1, 0)
    block = three_parts(block + pltpu.roll(block, 2, 0))
    owners = sent_ref.shape[0] // 8
    slots = slot_ref.shape[0]
    keys = slot_ref[...]
    label = (keys - span * jnp.floor(keys * (1.0 / span)) + 1.0) * lead_ref[...]
    here = iota((slots, 128), 1) == 64 + row_index()
    values = [lead_w3_ref[0:slots, :], lead_w3_ref[slots:, :], jnp.where(here, label, 0.0).astype(BF16)]
    values = jnp.concatenate(values, axis=1)
    values = jnp.concatenate([values, jnp.zeros((128 - slots, 384), BF16)], axis=0)
    match = (iota((owners, 128), 0) == lane_ref[...].astype(jnp.int32)[0:1, :]) & (iota((owners, 128), 1) < slots)
    placed = jnp.dot(match.astype(F32).astype(BF16), values, preferred_element_type=F32)
    for to in range(2):
        mine = [jnp.where(core == to, placed[:, 128 * i : 128 * i + 128], 0.0) for i in range(3)]
        wide[pl.ds(4 * owners * to + 0, owners, stride=4), :] = mine[0]
        wide[pl.ds(4 * owners * to + 1, owners, stride=4), :] = mine[1]
        wide[pl.ds(4 * owners * to + 2, owners, stride=4), :] = mine[2] + block[3:4, :]
        wide[pl.ds(4 * owners * to + 3, owners, stride=4), :] = jnp.broadcast_to(block[7:8, :], (owners, 128))
    sent_ref[...] = wide[...].astype(BF16)


def finish(got_ref, w1_ref, solution_ref, phi_ref, wide):
    wide[...] = got_ref[...].astype(F32)
    peers = got_ref.shape[0] // 8
    parts = [wide[pl.ds(i, peers, stride=4), :] + wide[pl.ds(4 * peers + i, peers, stride=4), :] for i in range(4)]
    total = jnp.concatenate([jnp.sum(parts[i], axis=0, keepdims=True) for i in (2, 3)], axis=0)
    half = w1_ref.shape[0]
    labels = pltpu.roll(jnp.broadcast_to(total[0:1, :], (half, 128)), 64, 1)
    match = (labels == (iota((half, 128), 0) + 1).astype(F32)) & (iota((half, 128), 1) < peers)
    values = jnp.concatenate(parts[0:2], axis=1)
    values = jnp.concatenate([values, jnp.zeros((128 - peers, 256), F32)], axis=0).astype(BF16)
    w3 = jnp.dot(match.astype(F32).astype(BF16), values, preferred_element_type=F32)
    first = iota((8, 128), 0) < 4
    sums = whole_sums(jnp.where(first, total[0:1, :], total[1:2, :]))

    def pick(j):
        return jnp.broadcast_to(sums[:, j : j + 1], (8, 128))

    t11, t13, t33, s00, s02, s22, s24, s04, s44 = [pick(j) for j in range(9)]

    def norm(square):
        return jnp.maximum(square, 0.0) + EPS

    b0 = norm(s00)
    ib0 = 1.0 / b0
    a1 = norm(t11 * ib0)
    x22 = ib0 / a1
    x20 = -ib0
    x00 = a1 * ib0
    b1 = norm(x22 * s22 + 2.0 * x20 * s02 + x00 * s00)
    ib1 = 1.0 / b1
    y33 = x22 * ib1
    y31 = x20 * ib1 - x22
    y11 = x00 * ib1 - 2.0 * x20 + b1 * x22
    a2 = norm(y33 * t33 + 2.0 * y31 * t13 + y11 * t11)
    ia2 = 1.0 / a2
    ratio = a2 * ib1
    z44 = y33 * ia2
    z22 = y11 * ia2 - 2.0 * y31 + ratio * x22
    z00 = ratio * x00
    z42 = y31 * ia2 - y33
    z40 = -x20 * ib1
    z20 = x20 + (a2 * x20 - x00) * ib1
    b2 = norm(z44 * s44 + z22 * s22 + z00 * s00 + 2.0 * (z42 * s24 + z40 * s04 + z20 * s02))
    ir1 = 1.0 / (a1 + b1)
    ir2 = 1.0 / (a1 * a2 * ir1 + b2)
    k1 = ir1 + (1.0 + a2 * ir1 * (b1 * ir1)) * ir2
    k3 = -ir1 * ir2
    phi_bar2 = jnp.sqrt(b0 * (b1 * ir1) * (b2 * ir2))

    phi_ref[...] = jnp.where(iota((1, 128), 1) == 0, phi_bar2[0:1, :], phi_bar2[4:5, :])[:, 0:2]
    for r in range(2):
        lanes = slice(128 * r, 128 * r + 128)
        scale1, scale3 = k1[4 * r : 4 * r + 1, :], k3[4 * r : 4 * r + 1, :]
        solution_ref[pl.ds(r, half, stride=2), :] = w1_ref[:, lanes].astype(F32) * scale1 + w3[:, lanes] * scale3


def struct(shape, dtype):
    return jax.ShapeDtypeStruct(shape, dtype)


def on_device(tiles, coords, counts, rhs):
    chips = lax.axis_size("y")
    n_row = lax.axis_size("z") * lax.axis_size("x")
    n_col = chips * lax.axis_size("core")
    slots = tiles.shape[2]
    rows = 2 * slots
    span = rhs.shape[1] // 128
    places = coords[0, 0].T

    def call(body, specs, outs, scratch, *operands, out_specs=None):
        return pl.pallas_call(
            body,
            out_shape=outs,
            in_specs=specs,
            out_specs=[VMEM] * len(outs) if out_specs is None else out_specs,
            scratch_shapes=scratch,
            compiler_params=pltpu.CompilerParams(vmem_limit_bytes=32 * 1024 * 1024),
        )(*operands)

    def exchange(sent, axis):
        return lax.all_to_all(sent, axis, split_axis=0, concat_axis=0, tiled=True)

    def exchange_col(sent):
        return lax.all_gather(exchange(sent, "y"), "core", axis=0, tiled=True)

    wide = pltpu.VMEM((rows, 128), F32)
    piece = struct((span, 256), BF16)
    own = struct((rows, 128), BF16)
    slot_table = struct((slots, 128), F32)
    lane_table = struct((8, 128), BF16)
    tile = tiles[0, 0]
    sent, u0 = call(
        begin,
        [VMEM],
        [struct((chips, 2 * span, 128), BF16), piece],
        [pltpu.VMEM((2 * span, 128), F32)],
        rhs,
    )
    slot_v, slot_u, lane_v, lane_u, held, turned, fetch = call(
        functools.partial(tables, spans=(span, chips, lax.axis_size("core"))),
        [SMEM, SMEM, VMEM],
        [slot_table] * 2 + [lane_table] * 2 + [struct(tile.shape, BF16)] * 2 + [struct((2, slots), jnp.int32)],
        [pltpu.SMEM((slots,), jnp.int32), pltpu.SMEM((2, slots), jnp.int32)],
        places, counts, tile,
        out_specs=[VMEM] * 6 + [SMEM],
    )
    u_group = exchange_col(sent).reshape(n_col * span, 2, 128)
    sent, own_u = call(
        first_adjoint,
        [SMEM] + [VMEM] * 3,
        [struct((n_row, rows + 8, 128), BF16), own],
        [wide, wide],
        fetch, lane_v, u_group, held,
    )
    sent, own_w1, w1, v_map = call(
        first_forward,
        [VMEM] * 4,
        [struct((chips, rows + 8, 128), BF16), own, piece, struct((n_row // 4, 128), F32)],
        [wide, wide],
        slot_v, lane_u, exchange(sent, ROW), turned,
    )
    sent, own_w2, w2, u_map = call(
        second_adjoint,
        [VMEM] * 4,
        [struct((lax.axis_size("z"), rows + 8, 128), BF16), own, piece, struct((n_col // 4, 128), F32)],
        [wide, wide],
        slot_u, lane_v, exchange_col(sent), held,
    )
    (sent,) = call(
        regroup,
        [VMEM] * 2,
        [struct((lax.axis_size("x"), rows, 128), BF16)],
        [pltpu.VMEM((lax.axis_size("z") // 4, 128), F32)],
        v_map, exchange(sent, "z"),
    )
    sent, lead_w3, lead = call(
        second_forward,
        [VMEM] * 9,
        [struct((n_col, slots + 8, 128), BF16), own, slot_table],
        [wide, wide],
        slot_v, v_map, exchange(sent, "x"), turned, own_w1, w2, u0, own_w2, own_u,
    )
    (sent,) = call(
        functools.partial(gather_sums, span=span),
        [VMEM] * 6,
        [struct((n_row * 8, 128), BF16)],
        [pltpu.VMEM((n_row * 8, 128), F32)],
        exchange(sent, ("core", "y")), u_map, lane_v, slot_v, lead_w3, lead,
    )
    result, phi_bar = call(
        finish,
        [VMEM] * 2,
        [struct((2 * span, 128), F32), struct((1, 2), F32)],
        [pltpu.VMEM((n_row * 8, 128), F32)],
        exchange(sent.reshape(n_row * 2, 4, 128), ("core",) + ROW).reshape(n_row * 8, 128), w1,
    )
    result = result.reshape(span, 2, 128).transpose(1, 0, 2).reshape(2, span * 128)
    return (result, phi_bar.reshape(2))


def solution(mesh):
    n_row, n_col = mesh.devices.shape
    fine = Mesh(mesh.devices.reshape(n_row // 4, 4, n_col // 2, 2), ROW + COL)
    return jax.shard_map(
        on_device,
        mesh=fine,
        in_specs=(P(ROW, COL, None, None, None), P(ROW, COL, None, None), P(ROW, COL), P(None, ROW + COL)),
        out_specs=(P(None, COL + ROW), P()),
        check_vma=False,
    )
```

```python
import functools

import jax
import jax.numpy as jnp
from jax import lax
from jax.experimental import pallas as pl
from jax.experimental.pallas import tpu as pltpu
from jax.sharding import Mesh
from jax.sharding import PartitionSpec as P

EPS = 1e-06
F32 = jnp.float32
BF16 = jnp.bfloat16
ROW = ("z", "x")
COL = ("y", "core")
VMEM = pl.BlockSpec(memory_space=pltpu.VMEM)
SMEM = pl.BlockSpec(memory_space=pltpu.SMEM)


def iota(shape, dim):
    return lax.broadcasted_iota(jnp.int32, shape, dim)


def row_index():
    return lax.axis_index("z") * lax.axis_size("x") + lax.axis_index("x")


def col_index():
    return lax.axis_index("y") * lax.axis_size("core") + lax.axis_index("core")


def slot_keys(sorted_ref, axis):
    slots = sorted_ref.shape[1]
    row = iota((slots, 128), 0)
    keys = jnp.full((slots, 128), -8, jnp.int32)
    for k in range(slots):
        block = sorted_ref[axis, k]
        keys = jnp.where(row == k, jnp.where(block < 0, -8, block), keys)
    return keys.astype(F32)


def with_range(slot_ref, me, span):
    return jnp.concatenate([slot_ref[...], (me * span + iota((span, 128), 0)).astype(F32)], axis=0)


def lane_keys(sorted_ref, axis):
    slots = sorted_ref.shape[1]
    slot = iota((8, 128), 1) % slots
    keys = jnp.full((8, 128), -1, jnp.int32)
    for k in range(slots):
        keys = jnp.where(slot == k, sorted_ref[axis, k], keys)
    keys = keys.astype(F32)
    high = jnp.floor(keys * (1.0 / 64.0))
    sub = iota((8, 128), 0)
    return jnp.where(sub == 0, high, jnp.where(sub == 1, keys - 64.0 * high, 0.0)).astype(BF16)


def read_keys(got_ref, map_ref):
    rows = got_ref.shape[1] - 8
    quarter = iota((8, 128), 1) // 32
    for g in range(got_ref.shape[0] // 4):
        both = got_ref[4 * g, rows:, :].astype(F32)
        for i in range(1, 4):
            both = jnp.where(quarter == i, got_ref[4 * g + i, rows:, :].astype(F32), both)
        map_ref[g : g + 1, :] = both[0:1, :] * 64.0 + both[1:2, :]


def four_peers(got_ref, g):
    halves = []
    for r in range(2):
        halves.append(jnp.concatenate([got_ref[4 * g + i, 32 * r : 32 * r + 32, :] for i in range(4)], axis=0))
    return jnp.concatenate(halves, axis=1)


def sum_by_key(got_ref, map_ref, keys):
    total = jnp.zeros((keys.shape[0], 256), F32)
    for g in range(0, got_ref.shape[0] // 4, 2):
        match = jnp.concatenate([(keys == map_ref[g + i : g + i + 1, :]).astype(F32) for i in range(2)], axis=1)
        values = jnp.concatenate([four_peers(got_ref, g + i) for i in range(2)], axis=0)
        total = total + jnp.dot(match.astype(BF16), values, preferred_element_type=F32)
    return total


def products(held_ref, tile_ref, out_ref):
    pair = iota((8, 128), 0) // 2
    for j in range(tile_ref.shape[0] // 4):
        rows = held_ref[8 * j : 8 * j + 8, :]
        left = jnp.concatenate([jnp.where(pair == i, rows, 0.0) for i in range(4)], axis=1).astype(BF16)
        right = jnp.concatenate([tile_ref[4 * j + i] for i in range(4)], axis=0)
        out_ref[8 * j : 8 * j + 8, :] = jnp.dot(left, right, preferred_element_type=F32)


def split_rows(ref):
    half = ref.shape[0] // 2
    return jnp.concatenate([ref[pl.ds(r, half, stride=2), :] for r in range(2)], axis=0)


def hold(held_ref, own):
    half = held_ref.shape[0] // 2
    for r in range(2):
        held_ref[pl.ds(r, half, stride=2), :] = own[:, 128 * r : 128 * r + 128].astype(F32)


def send_all(sent_ref, values, extra):
    rows = values.shape[0]
    for peer in range(sent_ref.shape[0]):
        sent_ref[peer, 0:rows, :] = values
        if extra is not None:
            sent_ref[peer, rows:, :] = extra


def begin(rhs_ref, sent_ref, piece_ref, rows):
    for b in range(rows.shape[0] // 2):
        rows[2 * b : 2 * b + 2, :] = rhs_ref[:, 128 * b : 128 * b + 128]
    send_all(sent_ref, rows[...].astype(BF16), None)
    half = rows.shape[0] // 2
    piece_ref[...] = jnp.concatenate([rows[pl.ds(r, half, stride=2), :] for r in range(2)], axis=1).astype(BF16)


def tables(
    places_ref, counts_ref, tile_ref,
    slot_v_ref, slot_u_ref, lane_v_ref, lane_u_ref, held_ref, turned_ref, fetch_ref, order_ref, sorted_ref, spans,
):
    count = counts_ref[0, 0]
    span, chips, cores = spans
    slots = places_ref.shape[1]
    seen = jnp.int32(0)
    for k in range(slots):
        odd = (places_ref[0, k] // span) % 2
        order_ref[jnp.where(odd == 1, slots // 2 + seen, k - seen)] = k
        seen = seen + odd
    for i in range(slots):
        k = order_ref[i]
        held_ref[i] = tile_ref[k]
        turned_ref[i] = jnp.transpose(tile_ref[k])
        block = places_ref[0, k]
        owner = block // span
        used = k < count
        sorted_ref[0, i] = jnp.where(used, block, -1)
        sorted_ref[1, i] = jnp.where(used, places_ref[1, k], -1)
        fetch_ref[0, i] = ((owner % cores) * chips + owner // cores) * span + block % span
        fetch_ref[1, i] = used.astype(jnp.int32)
    slot_u_ref[...] = slot_keys(sorted_ref, 0)
    slot_v_ref[...] = slot_keys(sorted_ref, 1)
    lane_u_ref[...] = lane_keys(sorted_ref, 0)
    lane_v_ref[...] = lane_keys(sorted_ref, 1)


def first_adjoint(fetch_ref, lane_ref, u_ref, tile_ref, sent_ref, own_u_ref, held, out):
    for k in range(fetch_ref.shape[1]):
        held[2 * k : 2 * k + 2, :] = u_ref[fetch_ref[0, k]].astype(F32) * fetch_ref[1, k].astype(F32)
    own_u_ref[...] = split_rows(held).astype(BF16)
    products(held, tile_ref, out)
    send_all(sent_ref, split_rows(out).astype(BF16), lane_ref[...])


def keep(w, w_ref, piece_ref, held):
    slots = held.shape[0] // 2
    w = w.astype(BF16)
    own = w[0:slots, :]
    piece_ref[...] = w[slots:, :]
    hold(held, own)
    w_ref[...] = jnp.concatenate([own[:, 0:128], own[:, 128:256]], axis=0)


def first_forward(slot_ref, lane_ref, got_ref, turned_ref, sent_ref, w_ref, piece_ref, map_ref, held, out):
    read_keys(got_ref, map_ref)
    keys = with_range(slot_ref, row_index(), piece_ref.shape[0])
    keep(sum_by_key(got_ref, map_ref, keys), w_ref, piece_ref, held)
    products(held, turned_ref, out)
    send_all(sent_ref, split_rows(out).astype(BF16), lane_ref[...])


def second_adjoint(slot_ref, got_ref, tile_ref, sent_ref, w_ref, piece_ref, map_ref, held, out):
    read_keys(got_ref, map_ref)
    keys = with_range(slot_ref, col_index(), piece_ref.shape[0])
    keep(sum_by_key(got_ref, map_ref, keys), w_ref, piece_ref, held)
    products(held, tile_ref, out)
    send_all(sent_ref, split_rows(out).astype(BF16), None)


def regroup(map_ref, got_ref, sent_ref, line_ref):
    me = lax.axis_index("x")
    quarter = iota((8, 128), 1) // 32
    for g in range(line_ref.shape[0]):
        keys = jnp.zeros((8, 128), F32)
        for i in range(4):
            row = jnp.broadcast_to(map_ref[4 * g + i : 4 * g + i + 1, :], (8, 128))
            keys = jnp.where(quarter == i, pltpu.roll(row, (i - me + 4) % 4 * 32, 1), keys)
        line_ref[g : g + 1, :] = keys[0:1, :]
    target = map_ref[pl.ds(lax.axis_index("z"), 1), :]
    column = jnp.transpose(jnp.broadcast_to(target, (128, 128)))
    total = sum_by_key(got_ref, line_ref, column).astype(BF16)
    for peer in range(sent_ref.shape[0]):
        for r in range(2):
            sent_ref[peer, 32 * r : 32 * r + 32, :] = total[32 * peer : 32 * peer + 32, 128 * r : 128 * r + 128]


def leaders(map_ref, slot_ref, me):
    keys = slot_ref[...]
    quarter = iota(keys.shape, 1) // 32
    earlier = jnp.zeros(keys.shape, F32)
    for g in range(map_ref.shape[0]):
        earlier = earlier + ((keys == map_ref[g : g + 1, :]) & (4 * g + quarter < me)).astype(F32)
    count = jnp.sum(earlier, axis=1, keepdims=True)
    return ((count == 0.0) & (keys >= 0.0)).astype(F32)


def sum_halves(first, second):
    folds = []
    for values in (first, second):
        fold = jnp.sum(values.reshape(values.shape[0] // 8, 8, 128), axis=0)
        folds.append(fold + pltpu.roll(fold, 4, 0))
    return jnp.sum(jnp.where(iota((8, 128), 0) < 4, folds[0], folds[1]), axis=1, keepdims=True)


def sum_piece(values):
    return sum_halves(values[:, 0:128], values[:, 128:256])


def sum_slots(values):
    half = values.shape[0] // 2
    return sum_halves(values[0:half, :], values[half:, :])


def three_parts(values):
    values = jnp.where(iota(values.shape, 1) < 16, values, 0.0)
    high = values.astype(BF16).astype(F32)
    middle = (values - high).astype(BF16).astype(F32)
    low = (values - high - middle).astype(BF16).astype(F32)
    return high + pltpu.roll(middle, 16, 1) + pltpu.roll(low, 32, 1)


def whole_sums(parts):
    return parts + pltpu.roll(parts, 112, 1) + pltpu.roll(parts, 96, 1)


def second_forward(
    slot_ref, map_ref, got_ref, turned_ref, own_w1_ref, w2_ref, u0_ref, own_w2_ref, own_u_ref,
    sent_ref, lead_w3_ref, lead_ref, held, out,
):
    w3 = got_ref[0].astype(F32)
    for peer in range(1, got_ref.shape[0]):
        w3 = w3 + got_ref[peer].astype(F32)
    w3 = w3.astype(BF16).astype(F32)
    half = w3.shape[0] // 2
    for r in range(2):
        held[pl.ds(r, half, stride=2), :] = w3[half * r : half * r + half, :]
    products(held, turned_ref, out)
    sent = split_rows(out).astype(BF16)
    lead = leaders(map_ref, slot_ref, row_index())
    lead_ref[...] = lead
    lead = jnp.concatenate([lead, lead], axis=0)
    lead_w3 = w3 * lead
    lead_w3_ref[...] = lead_w3.astype(BF16)
    w1 = own_w1_ref[...].astype(F32)
    w2 = w2_ref[...].astype(F32)
    u0 = u0_ref[...].astype(F32)
    c4 = sent.astype(F32)
    sums = [
        sum_slots(w1 * w1 * lead),
        sum_slots(w1 * lead_w3),
        sum_slots(w3 * lead_w3),
        sum_piece(u0 * u0),
        sum_piece(u0 * w2),
        sum_piece(w2 * w2),
        sum_slots(c4 * own_w2_ref[...].astype(F32)),
        sum_slots(c4 * own_u_ref[...].astype(F32)),
    ]
    lane = iota((8, 128), 1)
    block = jnp.zeros((8, 128), F32)
    for j, value in enumerate(sums):
        block = jnp.where(lane == j, value, block)
    block = three_parts(block).astype(BF16)
    chips = sent_ref.shape[0] // 2
    for core in range(2):
        for r in range(2):
            values = sent[half * r + half // 2 * core : half * r + half // 2 * core + half // 2, :]
            for chip in range(chips):
                sent_ref[core * chips + chip, half // 2 * r : half // 2 * r + half // 2, :] = values
        for chip in range(chips):
            sent_ref[core * chips + chip, half:, :] = block


def half_slots(got_ref, g):
    core = lax.axis_index("core")
    halves = []
    for r in range(2):
        for i in range(4):
            values = got_ref[4 * g + i, 16 * r : 16 * r + 16, :]
            zeros = jnp.zeros_like(values)
            halves += [jnp.where(core == 0, values, zeros), jnp.where(core == 0, zeros, values)]
    return jnp.concatenate([jnp.concatenate(halves[0:8], axis=0), jnp.concatenate(halves[8:16], axis=0)], axis=1)


def gather_sums(got_ref, map_ref, lane_ref, slot_ref, lead_w3_ref, lead_ref, sent_ref, wide, span):
    peers = got_ref.shape[0]
    rows = got_ref.shape[1] - 8
    core = lax.axis_index("core")
    partial = got_ref[0, rows:, :].astype(F32)
    for peer in range(1, peers):
        partial = partial + got_ref[peer, rows:, :].astype(F32)
    partial = jnp.where(core == 0, partial, 0.0)
    groups = peers // 4
    values = jnp.concatenate([half_slots(got_ref, g) for g in range(groups)], axis=0)
    square = jnp.zeros((8, 256), F32)
    for g in range(groups):
        column = jnp.transpose(jnp.broadcast_to(map_ref[g : g + 1, :], (128, 128)))
        match = [jnp.where(column == map_ref[h : h + 1, :], 1.0 if h == g else 2.0, 0.0) for h in range(g, groups)]
        total = jnp.dot(jnp.concatenate(match, axis=1).astype(BF16), values[128 * g :, :], preferred_element_type=F32)
        square = square + jnp.sum((values[128 * g : 128 * g + 128, :].astype(F32) * total).reshape(16, 8, 256), axis=0)
    lane = iota((8, 128), 1)
    block = jnp.where(lane == 8, sum_piece(square), whole_sums(partial))
    block = block + pltpu.roll(block, 1, 0)
    block = three_parts(block + pltpu.roll(block, 2, 0))
    owners = sent_ref.shape[0] // 8
    slots = slot_ref.shape[0]
    keys = slot_ref[...]
    label = (keys - span * jnp.floor(keys * (1.0 / span)) + 1.0) * lead_ref[...]
    here = iota((slots, 128), 1) == 64 + row_index()
    values = [lead_w3_ref[0:slots, :], lead_w3_ref[slots:, :], jnp.where(here, label, 0.0).astype(BF16)]
    values = jnp.concatenate(values, axis=1)
    values = jnp.concatenate([values, jnp.zeros((128 - slots, 384), BF16)], axis=0)
    match = (iota((owners, 128), 0) == lane_ref[...].astype(jnp.int32)[0:1, :]) & (iota((owners, 128), 1) < slots)
    placed = jnp.dot(match.astype(F32).astype(BF16), values, preferred_element_type=F32)
    for to in range(2):
        mine = [jnp.where(core == to, placed[:, 128 * i : 128 * i + 128], 0.0) for i in range(3)]
        wide[pl.ds(4 * owners * to + 0, owners, stride=4), :] = mine[0]
        wide[pl.ds(4 * owners * to + 1, owners, stride=4), :] = mine[1]
        wide[pl.ds(4 * owners * to + 2, owners, stride=4), :] = mine[2] + block[3:4, :]
        wide[pl.ds(4 * owners * to + 3, owners, stride=4), :] = jnp.broadcast_to(block[7:8, :], (owners, 128))
    sent_ref[...] = wide[...].astype(BF16)


def finish(got_ref, w1_ref, solution_ref, phi_ref, wide):
    wide[...] = got_ref[...].astype(F32)
    peers = got_ref.shape[0] // 8
    parts = [wide[pl.ds(i, peers, stride=4), :] + wide[pl.ds(4 * peers + i, peers, stride=4), :] for i in range(4)]
    total = jnp.concatenate([jnp.sum(parts[i], axis=0, keepdims=True) for i in (2, 3)], axis=0)
    half = w1_ref.shape[0]
    labels = pltpu.roll(jnp.broadcast_to(total[0:1, :], (half, 128)), 64, 1)
    match = (labels == (iota((half, 128), 0) + 1).astype(F32)) & (iota((half, 128), 1) < peers)
    values = jnp.concatenate(parts[0:2], axis=1)
    values = jnp.concatenate([values, jnp.zeros((128 - peers, 256), F32)], axis=0).astype(BF16)
    w3 = jnp.dot(match.astype(F32).astype(BF16), values, preferred_element_type=F32)
    first = iota((8, 128), 0) < 4
    sums = whole_sums(jnp.where(first, total[0:1, :], total[1:2, :]))

    def pick(j):
        return jnp.broadcast_to(sums[:, j : j + 1], (8, 128))

    t11, t13, t33, s00, s02, s22, s24, s04, s44 = [pick(j) for j in range(9)]

    def norm(square):
        return jnp.maximum(square, 0.0) + EPS

    b0 = norm(s00)
    ib0 = 1.0 / b0
    a1 = norm(t11 * ib0)
    x22 = ib0 / a1
    x20 = -ib0
    x00 = a1 * ib0
    b1 = norm(x22 * s22 + 2.0 * x20 * s02 + x00 * s00)
    ib1 = 1.0 / b1
    y33 = x22 * ib1
    y31 = x20 * ib1 - x22
    y11 = x00 * ib1 - 2.0 * x20 + b1 * x22
    a2 = norm(y33 * t33 + 2.0 * y31 * t13 + y11 * t11)
    ia2 = 1.0 / a2
    ratio = a2 * ib1
    z44 = y33 * ia2
    z22 = y11 * ia2 - 2.0 * y31 + ratio * x22
    z00 = ratio * x00
    z42 = y31 * ia2 - y33
    z40 = -x20 * ib1
    z20 = x20 + (a2 * x20 - x00) * ib1
    b2 = norm(z44 * s44 + z22 * s22 + z00 * s00 + 2.0 * (z42 * s24 + z40 * s04 + z20 * s02))
    ir1 = 1.0 / (a1 + b1)
    ir2 = 1.0 / (a1 * a2 * ir1 + b2)
    k1 = ir1 + (1.0 + a2 * ir1 * (b1 * ir1)) * ir2
    k3 = -ir1 * ir2
    phi_bar2 = jnp.sqrt(b0 * (b1 * ir1) * (b2 * ir2))

    phi_ref[...] = jnp.where(iota((1, 128), 1) == 0, phi_bar2[0:1, :], phi_bar2[4:5, :])[:, 0:2]
    for r in range(2):
        lanes = slice(128 * r, 128 * r + 128)
        scale1, scale3 = k1[4 * r : 4 * r + 1, :], k3[4 * r : 4 * r + 1, :]
        solution_ref[pl.ds(r, half, stride=2), :] = w1_ref[:, lanes].astype(F32) * scale1 + w3[:, lanes] * scale3


def struct(shape, dtype):
    return jax.ShapeDtypeStruct(shape, dtype)


def on_device(tiles, coords, counts, rhs):
    chips = lax.axis_size("y")
    n_row = lax.axis_size("z") * lax.axis_size("x")
    n_col = chips * lax.axis_size("core")
    slots = tiles.shape[2]
    rows = 2 * slots
    span = rhs.shape[1] // 128
    places = coords[0, 0].T

    def call(body, specs, outs, scratch, *operands, out_specs=None):
        return pl.pallas_call(
            body,
            out_shape=outs,
            in_specs=specs,
            out_specs=[VMEM] * len(outs) if out_specs is None else out_specs,
            scratch_shapes=scratch,
            compiler_params=pltpu.CompilerParams(vmem_limit_bytes=32 * 1024 * 1024),
        )(*operands)

    def exchange(sent, axis):
        return lax.all_to_all(sent, axis, split_axis=0, concat_axis=0, tiled=True)

    def exchange_col(sent):
        return lax.all_gather(exchange(sent, "y"), "core", axis=0, tiled=True)

    wide = pltpu.VMEM((rows, 128), F32)
    piece = struct((span, 256), BF16)
    own = struct((rows, 128), BF16)
    slot_table = struct((slots, 128), F32)
    lane_table = struct((8, 128), BF16)
    tile = tiles[0, 0]
    sent, u0 = call(
        begin,
        [VMEM],
        [struct((chips, 2 * span, 128), BF16), piece],
        [pltpu.VMEM((2 * span, 128), F32)],
        rhs,
    )
    slot_v, slot_u, lane_v, lane_u, held, turned, fetch = call(
        functools.partial(tables, spans=(span, chips, lax.axis_size("core"))),
        [SMEM, SMEM, VMEM],
        [slot_table] * 2 + [lane_table] * 2 + [struct(tile.shape, BF16)] * 2 + [struct((2, slots), jnp.int32)],
        [pltpu.SMEM((slots,), jnp.int32), pltpu.SMEM((2, slots), jnp.int32)],
        places, counts, tile,
        out_specs=[VMEM] * 6 + [SMEM],
    )
    u_group = exchange_col(sent).reshape(n_col * span, 2, 128)
    sent, own_u = call(
        first_adjoint,
        [SMEM] + [VMEM] * 3,
        [struct((n_row, rows + 8, 128), BF16), own],
        [wide, wide],
        fetch, lane_v, u_group, held,
    )
    sent, own_w1, w1, v_map = call(
        first_forward,
        [VMEM] * 4,
        [struct((chips, rows + 8, 128), BF16), own, piece, struct((n_row // 4, 128), F32)],
        [wide, wide],
        slot_v, lane_u, exchange(sent, ROW), turned,
    )
    sent, own_w2, w2, u_map = call(
        second_adjoint,
        [VMEM] * 3,
        [struct((lax.axis_size("z"), rows, 128), BF16), own, piece, struct((n_col // 4, 128), F32)],
        [wide, wide],
        slot_u, exchange_col(sent), held,
    )
    (sent,) = call(
        regroup,
        [VMEM] * 2,
        [struct((lax.axis_size("x"), rows, 128), BF16)],
        [pltpu.VMEM((lax.axis_size("z") // 4, 128), F32)],
        v_map, exchange(sent, "z"),
    )
    sent, lead_w3, lead = call(
        second_forward,
        [VMEM] * 9,
        [struct((n_col, slots + 8, 128), BF16), own, slot_table],
        [wide, wide],
        slot_v, v_map, exchange(sent, "x"), turned, own_w1, w2, u0, own_w2, own_u,
    )
    (sent,) = call(
        functools.partial(gather_sums, span=span),
        [VMEM] * 6,
        [struct((n_row * 8, 128), BF16)],
        [pltpu.VMEM((n_row * 8, 128), F32)],
        exchange(sent, ("core", "y")), u_map, lane_v, slot_v, lead_w3, lead,
    )
    result, phi_bar = call(
        finish,
        [VMEM] * 2,
        [struct((2 * span, 128), F32), struct((1, 2), F32)],
        [pltpu.VMEM((n_row * 8, 128), F32)],
        exchange(sent.reshape(n_row * 2, 4, 128), ("core",) + ROW).reshape(n_row * 8, 128), w1,
    )
    result = result.reshape(span, 2, 128).transpose(1, 0, 2).reshape(2, span * 128)
    return (result, phi_bar.reshape(2))


def solution(mesh):
    n_row, n_col = mesh.devices.shape
    fine = Mesh(mesh.devices.reshape(n_row // 4, 4, n_col // 2, 2), ROW + COL)
    return jax.shard_map(
        on_device,
        mesh=fine,
        in_specs=(P(ROW, COL, None, None, None), P(ROW, COL, None, None), P(ROW, COL), P(None, ROW + COL)),
        out_specs=(P(None, COL + ROW), P()),
        check_vma=False,
    )
```

```python
import functools

import jax
import jax.numpy as jnp
from jax import lax
from jax.experimental import pallas as pl
from jax.experimental.pallas import tpu as pltpu
from jax.sharding import Mesh
from jax.sharding import PartitionSpec as P

EPS = 1e-06
F32 = jnp.float32
BF16 = jnp.bfloat16
ROW = ("z", "x")
COL = ("y", "core")
VMEM = pl.BlockSpec(memory_space=pltpu.VMEM)
SMEM = pl.BlockSpec(memory_space=pltpu.SMEM)


def iota(shape, dim):
    return lax.broadcasted_iota(jnp.int32, shape, dim)


def row_index():
    return lax.axis_index("z") * lax.axis_size("x") + lax.axis_index("x")


def col_index():
    return lax.axis_index("y") * lax.axis_size("core") + lax.axis_index("core")


def slot_keys(sorted_ref, axis):
    slots = sorted_ref.shape[1]
    row = iota((slots, 128), 0)
    keys = jnp.full((slots, 128), -8, jnp.int32)
    for k in range(slots):
        block = sorted_ref[axis, k]
        keys = jnp.where(row == k, jnp.where(block < 0, -8, block), keys)
    return keys.astype(F32)


def with_range(slot_ref, me, span):
    return jnp.concatenate([slot_ref[...], (me * span + iota((span, 128), 0)).astype(F32)], axis=0)


def lane_keys(sorted_ref, axis):
    slots = sorted_ref.shape[1]
    slot = iota((8, 128), 1) % slots
    keys = jnp.full((8, 128), -1, jnp.int32)
    for k in range(slots):
        keys = jnp.where(slot == k, sorted_ref[axis, k], keys)
    keys = keys.astype(F32)
    high = jnp.floor(keys * (1.0 / 64.0))
    sub = iota((8, 128), 0)
    return jnp.where(sub == 0, high, jnp.where(sub == 1, keys - 64.0 * high, 0.0)).astype(BF16)


def read_keys(got_ref, map_ref):
    rows = got_ref.shape[1] - 8
    quarter = iota((8, 128), 1) // 32
    for g in range(got_ref.shape[0] // 4):
        both = got_ref[4 * g, rows:, :].astype(F32)
        for i in range(1, 4):
            both = jnp.where(quarter == i, got_ref[4 * g + i, rows:, :].astype(F32), both)
        map_ref[g : g + 1, :] = both[0:1, :] * 64.0 + both[1:2, :]


def four_peers(got_ref, g):
    halves = []
    for r in range(2):
        halves.append(jnp.concatenate([got_ref[4 * g + i, 32 * r : 32 * r + 32, :] for i in range(4)], axis=0))
    return jnp.concatenate(halves, axis=1)


def sum_by_key(got_ref, map_ref, keys):
    total = jnp.zeros((keys.shape[0], 256), F32)
    for g in range(0, got_ref.shape[0] // 4, 2):
        match = jnp.concatenate([(keys == map_ref[g + i : g + i + 1, :]).astype(F32) for i in range(2)], axis=1)
        values = jnp.concatenate([four_peers(got_ref, g + i) for i in range(2)], axis=0)
        total = total + jnp.dot(match.astype(BF16), values, preferred_element_type=F32)
    return total


def products(held_ref, tile_ref, out_ref):
    pair = iota((8, 128), 0) // 2
    for j in range(tile_ref.shape[0] // 4):
        rows = held_ref[8 * j : 8 * j + 8, :]
        left = jnp.concatenate([jnp.where(pair == i, rows, 0.0) for i in range(4)], axis=1).astype(BF16)
        right = jnp.concatenate([tile_ref[4 * j + i] for i in range(4)], axis=0)
        out_ref[8 * j : 8 * j + 8, :] = jnp.dot(left, right, preferred_element_type=F32)


def split_rows(ref):
    half = ref.shape[0] // 2
    return jnp.concatenate([ref[pl.ds(r, half, stride=2), :] for r in range(2)], axis=0)


def hold(held_ref, own):
    half = held_ref.shape[0] // 2
    for r in range(2):
        held_ref[pl.ds(r, half, stride=2), :] = own[:, 128 * r : 128 * r + 128].astype(F32)


def send_all(sent_ref, values, extra):
    rows = values.shape[0]
    for peer in range(sent_ref.shape[0]):
        sent_ref[peer, 0:rows, :] = values
        if extra is not None:
            sent_ref[peer, rows:, :] = extra


def begin(rhs_ref, sent_ref, piece_ref, rows):
    for b in range(rows.shape[0] // 2):
        rows[2 * b : 2 * b + 2, :] = rhs_ref[:, 128 * b : 128 * b + 128]
    send_all(sent_ref, rows[...].astype(BF16), None)
    half = rows.shape[0] // 2
    piece_ref[...] = jnp.concatenate([rows[pl.ds(r, half, stride=2), :] for r in range(2)], axis=1).astype(BF16)


def tables(
    places_ref, counts_ref, tile_ref,
    slot_v_ref, slot_u_ref, lane_v_ref, lane_u_ref, held_ref, turned_ref, fetch_ref, order_ref, sorted_ref, spans,
):
    count = counts_ref[0, 0]
    span, chips, cores = spans
    slots = places_ref.shape[1]
    seen = jnp.int32(0)
    for k in range(slots):
        odd = (places_ref[0, k] // span) % 2
        order_ref[jnp.where(odd == 1, slots // 2 + seen, k - seen)] = k
        seen = seen + odd
    for i in range(slots):
        k = order_ref[i]
        turned_ref[i] = jnp.transpose(tile_ref[k])
        block = places_ref[0, k]
        owner = block // span
        used = k < count
        held_ref[i] = jnp.where(used, tile_ref[k], jnp.zeros_like(tile_ref[k]))
        sorted_ref[0, i] = jnp.where(used, block, -1)
        sorted_ref[1, i] = jnp.where(used, places_ref[1, k], -1)
        fetch_ref[i] = ((owner % cores) * chips + owner // cores) * span + block % span
    slot_u_ref[...] = slot_keys(sorted_ref, 0)
    slot_v_ref[...] = slot_keys(sorted_ref, 1)
    lane_u_ref[...] = lane_keys(sorted_ref, 0)
    lane_v_ref[...] = lane_keys(sorted_ref, 1)


def first_adjoint(fetch_ref, lane_ref, u_ref, tile_ref, sent_ref, own_u_ref, held, out):
    for k in range(fetch_ref.shape[0]):
        held[2 * k : 2 * k + 2, :] = u_ref[fetch_ref[k]].astype(F32)
    own_u_ref[...] = split_rows(held).astype(BF16)
    products(held, tile_ref, out)
    send_all(sent_ref, split_rows(out).astype(BF16), lane_ref[...])


def keep(w, w_ref, piece_ref, held):
    slots = held.shape[0] // 2
    w = w.astype(BF16)
    own = w[0:slots, :]
    piece_ref[...] = w[slots:, :]
    hold(held, own)
    w_ref[...] = jnp.concatenate([own[:, 0:128], own[:, 128:256]], axis=0)


def first_forward(slot_ref, lane_ref, got_ref, turned_ref, sent_ref, w_ref, piece_ref, map_ref, held, out):
    read_keys(got_ref, map_ref)
    keys = with_range(slot_ref, row_index(), piece_ref.shape[0])
    keep(sum_by_key(got_ref, map_ref, keys), w_ref, piece_ref, held)
    products(held, turned_ref, out)
    send_all(sent_ref, split_rows(out).astype(BF16), lane_ref[...])


def second_adjoint(slot_ref, got_ref, tile_ref, sent_ref, w_ref, piece_ref, map_ref, held, out):
    read_keys(got_ref, map_ref)
    keys = with_range(slot_ref, col_index(), piece_ref.shape[0])
    keep(sum_by_key(got_ref, map_ref, keys), w_ref, piece_ref, held)
    products(held, tile_ref, out)
    send_all(sent_ref, split_rows(out).astype(BF16), None)


def regroup(map_ref, got_ref, sent_ref, line_ref):
    me = lax.axis_index("x")
    quarter = iota((8, 128), 1) // 32
    for g in range(line_ref.shape[0]):
        keys = jnp.zeros((8, 128), F32)
        for i in range(4):
            row = jnp.broadcast_to(map_ref[4 * g + i : 4 * g + i + 1, :], (8, 128))
            keys = jnp.where(quarter == i, pltpu.roll(row, (i - me + 4) % 4 * 32, 1), keys)
        line_ref[g : g + 1, :] = keys[0:1, :]
    target = map_ref[pl.ds(lax.axis_index("z"), 1), :]
    column = jnp.transpose(jnp.broadcast_to(target, (128, 128)))
    total = sum_by_key(got_ref, line_ref, column).astype(BF16)
    for peer in range(sent_ref.shape[0]):
        for r in range(2):
            sent_ref[peer, 32 * r : 32 * r + 32, :] = total[32 * peer : 32 * peer + 32, 128 * r : 128 * r + 128]


def leaders(map_ref, slot_ref, me):
    keys = slot_ref[...]
    quarter = iota(keys.shape, 1) // 32
    earlier = jnp.zeros(keys.shape, F32)
    for g in range(map_ref.shape[0]):
        earlier = earlier + ((keys == map_ref[g : g + 1, :]) & (4 * g + quarter < me)).astype(F32)
    count = jnp.sum(earlier, axis=1, keepdims=True)
    return ((count == 0.0) & (keys >= 0.0)).astype(F32)


def sum_halves(first, second):
    folds = []
    for values in (first, second):
        fold = jnp.sum(values.reshape(values.shape[0] // 8, 8, 128), axis=0)
        folds.append(fold + pltpu.roll(fold, 4, 0))
    return jnp.sum(jnp.where(iota((8, 128), 0) < 4, folds[0], folds[1]), axis=1, keepdims=True)


def sum_piece(values):
    return sum_halves(values[:, 0:128], values[:, 128:256])


def sum_slots(values):
    half = values.shape[0] // 2
    return sum_halves(values[0:half, :], values[half:, :])


def three_parts(values):
    values = jnp.where(iota(values.shape, 1) < 16, values, 0.0)
    high = values.astype(BF16).astype(F32)
    middle = (values - high).astype(BF16).astype(F32)
    low = (values - high - middle).astype(BF16).astype(F32)
    return high + pltpu.roll(middle, 16, 1) + pltpu.roll(low, 32, 1)


def whole_sums(parts):
    return parts + pltpu.roll(parts, 112, 1) + pltpu.roll(parts, 96, 1)


def second_forward(
    slot_ref, map_ref, got_ref, turned_ref, own_w1_ref, w2_ref, u0_ref, own_w2_ref, own_u_ref,
    sent_ref, lead_w3_ref, lead_ref, held, out,
):
    w3 = got_ref[0].astype(F32)
    for peer in range(1, got_ref.shape[0]):
        w3 = w3 + got_ref[peer].astype(F32)
    w3 = w3.astype(BF16).astype(F32)
    half = w3.shape[0] // 2
    for r in range(2):
        held[pl.ds(r, half, stride=2), :] = w3[half * r : half * r + half, :]
    products(held, turned_ref, out)
    sent = split_rows(out).astype(BF16)
    lead = leaders(map_ref, slot_ref, row_index())
    lead_ref[...] = lead
    lead = jnp.concatenate([lead, lead], axis=0)
    lead_w3 = w3 * lead
    lead_w3_ref[...] = lead_w3.astype(BF16)
    w1 = own_w1_ref[...].astype(F32)
    w2 = w2_ref[...].astype(F32)
    u0 = u0_ref[...].astype(F32)
    c4 = sent.astype(F32)
    sums = [
        sum_slots(w1 * w1 * lead),
        sum_slots(w1 * lead_w3),
        sum_slots(w3 * lead_w3),
        sum_piece(u0 * u0),
        sum_piece(u0 * w2),
        sum_piece(w2 * w2),
        sum_slots(c4 * own_w2_ref[...].astype(F32)),
        sum_slots(c4 * own_u_ref[...].astype(F32)),
    ]
    lane = iota((8, 128), 1)
    block = jnp.zeros((8, 128), F32)
    for j, value in enumerate(sums):
        block = jnp.where(lane == j, value, block)
    block = three_parts(block).astype(BF16)
    chips = sent_ref.shape[0] // 2
    for core in range(2):
        for r in range(2):
            values = sent[half * r + half // 2 * core : half * r + half // 2 * core + half // 2, :]
            for chip in range(chips):
                sent_ref[core * chips + chip, half // 2 * r : half // 2 * r + half // 2, :] = values
        for chip in range(chips):
            sent_ref[core * chips + chip, half:, :] = block


def half_slots(got_ref, g):
    core = lax.axis_index("core")
    halves = []
    for r in range(2):
        for i in range(4):
            values = got_ref[4 * g + i, 16 * r : 16 * r + 16, :]
            zeros = jnp.zeros_like(values)
            halves += [jnp.where(core == 0, values, zeros), jnp.where(core == 0, zeros, values)]
    return jnp.concatenate([jnp.concatenate(halves[0:8], axis=0), jnp.concatenate(halves[8:16], axis=0)], axis=1)


def gather_sums(got_ref, map_ref, lane_ref, slot_ref, lead_w3_ref, lead_ref, sent_ref, wide, span):
    peers = got_ref.shape[0]
    rows = got_ref.shape[1] - 8
    core = lax.axis_index("core")
    partial = got_ref[0, rows:, :].astype(F32)
    for peer in range(1, peers):
        partial = partial + got_ref[peer, rows:, :].astype(F32)
    partial = jnp.where(core == 0, partial, 0.0)
    groups = peers // 4
    values = jnp.concatenate([half_slots(got_ref, g) for g in range(groups)], axis=0)
    square = jnp.zeros((8, 256), F32)
    for g in range(groups):
        column = jnp.transpose(jnp.broadcast_to(map_ref[g : g + 1, :], (128, 128)))
        match = [jnp.where(column == map_ref[h : h + 1, :], 1.0 if h == g else 2.0, 0.0) for h in range(g, groups)]
        total = jnp.dot(jnp.concatenate(match, axis=1).astype(BF16), values[128 * g :, :], preferred_element_type=F32)
        square = square + jnp.sum((values[128 * g : 128 * g + 128, :].astype(F32) * total).reshape(16, 8, 256), axis=0)
    lane = iota((8, 128), 1)
    block = jnp.where(lane == 8, sum_piece(square), whole_sums(partial))
    block = block + pltpu.roll(block, 1, 0)
    block = three_parts(block + pltpu.roll(block, 2, 0))
    owners = sent_ref.shape[0] // 8
    slots = slot_ref.shape[0]
    keys = slot_ref[...]
    label = (keys - span * jnp.floor(keys * (1.0 / span)) + 1.0) * lead_ref[...]
    here = iota((slots, 128), 1) == 64 + row_index()
    values = [lead_w3_ref[0:slots, :], lead_w3_ref[slots:, :], jnp.where(here, label, 0.0).astype(BF16)]
    values = jnp.concatenate(values, axis=1)
    values = jnp.concatenate([values, jnp.zeros((128 - slots, 384), BF16)], axis=0)
    match = (iota((owners, 128), 0) == lane_ref[...].astype(jnp.int32)[0:1, :]) & (iota((owners, 128), 1) < slots)
    placed = jnp.dot(match.astype(F32).astype(BF16), values, preferred_element_type=F32)
    for to in range(2):
        mine = [jnp.where(core == to, placed[:, 128 * i : 128 * i + 128], 0.0) for i in range(3)]
        wide[pl.ds(4 * owners * to + 0, owners, stride=4), :] = mine[0]
        wide[pl.ds(4 * owners * to + 1, owners, stride=4), :] = mine[1]
        wide[pl.ds(4 * owners * to + 2, owners, stride=4), :] = mine[2] + block[3:4, :]
        wide[pl.ds(4 * owners * to + 3, owners, stride=4), :] = jnp.broadcast_to(block[7:8, :], (owners, 128))
    sent_ref[...] = wide[...].astype(BF16)


def finish(got_ref, w1_ref, solution_ref, phi_ref, wide):
    wide[...] = got_ref[...].astype(F32)
    peers = got_ref.shape[0] // 8
    parts = [wide[pl.ds(i, peers, stride=4), :] + wide[pl.ds(4 * peers + i, peers, stride=4), :] for i in range(4)]
    total = jnp.concatenate([jnp.sum(parts[i], axis=0, keepdims=True) for i in (2, 3)], axis=0)
    half = w1_ref.shape[0]
    labels = pltpu.roll(jnp.broadcast_to(total[0:1, :], (half, 128)), 64, 1)
    match = (labels == (iota((half, 128), 0) + 1).astype(F32)) & (iota((half, 128), 1) < peers)
    values = jnp.concatenate(parts[0:2], axis=1)
    values = jnp.concatenate([values, jnp.zeros((128 - peers, 256), F32)], axis=0).astype(BF16)
    w3 = jnp.dot(match.astype(F32).astype(BF16), values, preferred_element_type=F32)
    first = iota((8, 128), 0) < 4
    sums = whole_sums(jnp.where(first, total[0:1, :], total[1:2, :]))

    def pick(j):
        return jnp.broadcast_to(sums[:, j : j + 1], (8, 128))

    t11, t13, t33, s00, s02, s22, s24, s04, s44 = [pick(j) for j in range(9)]

    def norm(square):
        return jnp.maximum(square, 0.0) + EPS

    b0 = norm(s00)
    ib0 = 1.0 / b0
    a1 = norm(t11 * ib0)
    x22 = ib0 / a1
    x20 = -ib0
    x00 = a1 * ib0
    b1 = norm(x22 * s22 + 2.0 * x20 * s02 + x00 * s00)
    ib1 = 1.0 / b1
    y33 = x22 * ib1
    y31 = x20 * ib1 - x22
    y11 = x00 * ib1 - 2.0 * x20 + b1 * x22
    a2 = norm(y33 * t33 + 2.0 * y31 * t13 + y11 * t11)
    ia2 = 1.0 / a2
    ratio = a2 * ib1
    z44 = y33 * ia2
    z22 = y11 * ia2 - 2.0 * y31 + ratio * x22
    z00 = ratio * x00
    z42 = y31 * ia2 - y33
    z40 = -x20 * ib1
    z20 = x20 + (a2 * x20 - x00) * ib1
    b2 = norm(z44 * s44 + z22 * s22 + z00 * s00 + 2.0 * (z42 * s24 + z40 * s04 + z20 * s02))
    ir1 = 1.0 / (a1 + b1)
    ir2 = 1.0 / (a1 * a2 * ir1 + b2)
    k1 = ir1 + (1.0 + a2 * ir1 * (b1 * ir1)) * ir2
    k3 = -ir1 * ir2
    phi_bar2 = jnp.sqrt(b0 * (b1 * ir1) * (b2 * ir2))

    phi_ref[...] = jnp.where(iota((1, 128), 1) == 0, phi_bar2[0:1, :], phi_bar2[4:5, :])[:, 0:2]
    for r in range(2):
        lanes = slice(128 * r, 128 * r + 128)
        scale1, scale3 = k1[4 * r : 4 * r + 1, :], k3[4 * r : 4 * r + 1, :]
        solution_ref[pl.ds(r, half, stride=2), :] = w1_ref[:, lanes].astype(F32) * scale1 + w3[:, lanes] * scale3


def struct(shape, dtype):
    return jax.ShapeDtypeStruct(shape, dtype)


def on_device(tiles, coords, counts, rhs):
    chips = lax.axis_size("y")
    n_row = lax.axis_size("z") * lax.axis_size("x")
    n_col = chips * lax.axis_size("core")
    slots = tiles.shape[2]
    rows = 2 * slots
    span = rhs.shape[1] // 128
    places = coords[0, 0].T

    def call(body, specs, outs, scratch, *operands, out_specs=None):
        return pl.pallas_call(
            body,
            out_shape=outs,
            in_specs=specs,
            out_specs=[VMEM] * len(outs) if out_specs is None else out_specs,
            scratch_shapes=scratch,
            compiler_params=pltpu.CompilerParams(vmem_limit_bytes=32 * 1024 * 1024),
        )(*operands)

    def exchange(sent, axis):
        return lax.all_to_all(sent, axis, split_axis=0, concat_axis=0, tiled=True)

    def exchange_col(sent):
        return lax.all_gather(exchange(sent, "y"), "core", axis=0, tiled=True)

    wide = pltpu.VMEM((rows, 128), F32)
    piece = struct((span, 256), BF16)
    own = struct((rows, 128), BF16)
    slot_table = struct((slots, 128), F32)
    lane_table = struct((8, 128), BF16)
    tile = tiles[0, 0]
    sent, u0 = call(
        begin,
        [VMEM],
        [struct((chips, 2 * span, 128), BF16), piece],
        [pltpu.VMEM((2 * span, 128), F32)],
        rhs,
    )
    slot_v, slot_u, lane_v, lane_u, held, turned, fetch = call(
        functools.partial(tables, spans=(span, chips, lax.axis_size("core"))),
        [SMEM, SMEM, VMEM],
        [slot_table] * 2 + [lane_table] * 2 + [struct(tile.shape, BF16)] * 2 + [struct((slots,), jnp.int32)],
        [pltpu.SMEM((slots,), jnp.int32), pltpu.SMEM((2, slots), jnp.int32)],
        places, counts, tile,
        out_specs=[VMEM] * 6 + [SMEM],
    )
    u_group = exchange_col(sent).reshape(n_col * span, 2, 128)
    sent, own_u = call(
        first_adjoint,
        [SMEM] + [VMEM] * 3,
        [struct((n_row, rows + 8, 128), BF16), own],
        [wide, wide],
        fetch, lane_v, u_group, held,
    )
    sent, own_w1, w1, v_map = call(
        first_forward,
        [VMEM] * 4,
        [struct((chips, rows + 8, 128), BF16), own, piece, struct((n_row // 4, 128), F32)],
        [wide, wide],
        slot_v, lane_u, exchange(sent, ROW), turned,
    )
    sent, own_w2, w2, u_map = call(
        second_adjoint,
        [VMEM] * 3,
        [struct((lax.axis_size("z"), rows, 128), BF16), own, piece, struct((n_col // 4, 128), F32)],
        [wide, wide],
        slot_u, exchange_col(sent), held,
    )
    (sent,) = call(
        regroup,
        [VMEM] * 2,
        [struct((lax.axis_size("x"), rows, 128), BF16)],
        [pltpu.VMEM((lax.axis_size("z") // 4, 128), F32)],
        v_map, exchange(sent, "z"),
    )
    sent, lead_w3, lead = call(
        second_forward,
        [VMEM] * 9,
        [struct((n_col, slots + 8, 128), BF16), own, slot_table],
        [wide, wide],
        slot_v, v_map, exchange(sent, "x"), turned, own_w1, w2, u0, own_w2, own_u,
    )
    (sent,) = call(
        functools.partial(gather_sums, span=span),
        [VMEM] * 6,
        [struct((n_row * 8, 128), BF16)],
        [pltpu.VMEM((n_row * 8, 128), F32)],
        exchange(sent, ("core", "y")), u_map, lane_v, slot_v, lead_w3, lead,
    )
    result, phi_bar = call(
        finish,
        [VMEM] * 2,
        [struct((2 * span, 128), F32), struct((1, 2), F32)],
        [pltpu.VMEM((n_row * 8, 128), F32)],
        exchange(sent.reshape(n_row * 2, 4, 128), ("core",) + ROW).reshape(n_row * 8, 128), w1,
    )
    result = result.reshape(span, 2, 128).transpose(1, 0, 2).reshape(2, span * 128)
    return (result, phi_bar.reshape(2))


def solution(mesh):
    n_row, n_col = mesh.devices.shape
    fine = Mesh(mesh.devices.reshape(n_row // 4, 4, n_col // 2, 2), ROW + COL)
    return jax.shard_map(
        on_device,
        mesh=fine,
        in_specs=(P(ROW, COL, None, None, None), P(ROW, COL, None, None), P(ROW, COL), P(None, ROW + COL)),
        out_specs=(P(None, COL + ROW), P()),
        check_vma=False,
    )
```
